32 devices in a mesh: dp: 2 (over x), ctx: 4 (over z), tp: 4 (over y, core).
Axes of the slice: x: 2, y: 2, z: 4, core: 2. Of those that a mesh axis runs over, the one named last changes fastest.
Arguments:
- teacher_in: bfloat16 [4, 512, 1600], P('dp', 'ctx'), may hold values from -6 to 6
- teacher_gain_a: bfloat16 [1600], replicated, may hold values from 0.5 to 1.5
- teacher_shift_a: bfloat16 [1600], replicated, may hold values from -3 to 3
- teacher_attn_in: bfloat16 [3, 1600, 1600], P(None, 'dp'), may hold values from -0.15625 to 0.15625
- teacher_attn_bias: bfloat16 [2, 1600], replicated, may hold values from -3 to 3
- teacher_attn_out: bfloat16 [1600, 1600], P('dp'), may hold values from -1.75 to 1.75
- teacher_out_bias: bfloat16 [1600], replicated, may hold values from -3 to 3
- teacher_gain_b: bfloat16 [1600], replicated, may hold values from 0.5 to 1.5
- teacher_shift_b: bfloat16 [1600], replicated, may hold values from -3 to 3
- teacher_up: bfloat16 [1600, 6400], P('dp', 'tp'), may hold values from -0.15625 to 0.15625
- teacher_up_bias: bfloat16 [6400], P('tp'), may hold values from -3 to 3
- teacher_down: bfloat16 [6400, 1600], P('tp', 'dp'), may hold values from -0.15625 to 0.15625
- teacher_down_bias: bfloat16 [1600], replicated, may hold values from -3 to 3
- student_in: bfloat16 [4, 512, 768], P('dp', 'ctx'), may hold values from -6 to 6
- student_gain_a: bfloat16 [768], replicated, may hold values from 0.5 to 1.5
- student_shift_a: bfloat16 [768], replicated, may hold values from -3 to 3
- student_attn_in: bfloat16 [3, 768, 768], P(None, 'dp', 'tp'), may hold values from -0.21875 to 0.21875
- student_attn_bias: bfloat16 [2, 768], P(None, 'tp'), may hold values from -3 to 3
- student_attn_out: bfloat16 [768, 768], P('tp', 'dp'), may hold values from -2.5 to 2.5
- student_out_bias: bfloat16 [768], replicated, may hold values from -3 to 3
- student_gain_b: bfloat16 [768], replicated, may hold values from 0.5 to 1.5
- student_shift_b: bfloat16 [768], replicated, may hold values from -3 to 3
- student_up: bfloat16 [768, 3072], P('dp', 'tp'), may hold values from -0.21875 to 0.21875
- student_up_bias: bfloat16 [3072], P('tp'), may hold values from -3 to 3
- student_down: bfloat16 [3072, 768], P('tp', 'dp'), may hold values from -0.21875 to 0.21875
- student_down_bias: bfloat16 [768], replicated, may hold values from -3 to 3
- out_grad: bfloat16 [4, 512, 768], P('dp', 'ctx'), may hold values from -6 to 6
- slot_lengths: int32 [4], replicated, may hold values from 1 to 512, 1536 in all
Outputs:
- teacher_result: bfloat16 [4, 512, 1600], P('dp', 'ctx')
- student_result: bfloat16 [4, 512, 768], P('dp', 'ctx')
- student_in_grad: float32 [4, 512, 768], P('dp', 'ctx')
- grad_gain_a: float32 [768], P(('dp', 'ctx'))
- grad_shift_a: float32 [768], P(('dp', 'ctx'))
- grad_attn_in: float32 [3, 768, 768], P(None, ('dp', 'ctx'), 'tp')
- grad_attn_bias: float32 [2, 768], P(None, 'tp')
- grad_attn_out: float32 [768, 768], P('tp', ('dp', 'ctx'))
- grad_out_bias: float32 [768], P(('dp', 'ctx'))
- grad_gain_b: float32 [768], P(('dp', 'ctx'))
- grad_shift_b: float32 [768], P(('dp', 'ctx'))
- grad_up: float32 [768, 3072], P(('dp', 'ctx'), 'tp')
- grad_up_bias: float32 [3072], P('tp')
- grad_down: float32 [3072, 768], P('tp', ('dp', 'ctx'))
- grad_down_bias: float32 [768], P(('dp', 'ctx'))
The draws below stay inside these ranges and needn't reach their ends.
Inputs may be any that keep to these rules, and one draw needn't show every extreme that they name: `slot_lengths`: valid positions of each slot; the longest slot is full, and the lengths add up to 1536.
All inputs are finite; a program needn't handle non-finite values.
Results may differ from the reference program's by a relative error of at most 0.022.
Values may be sent and summed in bfloat16 or wider, within the bound.
No kernel may reach another device: no remote copies, remote signals or barrier semaphores. Data moves between devices by JAX's collectives and lax.ppermute only.
A program may use at most 192 MiB of HBM per device.

```python
import math
import jax
import jax.numpy as jnp
import numpy as np
from jax import lax

DT = 1600
FT = 6400
DS = 768
FS = 3072
HD = 64
SLOTS = 4
LENGTH = 512


def with_spikes(entries, key, source, target, parts, factor):
    def block_of(axis_at):
        return (jnp.arange(entries.shape[axis_at]) // (entries.shape[axis_at] // parts)).reshape((-1,) + (1,) * (entries.ndim - 1 - axis_at))

    first = jax.random.permutation(key, parts)[block_of(target)]
    other_side = (block_of(target) + parts // 2) % parts
    return jnp.where((block_of(source) == first) | (block_of(source) == other_side), factor * entries, entries)


def levels(key, extent, pieces, least, largest):
    loudness = 1.0
    for axis_at, shards_of in pieces:
        steps = jax.random.uniform(jax.random.fold_in(jax.random.fold_in(key, 6), axis_at), (shards_of,), jnp.float32, least / len(pieces), largest / len(pieces))
        loudness = loudness * jnp.repeat(jnp.exp(steps), extent[axis_at] // shards_of).reshape((-1,) + (1,) * (len(extent) - 1 - axis_at))
    return loudness


def length_profile(number_of, total, limit, lean):
    weights = [(1 << 20) // math.isqrt(rank ** lean) + 1 for rank in range(2, number_of + 1)]
    surplus, counts = total - limit - (number_of - 1), [1] * (number_of - 1)
    while surplus > 0:
        movable = [i for i in range(number_of - 1) if counts[i] < limit]
        mass, remaining = sum([weights[i] for i in movable]), surplus
        for i in movable:
            more = min(limit - counts[i], max(1, remaining * weights[i] // mass), surplus)
            counts[i] = counts[i] + more
            surplus = surplus - more
    return np.array([limit] + counts)


def ragged(key, count, total, limit, skew):
    if count == 2:
        one = jax.random.randint(key, (), max(1, total - limit), min(limit, total - 1) + 1)
        return jnp.stack([one, total - one])
    sizes = jnp.asarray(length_profile(count, total, limit, skew), jnp.int32)
    couples = (count - 1) // 2
    source_of, sink = sizes[1:1 + 2 * couples:2], sizes[2:2 + 2 * couples:2]
    margin = jnp.minimum(source_of - 1, limit - sink)
    shifted = jax.random.randint(jax.random.fold_in(key, 1), (couples,), 0, 1 << 20) % (margin + 1)
    sizes = sizes.at[1:1 + 2 * couples:2].set(source_of - shifted).at[2:2 + 2 * couples:2].set(sink + shifted)
    return sizes[jax.random.permutation(jax.random.fold_in(key, 2), count)]


def noise(own_key, dims, scale, bound, cuts=(), kind=jnp.bfloat16):
    drawn = jax.random.normal(own_key, dims, jnp.float32) * scale
    if len(cuts) > 0:
        drawn = levels(own_key, dims, cuts, -0.22, 0.18) * drawn
    return jnp.clip(drawn, min=-bound, max=bound).astype(kind)


def gaussian_with(own_key, dims, deviation, reach, split, heavy, held_as=jnp.bfloat16):
    values = deviation * jax.random.normal(own_key, dims, jnp.float32)
    if split:
        values = values * levels(own_key, dims, split, -0.22, 0.18)
    return jnp.clip(with_spikes(values, jax.random.fold_in(own_key, 3), *heavy), -reach, reach).astype(held_as)


def setup_inputs(seed: int = 0) -> dict:
    arg_keys = jax.random.split(jax.random.key(seed), 29)
    teacher_in = noise(arg_keys[0], (SLOTS, LENGTH, DT), 1.0, 6.0, ((0, 2), (1, 4)))
    teacher_gain_a = jnp.clip(1.0 + 0.1 * jax.random.normal(arg_keys[1], (DT,), jnp.float32), 0.5, 1.5).astype(jnp.bfloat16)
    teacher_shift_a = noise(arg_keys[2], (DT,), 0.5, 3.0)
    teacher_attn_in = noise(arg_keys[3], (3, DT, DT), DT ** -0.5, 0.15625, ((1, 2),))
    teacher_attn_bias = noise(arg_keys[4], (2, DT), 0.5, 3.0)
    teacher_attn_out = noise(arg_keys[5], (DT, DT), ((LENGTH // 4 * 100 // DT) ** 0.5 * 0.1), 1.75, ((0, 2),))
    teacher_out_bias = noise(arg_keys[6], (DT,), 0.5, 3.0)
    teacher_gain_b = jnp.clip(1.0 + 0.1 * jax.random.normal(arg_keys[7], (DT,), jnp.float32), 0.5, 1.5).astype(jnp.bfloat16)
    teacher_shift_b = noise(arg_keys[8], (DT,), 0.5, 3.0)
    teacher_up = noise(arg_keys[9], (DT, FT), DT ** -0.5, 0.15625, ((0, 2), (1, 4)))
    teacher_up_bias = noise(arg_keys[10], (FT,), 0.5, 3.0, ((0, 4),))
    teacher_down = noise(arg_keys[11], (FT, DT), (FT // 4) ** -0.5, 0.15625, ((0, 4), (1, 2)))
    teacher_down_bias = noise(arg_keys[12], (DT,), 0.5, 3.0)
    student_in = noise(arg_keys[13], (SLOTS, LENGTH, DS), 1.0, 6.0, ((0, 2), (1, 4)))
    student_gain_a = jnp.clip(1.0 + 0.1 * jax.random.normal(arg_keys[14], (DS,), jnp.float32), 0.5, 1.5).astype(jnp.bfloat16)
    student_shift_a = noise(arg_keys[15], (DS,), 0.5, 3.0)
    student_attn_in = noise(arg_keys[16], (3, DS, DS), DS ** -0.5, 0.21875, ((1, 2), (2, 4)))
    student_attn_bias = noise(arg_keys[17], (2, DS), 0.5, 3.0, ((1, 4),))
    student_attn_out = noise(arg_keys[18], (DS, DS), ((LENGTH // 4 * 100 // DS) ** 0.5 * 0.1), 2.5, ((0, 4), (1, 2)))
    student_out_bias = noise(arg_keys[19], (DS,), 0.5, 3.0)
    student_gain_b = jnp.clip(1.0 + 0.1 * jax.random.normal(arg_keys[20], (DS,), jnp.float32), 0.5, 1.5).astype(jnp.bfloat16)
    student_shift_b = noise(arg_keys[21], (DS,), 0.5, 3.0)
    student_up = noise(arg_keys[22], (DS, FS), DS ** -0.5, 0.21875, ((0, 2), (1, 4)))
    student_up_bias = noise(arg_keys[23], (FS,), 0.5, 3.0, ((0, 4),))
    student_down = noise(arg_keys[24], (FS, DS), (FS // 4) ** -0.5, 0.21875, ((0, 4), (1, 2)))
    student_down_bias = noise(arg_keys[25], (DS,), 0.5, 3.0)
    out_grad = gaussian_with(arg_keys[26], (SLOTS, LENGTH, DS), 1.0, 6.0, ((0, 2), (1, 4)), (1, 2, 4, 2.0))
    slot_lengths = ragged(arg_keys[27], SLOTS, SLOTS * LENGTH * 3 // 4, LENGTH, 0).astype(jnp.int32)
    return dict(teacher_in=teacher_in, teacher_gain_a=teacher_gain_a, teacher_shift_a=teacher_shift_a, teacher_attn_in=teacher_attn_in, teacher_attn_bias=teacher_attn_bias, teacher_attn_out=teacher_attn_out, teacher_out_bias=teacher_out_bias, teacher_gain_b=teacher_gain_b, teacher_shift_b=teacher_shift_b, teacher_up=teacher_up, teacher_up_bias=teacher_up_bias, teacher_down=teacher_down, teacher_down_bias=teacher_down_bias, student_in=student_in, student_gain_a=student_gain_a, student_shift_a=student_shift_a, student_attn_in=student_attn_in, student_attn_bias=student_attn_bias, student_attn_out=student_attn_out, student_out_bias=student_out_bias, student_gain_b=student_gain_b, student_shift_b=student_shift_b, student_up=student_up, student_up_bias=student_up_bias, student_down=student_down, student_down_bias=student_down_bias, out_grad=out_grad, slot_lengths=slot_lengths)


@jax.custom_vjp
def low(v):
    return lax.optimization_barrier(v.astype(jnp.bfloat16)).astype(jnp.float32)

@jax.custom_vjp
def low_back(v):
    return v

def low_keep(v):
    return (low(v), None)

def low_pass(kept, grad):
    return (grad,)

def back_keep(v):
    return (v, None)

def back_low(kept, grad):
    return (low(grad),)
low.defvjp(low_keep, low_pass)
low_back.defvjp(back_keep, back_low)
norm_eps = 1e-05
masked_score = -1000000000.0
highest = lax.Precision.HIGHEST

def matmul(left, right):
    return jnp.dot(left, right, precision=highest)

def layer_norm(x, gain, shift):
    centered = x - lax.optimization_barrier(jnp.mean(x, axis=-1, keepdims=True))
    spread = lax.optimization_barrier(jnp.mean(centered * centered, axis=-1, keepdims=True))
    return centered * lax.rsqrt(spread + norm_eps) * gain + shift

def gelu_tanh(v):
    return jax.nn.gelu(v, approximate=True)

def maybe_back(value, backward):
    if backward:
        return low_back(value)
    return value

def attend(query, keys, values, valid_len, backward):
    length = query.shape[0]
    width = math.gcd(length, 512)
    key_place = jnp.arange(length, dtype=jnp.int32)
    scale = HD ** (-0.5)

    def one_block(begin):
        query_rows = lax.dynamic_slice_in_dim(query, begin, width, 0)
        scores = jnp.einsum('qhd,khd->hqk', query_rows, keys, precision=highest) * scale
        query_place = begin + jnp.arange(width, dtype=jnp.int32)
        allowed = (key_place[None, :] <= query_place[:, None]) & (key_place[None, :] < valid_len)
        scores = maybe_back(jnp.where(allowed[None], scores, masked_score), backward)
        top = lax.optimization_barrier(jnp.max(scores, axis=-1, keepdims=True))
        expd = jnp.exp(scores - top)
        weights = expd / lax.optimization_barrier(jnp.sum(expd, axis=-1, keepdims=True))
        return jnp.einsum('hqk,khd->qhd', low(weights), values, precision=highest)
    starts = (jnp.arange(length // width, dtype=jnp.int32) * width).astype(jnp.int32)
    blocks = lax.map(jax.checkpoint(one_block), starts)
    return blocks.reshape(query.shape)

def block(x, params, valid_len, backward):
    gain_a, shift_a, attn_in, attn_bias, attn_out, out_bias, gain_b, shift_b, up, up_bias, down, down_bias = params
    length, width = x.shape
    heads = width // HD
    normed = low(layer_norm(x, gain_a, shift_a))
    query = low(maybe_back(matmul(normed, attn_in[0]) + attn_bias[0], backward))
    keys = low(maybe_back(matmul(normed, attn_in[1]), backward))
    values = low(maybe_back(matmul(normed, attn_in[2]) + attn_bias[1], backward))
    head_shape = (length, heads, HD)
    attended = attend(query.reshape(head_shape), keys.reshape(head_shape), values.reshape(head_shape), valid_len, backward)
    attended = low(maybe_back(attended.reshape(length, width), backward))
    mid = x + maybe_back(matmul(attended, attn_out) + out_bias, backward)
    normed_b = low(layer_norm(mid, gain_b, shift_b))
    upper = maybe_back(matmul(normed_b, up) + up_bias, backward)
    activ = low(maybe_back(gelu_tanh(upper), backward))
    return mid + maybe_back(matmul(activ, down) + down_bias, backward)

def reference(teacher_in, teacher_gain_a, teacher_shift_a, teacher_attn_in, teacher_attn_bias, teacher_attn_out, teacher_out_bias, teacher_gain_b, teacher_shift_b, teacher_up, teacher_up_bias, teacher_down, teacher_down_bias, student_in, student_gain_a, student_shift_a, student_attn_in, student_attn_bias, student_attn_out, student_out_bias, student_gain_b, student_shift_b, student_up, student_up_bias, student_down, student_down_bias, out_grad, slot_lengths):
    teacher_params = tuple((item.astype(jnp.float32) for item in (teacher_gain_a, teacher_shift_a, teacher_attn_in, teacher_attn_bias, teacher_attn_out, teacher_out_bias, teacher_gain_b, teacher_shift_b, teacher_up, teacher_up_bias, teacher_down, teacher_down_bias)))
    student_params = tuple((item.astype(jnp.float32) for item in (student_gain_a, student_shift_a, student_attn_in, student_attn_bias, student_attn_out, student_out_bias, student_gain_b, student_shift_b, student_up, student_up_bias, student_down, student_down_bias)))
    places = jnp.arange(LENGTH, dtype=jnp.int32)

    def per_slot(totals, items):
        teacher_x, student_x, cotangent, valid_len = items
        teacher_y = block(teacher_x.astype(jnp.float32), teacher_params, valid_len, False)

        def student_fn(x, params):
            return block(x, params, valid_len, True)
        student_y, pullback = jax.vjp(student_fn, student_x.astype(jnp.float32), student_params)
        keeper = (places < valid_len).astype(jnp.float32)[:, None]
        x_grad, param_grads = pullback(cotangent.astype(jnp.float32) * keeper)
        totals = jax.tree.map(jnp.add, totals, param_grads)
        return (totals, (teacher_y.astype(jnp.bfloat16), student_y.astype(jnp.bfloat16), x_grad))
    zero_grads = jax.tree.map(jnp.zeros_like, student_params)
    totals, (teacher_all, student_all, grad_all) = lax.scan(per_slot, zero_grads, (teacher_in, student_in, out_grad, slot_lengths))
    return (teacher_all, student_all, grad_all) + tuple(totals)
```

```python
import functools
import math

import jax
import jax.numpy as jnp
from jax import lax
from jax.experimental import pallas as pl
from jax.experimental.pallas import tpu as pltpu
from jax.sharding import PartitionSpec as P

HD = 64
EPS = 1e-05
MASKED = -1000000000.0
BF = jnp.bfloat16
F32 = jnp.float32
GELU_C = math.sqrt(2.0 / math.pi)


def dense(left, right):
    return jnp.dot(left, right, preferred_element_type=F32)


def dense_tn(left, right):
    return lax.dot_general(left, right, (((0,), (0,)), ((), ())), preferred_element_type=F32)


def dense_nt(left, right):
    return lax.dot_general(left, right, (((1,), (1,)), ((), ())), preferred_element_type=F32)


def norm_parts(x):
    centered = x - jnp.mean(x, axis=-1, keepdims=True)
    spread = jnp.mean(centered * centered, axis=-1, keepdims=True)
    factor = lax.rsqrt(spread + EPS)
    return centered * factor, factor


def norm_back(d_out, xhat, factor, gain):
    e = d_out * gain
    return factor * (
        e - jnp.mean(e, axis=-1, keepdims=True) - xhat * jnp.mean(e * xhat, axis=-1, keepdims=True)
    )


def gelu_tanh(v):
    return 0.5 * v * (1.0 + jnp.tanh(GELU_C * (v + 0.044715 * v * v * v)))


def gelu_both(v):
    inner = jnp.tanh(GELU_C * (v + 0.044715 * v * v * v))
    slope = 0.5 * (1.0 + inner) + 0.5 * v * (1.0 - inner * inner) * GELU_C * (
        1.0 + 3.0 * 0.044715 * v * v
    )
    return 0.5 * v * (1.0 + inner), slope


def head_groups(width):
    groups = []
    start = 0
    while start < width:
        size = min(2 * HD, width - start)
        groups.append((start, size))
        start += size
    return groups


def masked_scores(info, slot, rows, query, key_blocks, base_of):
    scale = HD ** (-0.5)
    query_place = info[0] + lax.broadcasted_iota(jnp.int32, (rows, 1), 0)
    limit = info[1 + slot]
    out = []
    for index, keys in enumerate(key_blocks):
        width = keys.shape[0]
        key_place = base_of(index) + lax.broadcasted_iota(jnp.int32, (rows, width), 1)
        allowed = (key_place <= query_place) & (key_place < limit) & (key_place >= 0)
        scores = dense_nt(query, keys) * scale
        out.append(jnp.where(allowed, scores, MASKED))
    return out


def soft_parts(scores):
    top = functools.reduce(
        jnp.maximum, [jnp.max(item, axis=-1, keepdims=True) for item in scores]
    )
    raised = [jnp.exp(item - top) for item in scores]
    total = functools.reduce(
        jnp.add, [jnp.sum(item, axis=-1, keepdims=True) for item in raised]
    )
    return raised, total


def block_reader(refs, blocks, rows, relative):
    def read(index, lo, size):
        ref, offset, width = blocks[index]
        return refs[ref][0, pl.ds(offset, width), pl.ds(lo, size)]

    def base_of(info):
        def base(index):
            ref, offset, unused = blocks[index]
            if relative:
                return info[0] - ref * rows
            return offset
        return base

    return read, base_of


def attend_kernel(blocks, nrefs, relative, info, query_ref, *refs):
    kv_refs = refs[:nrefs]
    out_ref = refs[nrefs]
    slot = pl.program_id(0)
    rows, width = query_ref.shape[1], query_ref.shape[2]
    read, base_of = block_reader(kv_refs, blocks, rows, relative)
    base = base_of(info)
    for lo, size in head_groups(width):
        query = query_ref[0, :, pl.ds(lo, size)]
        lane = lax.broadcasted_iota(jnp.int32, (rows, size), 1)
        keys = [read(i, lo, size) for i in range(len(blocks))]
        values = [read(i, width + lo, size) for i in range(len(blocks))]
        result = None
        for head in range(size // HD):
            part = (lane // HD) == head
            one = query if size == HD else jnp.where(part, query, jnp.zeros_like(query))
            scores = masked_scores(info, slot, rows, one, keys, base)
            raised, total = soft_parts(scores)
            held = functools.reduce(
                jnp.add, [dense(r.astype(BF), v) for r, v in zip(raised, values)]
            )
            held = held / total
            result = held if result is None else jnp.where(part, held, result)
        out_ref[0, :, pl.ds(lo, size)] = result.astype(out_ref.dtype)


def back_kernel(blocks, nrefs, relative, info, query_ref, d_out_ref, *refs):
    kv_refs = refs[:nrefs]
    d_query_ref = refs[nrefs]
    d_refs = refs[nrefs + 1:]
    slot = pl.program_id(0)
    rows, width = query_ref.shape[1], query_ref.shape[2]
    scale = HD ** (-0.5)
    read, base_of = block_reader(kv_refs, blocks, rows, relative)
    base = base_of(info)
    for lo, size in head_groups(width):
        query = query_ref[0, :, pl.ds(lo, size)]
        d_out = d_out_ref[0, :, pl.ds(lo, size)]
        lane = lax.broadcasted_iota(jnp.int32, (rows, size), 1)
        keys = [read(i, lo, size) for i in range(len(blocks))]
        values = [read(i, width + lo, size) for i in range(len(blocks))]
        d_query = None
        d_keys = [None] * len(blocks)
        d_values = [None] * len(blocks)
        for head in range(size // HD):
            part = (lane // HD) == head
            if size == HD:
                one, d_one = query, d_out
            else:
                one = jnp.where(part, query, jnp.zeros_like(query))
                d_one = jnp.where(part, d_out, jnp.zeros_like(d_out))
            scores = masked_scores(info, slot, rows, one, keys, base)
            raised, total = soft_parts(scores)
            inverse = 1.0 / total
            probs = [r * inverse for r in raised]
            d_probs = [dense_nt(d_one, v) for v in values]
            delta = functools.reduce(
                jnp.add, [jnp.sum(p * d, axis=-1, keepdims=True) for p, d in zip(probs, d_probs)]
            )
            d_scores = [(p * (d - delta)).astype(BF) for p, d in zip(probs, d_probs)]
            held = functools.reduce(jnp.add, [dense(s, k) for s, k in zip(d_scores, keys)])
            d_query = held if d_query is None else jnp.where(part, held, d_query)
            for i in range(len(blocks)):
                dk = dense_tn(d_scores[i], one)
                dv = dense_tn(probs[i].astype(BF), d_one)
                d_keys[i] = dk if d_keys[i] is None else d_keys[i] + dk
                d_values[i] = dv if d_values[i] is None else d_values[i] + dv
        d_query_ref[0, :, pl.ds(lo, size)] = (d_query * scale).astype(d_query_ref.dtype)
        for i, (ref, offset, bw) in enumerate(blocks):
            target = d_refs[ref]
            target[0, pl.ds(offset, bw), pl.ds(lo, size)] = (d_keys[i] * scale).astype(target.dtype)
            target[0, pl.ds(offset, bw), pl.ds(width + lo, size)] = d_values[i].astype(target.dtype)


def slot_spec(shape):
    return pl.BlockSpec((1,) + tuple(shape[1:]), lambda s: (s, 0, 0))


def block_list(kv_list):
    if len(kv_list) > 1:
        return [(i, 0, item.shape[1]) for i, item in enumerate(kv_list)], True
    length = kv_list[0].shape[1]
    width = math.gcd(length, 512)
    return [(0, j * width, width) for j in range(length // width)], False


def attend(info, query, kv_list, name):
    blocks, relative = block_list(kv_list)
    slots, rows, width = query.shape
    keys = sum(item.shape[1] for item in kv_list)
    heads = width // HD
    return pl.pallas_call(
        functools.partial(attend_kernel, blocks, len(kv_list), relative),
        grid=(slots,),
        in_specs=[pl.BlockSpec(memory_space=pltpu.SMEM), slot_spec(query.shape)]
        + [slot_spec(item.shape) for item in kv_list],
        out_specs=slot_spec(query.shape),
        out_shape=jax.ShapeDtypeStruct(query.shape, BF),
        cost_estimate=pl.CostEstimate(
            flops=4 * slots * heads * rows * keys * HD,
            bytes_accessed=4 * slots * (rows + keys) * width,
            transcendentals=slots * heads * rows * keys,
        ),
        name=name,
    )(info, query, *kv_list)


def attend_back(info, query, d_out, kv_list, name):
    blocks, relative = block_list(kv_list)
    slots, rows, width = query.shape
    keys = sum(item.shape[1] for item in kv_list)
    heads = width // HD
    d_shapes = [
        jax.ShapeDtypeStruct(item.shape, F32 if (relative and i == 0) else BF)
        for i, item in enumerate(kv_list)
    ]
    outs = pl.pallas_call(
        functools.partial(back_kernel, blocks, len(kv_list), relative),
        grid=(slots,),
        in_specs=[
            pl.BlockSpec(memory_space=pltpu.SMEM),
            slot_spec(query.shape),
            slot_spec(query.shape),
        ]
        + [slot_spec(item.shape) for item in kv_list],
        out_specs=[slot_spec(query.shape)] + [slot_spec(item.shape) for item in kv_list],
        out_shape=[jax.ShapeDtypeStruct(query.shape, BF)] + d_shapes,
        cost_estimate=pl.CostEstimate(
            flops=10 * slots * heads * rows * keys * HD,
            bytes_accessed=4 * slots * (rows + 2 * keys) * width,
            transcendentals=slots * heads * rows * keys,
        ),
        name=name,
    )(info, query, d_out, *kv_list)
    return outs[0], list(outs[1:])


def make_body(n_dp, n_ctx, n_tp):
    def swap(x, axis, size, bit):
        return lax.ppermute(x, axis, [(i, i ^ bit) for i in range(size)])

    def pick(flag, first, second):
        return jnp.where(flag, first, second)

    def body(
        teacher_in,
        teacher_gain_a,
        teacher_shift_a,
        teacher_attn_in,
        teacher_attn_bias,
        teacher_attn_out,
        teacher_out_bias,
        teacher_gain_b,
        teacher_shift_b,
        teacher_up,
        teacher_up_bias,
        teacher_down,
        teacher_down_bias,
        student_in,
        student_gain_a,
        student_shift_a,
        student_attn_in,
        student_attn_bias,
        student_attn_out,
        student_out_bias,
        student_gain_b,
        student_shift_b,
        student_up,
        student_up_bias,
        student_down,
        student_down_bias,
        out_grad,
        slot_lengths,
    ):
        slots, rows, wide = teacher_in.shape
        narrow = student_in.shape[2]
        total = slots * rows
        s_cols = student_attn_in.shape[2]
        dp = lax.axis_index("dp")
        ctx = lax.axis_index("ctx")
        tp = lax.axis_index("tp")
        first = dp == 0
        even = (tp % 2) == 0
        local_lengths = lax.dynamic_slice_in_dim(slot_lengths, dp * slots, slots)
        info = jnp.concatenate([(ctx * rows)[None].astype(jnp.int32), local_lengths])

        def halves(x):
            mid = x.shape[-1] // 2
            left, right = x[..., :mid], x[..., mid:]
            return pick(first, left, right), pick(first, right, left)

        def join(own, peer):
            return pick(
                first,
                jnp.concatenate([own, peer], axis=-1),
                jnp.concatenate([peer, own], axis=-1),
            )

        def tp_sum(x):
            half = x.shape[0] // 2
            low, high = x[:half], x[half:]
            keep = pick(even, low, high)
            give = pick(even, high, low).astype(BF)
            keep = (keep + swap(give, "tp", n_tp, 1).astype(F32)).astype(BF)
            keep = (keep.astype(F32) + swap(keep, "tp", n_tp, 2).astype(F32)).astype(BF)
            other = swap(keep, "tp", n_tp, 1)
            return pick(
                even,
                jnp.concatenate([keep, other], axis=0),
                jnp.concatenate([other, keep], axis=0),
            ).astype(F32)

        def gather_keys(kv):
            if n_ctx > 4:
                return [lax.all_gather(kv, "ctx", axis=1, tiled=True)]
            out = [kv]
            for k in range(1, n_ctx):
                out.append(lax.ppermute(kv, "ctx", [(i, i + k) for i in range(n_ctx - k)]))
            return out

        def scatter_keys(parts):
            if n_ctx > 4:
                return lax.psum_scatter(
                    parts[0], "ctx", scatter_dimension=1, tiled=True
                ).astype(F32)
            out = parts[0]
            for k in range(1, n_ctx):
                got = lax.ppermute(parts[k], "ctx", [(i + k, i) for i in range(n_ctx - k)])
                out = out + got.astype(F32)
            return out

        def grad_scatter(g):
            half = g.shape[0] // n_dp
            keep = lax.dynamic_slice_in_dim(g, dp * half, half)
            give = lax.dynamic_slice_in_dim(g, (1 - dp) * half, half).astype(BF)
            keep = keep + swap(give, "dp", n_dp, 1).astype(F32)
            if n_ctx > 4:
                return lax.psum_scatter(
                    keep.astype(BF), "ctx", scatter_dimension=0, tiled=True
                ).astype(F32)
            piece = half // n_ctx
            out = lax.dynamic_slice_in_dim(keep, ctx * piece, piece)
            low = keep.astype(BF)
            for k in range(1, n_ctx):
                give = lax.dynamic_slice_in_dim(low, ((ctx + k) % n_ctx) * piece, piece)
                got = lax.ppermute(give, "ctx", [(i, (i + k) % n_ctx) for i in range(n_ctx)])
                out = out + got.astype(F32)
            return out

        def small_sum(v):
            v = v + swap(v, "dp", n_dp, 1)
            bit = 1
            while bit < n_ctx:
                v = v + swap(v, "ctx", n_ctx, bit)
                bit *= 2
            return v

        peer_qkv = swap(student_attn_in, "dp", n_dp, 1)
        t_x = teacher_in.reshape(total, wide).astype(F32)
        t_hat, unused = norm_parts(t_x)
        t_normed = (t_hat * teacher_gain_a.astype(F32) + teacher_shift_a.astype(F32)).astype(BF)
        t_mine, t_theirs = halves(t_normed)
        t_other = swap(t_theirs, "dp", n_dp, 1)

        gain_a = student_gain_a.astype(F32)
        gain_b = student_gain_b.astype(F32)
        s_x = student_in.reshape(total, narrow).astype(F32)
        s_hat, s_factor = norm_parts(s_x)
        s_normed = (s_hat * gain_a + student_shift_a.astype(F32)).astype(BF)
        s_mine, s_theirs = halves(s_normed)
        s_bias = student_attn_bias.astype(F32)

        def s_project(i):
            return dense(s_mine, student_attn_in[i]) + dense(s_theirs, peer_qkv[i])

        s_k = s_project(1).astype(BF)
        s_v = (s_project(2) + s_bias[1]).astype(BF)
        s_kv = jnp.concatenate([s_k, s_v], axis=1).reshape(slots, rows, 2 * s_cols)
        s_q = (s_project(0) + s_bias[0]).astype(BF).reshape(slots, rows, s_cols)
        s_kv_list = gather_keys(s_kv)

        peer_out = swap(student_attn_out, "dp", n_dp, 1)
        peer_up = swap(student_up, "dp", n_dp, 1)
        peer_down = swap(student_down, "dp", n_dp, 1)

        heads = wide // HD
        step = heads // n_tp
        group = heads - step * (n_tp - 1)
        t_cols = group * HD
        col0 = tp * (step * HD)
        w_in = lax.dynamic_slice_in_dim(teacher_attn_in, col0, t_cols, axis=2)
        t_bias = lax.dynamic_slice_in_dim(teacher_attn_bias, col0, t_cols, axis=1).astype(F32)
        t_rows = jnp.concatenate([t_mine, t_other], axis=0)
        k_part = dense(t_rows, w_in[1])
        v_part = dense(t_rows, w_in[2])
        q_part = dense(t_rows, w_in[0])
        kv_own = jnp.concatenate([k_part[:total], v_part[:total]], axis=1)
        kv_give = jnp.concatenate([k_part[total:].astype(BF), v_part[total:].astype(BF)], axis=1)
        kv_got = swap(kv_give, "dp", n_dp, 1)
        q_got = swap(q_part[total:].astype(BF), "dp", n_dp, 1)
        kv_bias = jnp.concatenate([jnp.zeros_like(t_bias[0]), t_bias[1]])
        t_kv = (kv_own + kv_got.astype(F32) + kv_bias).astype(BF).reshape(slots, rows, 2 * t_cols)
        t_q = (q_part[:total] + q_got.astype(F32) + t_bias[0]).astype(BF)
        t_q = t_q.reshape(slots, rows, t_cols)
        t_kv_list = gather_keys(t_kv)

        w_out = lax.dynamic_slice_in_dim(teacher_attn_out, col0, t_cols, axis=1)
        w_out_peer = swap(w_out, "dp", n_dp, 1)
        t_up = lax.all_gather(teacher_up, "dp", axis=0, tiled=True)
        t_down = lax.all_gather(teacher_down, "dp", axis=1, tiled=True)

        s_att = attend(info, s_q, s_kv_list, "student_attend").reshape(total, s_cols)
        s_branch = tp_sum(join(dense(s_att, student_attn_out), dense(s_att, peer_out)))
        s_mid = s_x + s_branch + student_out_bias.astype(F32)
        b_hat, b_factor = norm_parts(s_mid)
        b_normed = (b_hat * gain_b + student_shift_b.astype(F32)).astype(BF)
        b_mine, b_theirs = halves(b_normed)
        upper = dense(b_mine, student_up) + dense(b_theirs, peer_up) + student_up_bias.astype(F32)
        act, slope = gelu_both(upper)
        act = act.astype(BF)
        s_result_part = join(dense(act, student_down), dense(act, peer_down))

        place = ctx * rows + jnp.arange(rows, dtype=jnp.int32)
        keeper = (place[None, :] < local_lengths[:, None]).astype(F32).reshape(total, 1)
        cot = out_grad.reshape(total, narrow).astype(F32) * keeper
        d_b = cot.astype(BF)
        d_mine, d_theirs = halves(d_b)
        d_act = (dense_nt(d_mine, student_down) + dense_nt(d_theirs, peer_down)).astype(BF)
        d_upper = (d_act.astype(F32) * slope).astype(BF)
        d_norm_b = tp_sum(join(dense_nt(d_upper, student_up), dense_nt(d_upper, peer_up)))
        g_down = dense_tn(d_b, act)
        g_up = dense_tn(b_normed, d_upper)
        g_ffn = grad_scatter(jnp.concatenate([g_down, g_up], axis=1))
        d_mid = cot + norm_back(d_norm_b, b_hat, b_factor, gain_b)
        d_a = d_mid.astype(BF)
        a_mine, a_theirs = halves(d_a)
        d_att = (dense_nt(a_mine, student_attn_out) + dense_nt(a_theirs, peer_out)).astype(BF)
        d_q, d_kv_parts = attend_back(
            info, s_q, d_att.reshape(slots, rows, s_cols), s_kv_list, "student_back"
        )
        d_kv = scatter_keys(d_kv_parts).astype(BF)
        d_q = d_q.reshape(total, s_cols)
        d_kv = d_kv.reshape(total, 2 * s_cols)
        d_k, d_v = d_kv[:, :s_cols], d_kv[:, s_cols:]
        d_norm_a = tp_sum(
            join(
                dense_nt(d_q, student_attn_in[0])
                + dense_nt(d_k, student_attn_in[1])
                + dense_nt(d_v, student_attn_in[2]),
                dense_nt(d_q, peer_qkv[0])
                + dense_nt(d_k, peer_qkv[1])
                + dense_nt(d_v, peer_qkv[2]),
            )
        )
        g_att = grad_scatter(
            jnp.concatenate(
                [dense_tn(s_normed, d_q), dense_tn(s_normed, d_kv), dense_tn(d_a, s_att)], axis=1
            )
        )
        in_grad = d_mid + norm_back(d_norm_a, s_hat, s_factor, gain_a)

        t_att = attend(info, t_q, t_kv_list, "teacher_attend").reshape(total, t_cols)

        def spread(x):
            every = lax.all_gather(x, "tp", axis=0)
            parts = [every[i][:, : step * HD] for i in range(n_tp - 1)] + [every[n_tp - 1]]
            return jnp.concatenate(parts, axis=1)

        o_mine, o_theirs = halves(spread(t_att))
        t_branch = spread((dense(o_mine, w_out) + dense(o_theirs, w_out_peer)).astype(BF))
        t_mid = t_x + t_branch.astype(F32) + teacher_out_bias.astype(F32)
        m_hat, unused = norm_parts(t_mid)
        m_normed = (m_hat * teacher_gain_b.astype(F32) + teacher_shift_b.astype(F32)).astype(BF)
        t_act = gelu_tanh(dense(m_normed, t_up) + teacher_up_bias.astype(F32)).astype(BF)
        t_part = dense(t_act, t_down)
        both = tp_sum(jnp.concatenate([t_part, s_result_part], axis=1))
        t_result = (t_mid + both[:, :wide] + teacher_down_bias.astype(F32)).astype(BF)
        s_result = (s_mid + both[:, wide:] + student_down_bias.astype(F32)).astype(BF)

        early = small_sum(
            jnp.concatenate(
                [
                    jnp.sum(d_b.astype(F32), axis=0),
                    jnp.sum(d_norm_b * b_hat, axis=0),
                    jnp.sum(d_norm_b, axis=0),
                    jnp.sum(d_a.astype(F32), axis=0),
                    jnp.sum(d_upper.astype(F32), axis=0),
                ]
            )
        )
        late = small_sum(
            jnp.concatenate(
                [
                    jnp.sum(d_norm_a * s_hat, axis=0),
                    jnp.sum(d_norm_a, axis=0),
                    jnp.sum(d_q.astype(F32), axis=0),
                    jnp.sum(d_v.astype(F32), axis=0),
                ]
            )
        )
        piece = narrow // (n_dp * n_ctx)
        at = (dp * n_ctx + ctx) * piece

        def shard(v, index):
            return lax.dynamic_slice_in_dim(v, index * narrow + at, piece)

        hidden = student_up.shape[1]
        grad_down = g_ffn[:, :hidden].T
        grad_up = g_ffn[:, hidden:]
        grad_attn_in = jnp.stack([g_att[:, i * s_cols:(i + 1) * s_cols] for i in range(3)])
        grad_attn_out = g_att[:, 3 * s_cols:].T
        return (
            t_result.reshape(slots, rows, wide),
            s_result.reshape(slots, rows, narrow),
            in_grad.reshape(slots, rows, narrow),
            shard(late, 0),
            shard(late, 1),
            grad_attn_in,
            late[2 * narrow:].reshape(2, s_cols),
            grad_attn_out,
            shard(early, 3),
            shard(early, 1),
            shard(early, 2),
            grad_up,
            early[4 * narrow:],
            grad_down,
            shard(early, 0),
        )

    return body


def solution(mesh):
    sizes = mesh.shape
    return jax.shard_map(
        make_body(sizes["dp"], sizes["ctx"], sizes["tp"]),
        mesh=mesh,
        in_specs=(
            P("dp", "ctx", None),
            P(),
            P(),
            P(None, "dp", None),
            P(),
            P("dp", None),
            P(),
            P(),
            P(),
            P("dp", "tp"),
            P("tp"),
            P("tp", "dp"),
            P(),
            P("dp", "ctx", None),
            P(),
            P(),
            P(None, "dp", "tp"),
            P(None, "tp"),
            P("tp", "dp"),
            P(),
            P(),
            P(),
            P("dp", "tp"),
            P("tp"),
            P("tp", "dp"),
            P(),
            P("dp", "ctx", None),
            P(),
        ),
        out_specs=(
            P("dp", "ctx", None),
            P("dp", "ctx", None),
            P("dp", "ctx", None),
            P(("dp", "ctx")),
            P(("dp", "ctx")),
            P(None, ("dp", "ctx"), "tp"),
            P(None, "tp"),
            P("tp", ("dp", "ctx")),
            P(("dp", "ctx")),
            P(("dp", "ctx")),
            P(("dp", "ctx")),
            P(("dp", "ctx"), "tp"),
            P("tp"),
            P("tp", ("dp", "ctx")),
            P(("dp", "ctx")),
        ),
        check_vma=False,
    )
```

```python
import functools
import math

import jax
import jax.numpy as jnp
from jax import lax
from jax.experimental import pallas as pl
from jax.experimental.pallas import tpu as pltpu
from jax.sharding import PartitionSpec as P

HD = 64
PAIR = 2 * HD
EPS = 1e-05
MASKED = -1000000000.0
FAR = 1 << 30
BF = jnp.bfloat16
F32 = jnp.float32
GELU_C = math.sqrt(2.0 / math.pi)
SMEM = pl.BlockSpec(memory_space=pltpu.SMEM)
VMEM = pl.BlockSpec(memory_space=pltpu.VMEM)
ANY = pl.BlockSpec(memory_space=pl.ANY)
LIMIT = 60 * 1024 * 1024


def dense(left, right):
    return jnp.dot(left, right, preferred_element_type=F32)


def dense_tn(left, right):
    return lax.dot_general(left, right, (((0,), (0,)), ((), ())), preferred_element_type=F32)


def dense_nt(left, right):
    return lax.dot_general(left, right, (((1,), (1,)), ((), ())), preferred_element_type=F32)


def norm_parts(x):
    centered = x - jnp.mean(x, axis=-1, keepdims=True)
    spread = jnp.mean(centered * centered, axis=-1, keepdims=True)
    factor = lax.rsqrt(spread + EPS)
    return centered * factor, factor


def norm_back(d_out, xhat, factor, gain):
    e = d_out * gain
    return factor * (
        e - jnp.mean(e, axis=-1, keepdims=True) - xhat * jnp.mean(e * xhat, axis=-1, keepdims=True)
    )


def gelu_tanh(v):
    return 0.5 * v * (1.0 + jnp.tanh(GELU_C * (v + 0.044715 * v * v * v)))


def gelu_both(v):
    inner = jnp.tanh(GELU_C * (v + 0.044715 * v * v * v))
    slope = 0.5 * (1.0 + inner) + 0.5 * v * (1.0 - inner * inner) * GELU_C * (
        1.0 + 3.0 * 0.044715 * v * v
    )
    return 0.5 * v * (1.0 + inner), slope


BASE, DP, ODD, TP, CTX, LEN = 0, 1, 2, 3, 4, 5


def row(ref):
    return ref[...].astype(F32).reshape(1, -1)


def halves(info, x):
    mid = x.shape[-1] // 2
    first = info[DP] == 0
    left, right = x[:, :mid], x[:, mid:]
    return jnp.where(first, left, right), jnp.where(first, right, left)


def ordered(info, own_peer):
    mid = own_peer.shape[-1] // 2
    first = info[DP] == 0
    own, peer = own_peer[:, :mid], own_peer[:, mid:]
    return jnp.concatenate(
        [jnp.where(first, own, peer), jnp.where(first, peer, own)], axis=-1
    )


def run(kernel, name, outs, args, specs=None, scratch=(), flops=0, extra=0):
    out_shape = [jax.ShapeDtypeStruct(shape, kind) for shape, kind in outs]
    if specs is None:
        specs = [SMEM] + [VMEM] * (len(args) - 1)
    moved = sum(a.size * a.dtype.itemsize for a in args)
    moved += sum(math.prod(o.shape) * o.dtype.itemsize for o in out_shape)
    return pl.pallas_call(
        kernel,
        out_shape=out_shape,
        in_specs=specs,
        out_specs=[VMEM] * len(outs),
        scratch_shapes=list(scratch),
        compiler_params=pltpu.CompilerParams(vmem_limit_bytes=LIMIT),
        cost_estimate=pl.CostEstimate(
            flops=int(flops), bytes_accessed=int(moved), transcendentals=int(extra)
        ),
        name=name,
    )(*args)


def kv_tiles(heads):
    pairs = heads // 2
    return pairs, heads % 2, pairs * 2 * PAIR + (heads % 2) * PAIR


def put_kv(ref, k, v, heads):
    pairs, single, unused = kv_tiles(heads)
    for g in range(pairs):
        ref[:, 2 * g * PAIR:(2 * g + 1) * PAIR] = k[:, g * PAIR:(g + 1) * PAIR].astype(ref.dtype)
        ref[:, (2 * g + 1) * PAIR:(2 * g + 2) * PAIR] = v[:, g * PAIR:(g + 1) * PAIR].astype(
            ref.dtype
        )
    if single:
        tail = jnp.concatenate([k[:, pairs * PAIR:], v[:, pairs * PAIR:]], axis=1)
        ref[:, 2 * pairs * PAIR:] = tail.astype(ref.dtype)


def put_q(ref, q, heads):
    pairs, single, unused = kv_tiles(heads)
    q = q * (HD ** -0.5)
    ref[:, :pairs * PAIR] = q[:, :pairs * PAIR].astype(ref.dtype)
    if single:
        tail = q[:, pairs * PAIR:]
        ref[:, pairs * PAIR:] = jnp.concatenate([tail, jnp.zeros_like(tail)], axis=1).astype(
            ref.dtype
        )


def chunks_of(keys):
    width = math.gcd(keys, 512)
    return [(i * width, width) for i in range(keys // width)]


def key_rows(info, rows, blocks, chunks):
    out = []
    for start, width in chunks:
        place = start + lax.broadcasted_iota(jnp.int32, (1, width), 1)
        if blocks > 1:
            place = info[BASE] + place - 2 * rows * (place // rows)
            place = jnp.where(place < 0, FAR, place)
        out.append(place)
    return out


def soft(query, keys, places, bound):
    scores = [
        jnp.where(place <= bound, dense_nt(query, k), MASKED) for place, k in zip(places, keys)
    ]
    top = functools.reduce(jnp.maximum, [jnp.max(s, axis=-1, keepdims=True) for s in scores])
    raised = [jnp.exp(s - top) for s in scores]
    total = functools.reduce(jnp.add, [jnp.sum(r, axis=-1, keepdims=True) for r in raised])
    return raised, 1.0 / total


def add_all(items):
    return functools.reduce(jnp.add, items)


def query_bound(info, slot, rows):
    place = info[BASE] + lax.broadcasted_iota(jnp.int32, (rows, 1), 0)
    return jnp.minimum(place, info[LEN + slot] - 1)


def attend_slot(query_of, kv_of, heads, rows, places, bound):
    pairs, single, unused = kv_tiles(heads)
    lane = lax.broadcasted_iota(jnp.int32, (rows, PAIR), 1)
    low = lane < HD
    out = []
    for g in range(pairs):
        query = query_of(g)
        keys, values = kv_of(2 * g), kv_of(2 * g + 1)
        held = []
        for part in (low, jnp.logical_not(low)):
            one = jnp.where(part, query, jnp.zeros_like(query))
            raised, inverse = soft(one, keys, places, bound)
            held.append(add_all([dense(r.astype(BF), v) for r, v in zip(raised, values)]) * inverse)
        out.append(jnp.where(low, held[0], held[1]))
    if single:
        keys = kv_of(2 * pairs)
        raised, inverse = soft(query_of(pairs), keys, places, bound)
        held = add_all([dense(r.astype(BF), v) for r, v in zip(raised, keys)]) * inverse
        out.append(held[:, HD:])
    return out


def load_blocks(kv_s, kv_refs, slot, rows):
    if kv_s is not None:
        for i, ref in enumerate(kv_refs):
            kv_s[i * rows:(i + 1) * rows, :] = ref[slot]


def kv_reader(kv_s, kv_refs, slot, chunks):
    def kv_of(tile):
        if kv_s is not None:
            return [kv_s[a:a + w, tile * PAIR:(tile + 1) * PAIR] for a, w in chunks]
        return [kv_refs[0][slot, a:a + w, tile * PAIR:(tile + 1) * PAIR] for a, w in chunks]
    return kv_of


def student_attend_kernel(heads, blocks, info, q_ref, own_ref, peer_ref, *refs):
    kv_refs = refs[:blocks]
    att_ref, give_ref, keep_ref = refs[blocks:blocks + 3]
    kv_s = refs[blocks + 3] if blocks > 1 else None
    slots, rows, unused = q_ref.shape
    keys = blocks * kv_refs[0].shape[1]
    chunks = chunks_of(keys)
    half = own_ref.shape[1]

    def one_slot(i, carry):
        slot = jnp.where(i == 0, 1 - info[ODD], info[ODD])
        load_blocks(kv_s, kv_refs, slot, rows)
        out = attend_slot(
            lambda g: q_ref[slot, :, g * PAIR:(g + 1) * PAIR],
            kv_reader(kv_s, kv_refs, slot, chunks),
            heads,
            rows,
            key_rows(info, rows, blocks, chunks),
            query_bound(info, slot, rows),
        )
        att = jnp.concatenate(out, axis=1).astype(BF)
        att_ref[slot] = att
        part = jnp.concatenate([dense(att, own_ref[...]), dense(att, peer_ref[...])], axis=1)

        @pl.when(i == 0)
        def _():
            give_ref[...] = part.astype(BF)

        @pl.when(i == 1)
        def _():
            keep_ref[...] = part

        return carry

    lax.fori_loop(0, slots, one_slot, 0)


def teacher_attend_kernel(heads, blocks, info, q_ref, *refs):
    kv_refs = refs[:blocks]
    att_ref, tail_ref = refs[blocks:blocks + 2]
    kv_s = refs[blocks + 2] if blocks > 1 else None
    slots, rows, unused = q_ref.shape
    chunks = chunks_of(blocks * kv_refs[0].shape[1])
    pairs = heads // 2

    def one_slot(slot, carry):
        load_blocks(kv_s, kv_refs, slot, rows)
        out = attend_slot(
            lambda g: q_ref[slot, :, g * PAIR:(g + 1) * PAIR],
            kv_reader(kv_s, kv_refs, slot, chunks),
            heads,
            rows,
            key_rows(info, rows, blocks, chunks),
            query_bound(info, slot, rows),
        )
        for g in range(pairs):
            att_ref[slot, :, g * PAIR:(g + 1) * PAIR] = out[g].astype(BF)
        tail_ref[slot] = out[pairs].astype(BF)
        return carry

    lax.fori_loop(0, slots, one_slot, 0)


def keep_mask(info, slots, rows):
    row = lax.broadcasted_iota(jnp.int32, (rows, 1), 0) + info[BASE]
    return jnp.concatenate([row < info[LEN + s] for s in range(slots)], axis=0)


def student_back_kernel(
    heads, blocks, info, mid_ref, gain, r_ref, other_ref, grad_ref, own_ref, peer_ref, q_ref, *refs
):
    kv_refs = refs[:blocks]
    d_mid_ref, d_a_ref, d_q_ref, sums_ref = refs[blocks:blocks + 4]
    d_refs = refs[blocks + 4:2 * blocks + 4]
    d_att_s = refs[2 * blocks + 4]
    d_s = refs[2 * blocks + 5]
    kv_s = refs[2 * blocks + 6] if blocks > 1 else None
    slots, rows, unused = q_ref.shape
    chunks = chunks_of(blocks * kv_refs[0].shape[1])
    pairs, single, unused = kv_tiles(heads)
    scale = HD ** -0.5

    d_s[pl.ds(info[ODD] * rows, rows), :] = ordered(info, r_ref[...]).astype(F32)
    d_s[pl.ds((1 - info[ODD]) * rows, rows), :] = ordered(info, other_ref[...]).astype(F32)
    xhat, factor = norm_parts(mid_ref[...])
    d_norm = d_s[...]
    cot = jnp.where(keep_mask(info, slots, rows), grad_ref[...].astype(F32), 0.0)
    d_mid = cot + norm_back(d_norm, xhat, factor, row(gain))
    d_a = d_mid.astype(BF)
    d_mid_ref[...] = d_mid
    d_a_ref[...] = d_a
    sums_ref[0:1, :] = jnp.sum(d_norm * xhat, axis=0, keepdims=True)
    sums_ref[1:2, :] = jnp.sum(d_norm, axis=0, keepdims=True)
    sums_ref[2:3, :] = jnp.sum(d_a.astype(F32), axis=0, keepdims=True)
    mine, theirs = halves(info, d_a)
    d_att = dense_nt(mine, own_ref[...]) + dense_nt(theirs, peer_ref[...])
    width = heads * HD
    d_att_s[:, :pairs * PAIR] = d_att[:, :pairs * PAIR].astype(BF)
    if single:
        tail = d_att[:, pairs * PAIR:width]
        d_att_s[:, pairs * PAIR:] = jnp.concatenate([jnp.zeros_like(tail), tail], axis=1).astype(BF)

    def put(slot, tile, i, value):
        start, size = chunks[i]
        if blocks == 1:
            d_refs[0][slot, start:start + size, tile * PAIR:(tile + 1) * PAIR] = value.astype(
                d_refs[0].dtype
            )
        else:
            for b in range(blocks):
                d_refs[b][slot, :, tile * PAIR:(tile + 1) * PAIR] = value[
                    b * rows:(b + 1) * rows
                ].astype(d_refs[b].dtype)

    def one_slot(slot, carry):
        load_blocks(kv_s, kv_refs, slot, rows)
        kv_of = kv_reader(kv_s, kv_refs, slot, chunks)
        places = key_rows(info, rows, blocks, chunks)
        bound = query_bound(info, slot, rows)
        low = lax.broadcasted_iota(jnp.int32, (rows, PAIR), 1) < HD
        row0 = pl.multiple_of(slot * rows, rows)

        def head(query, d_out, keys, values):
            raised, inverse = soft(query, keys, places, bound)
            probs = [r * inverse for r in raised]
            d_probs = [dense_nt(d_out, v) for v in values]
            delta = add_all(
                [jnp.sum(p * d, axis=-1, keepdims=True) for p, d in zip(probs, d_probs)]
            )
            d_scores = [(p * (d - delta)).astype(BF) for p, d in zip(probs, d_probs)]
            d_query = add_all([dense(s, k) for s, k in zip(d_scores, keys)]) * scale
            d_keys = [dense_tn(s, query) for s in d_scores]
            d_values = [dense_tn(p.astype(BF), d_out) for p in probs]
            return d_query, d_keys, d_values

        for g in range(pairs):
            query = q_ref[slot, :, g * PAIR:(g + 1) * PAIR]
            d_out = d_att_s[pl.ds(row0, rows), g * PAIR:(g + 1) * PAIR]
            keys, values = kv_of(2 * g), kv_of(2 * g + 1)
            zero = jnp.zeros_like(query)
            a = head(jnp.where(low, query, zero), jnp.where(low, d_out, zero), keys, values)
            b = head(jnp.where(low, zero, query), jnp.where(low, zero, d_out), keys, values)
            d_q_ref[slot, :, g * PAIR:(g + 1) * PAIR] = jnp.where(low, a[0], b[0]).astype(BF)
            for i in range(len(chunks)):
                put(slot, 2 * g, i, a[1][i] + b[1][i])
                put(slot, 2 * g + 1, i, a[2][i] + b[2][i])
        if single:
            query = q_ref[slot, :, pairs * PAIR:]
            d_out = d_att_s[pl.ds(row0, rows), pairs * PAIR:]
            keys = kv_of(2 * pairs)
            a = head(query, d_out, keys, keys)
            d_q_ref[slot, :, pairs * PAIR:] = a[0][:, :HD].astype(BF)
            for i in range(len(chunks)):
                put(slot, 2 * pairs, i, a[1][i] + a[2][i])
        return carry

    lax.fori_loop(0, slots, one_slot, 0)


def student_qkv_kernel(heads, info, x, gain, shift, own, peer, bias, normed_ref, q_ref, kv_ref):
    xhat, unused = norm_parts(x[...].astype(F32))
    normed = (xhat * row(gain) + row(shift)).astype(BF)
    normed_ref[...] = normed
    mine, theirs = halves(info, normed)

    def project(i):
        return dense_nt(mine, own[i]) + dense_nt(theirs, peer[i])

    put_kv(kv_ref, project(1), project(2) + bias[1:2, :].astype(F32), heads)
    put_q(q_ref, (project(0) + bias[0:1, :].astype(F32)).astype(BF), heads)


def student_ffn_kernel(
    info, x, out_bias, gain, shift, up_bias, r_ref, other_ref, up_own, up_peer, down_own,
    down_peer, grad, mid_ref, normed_ref, act_ref, d_upper_ref, give_ref, keep_ref, part_s,
):
    rows = r_ref.shape[0]
    slots = x.shape[0] // rows
    keep_at = pl.multiple_of(info[ODD] * rows, rows)
    give_at = pl.multiple_of((1 - info[ODD]) * rows, rows)
    for at, ref in ((keep_at, r_ref), (give_at, other_ref)):
        mid_ref[pl.ds(at, rows), :] = (
            x[pl.ds(at, rows), :].astype(F32) + ordered(info, ref[...]).astype(F32) + row(out_bias)
        )
    xhat, unused = norm_parts(mid_ref[...])
    normed = (xhat * row(gain) + row(shift)).astype(BF)
    normed_ref[...] = normed
    mine, theirs = halves(info, normed)
    upper = dense(mine, up_own[...]) + dense(theirs, up_peer[...]) + row(up_bias)
    act, slope = gelu_both(upper)
    act_ref[...] = act.astype(BF)
    d_b = jnp.where(keep_mask(info, slots, rows), grad[...].astype(F32), 0.0).astype(BF)
    d_mine, d_theirs = halves(info, d_b)
    d_act = (dense_nt(d_mine, down_own[...]) + dense_nt(d_theirs, down_peer[...])).astype(BF)
    d_upper = (d_act.astype(F32) * slope).astype(BF)
    d_upper_ref[...] = d_upper
    half = up_own.shape[0]
    part_s[:, :half] = dense_nt(d_upper, up_own[...])
    part_s[:, half:] = dense_nt(d_upper, up_peer[...])
    give_ref[...] = part_s[pl.ds(give_at, rows), :].astype(BF)
    keep_ref[...] = part_s[pl.ds(keep_at, rows), :]


def split_rows(info, n_ctx, grad_s, give_ref, keep_ref):
    full = grad_s.shape[0]
    piece = full // (2 * n_ctx)
    bit = lax.rem(info[CTX], 2)
    for d in range(2):
        for j in range(n_ctx // 2):
            to = (d * (n_ctx // 2) + j) * piece
            base = (d * n_ctx + 2 * j) * piece
            keep_ref[to:to + piece, :] = grad_s[
                pl.ds(pl.multiple_of(base + bit * piece, 16), piece), :
            ]
            give_ref[to:to + piece, :] = grad_s[
                pl.ds(pl.multiple_of(base + (1 - bit) * piece, 16), piece), :
            ].astype(give_ref.dtype)


def student_ffn_grads_kernel(
    n_ctx, info, normed, act, d_upper, grad, down_own, down_peer,
    give_ref, keep_ref, part_give, part_keep, sums_ref, grad_s, part_s,
):
    rows = part_give.shape[0]
    slots = normed.shape[0] // rows
    d_b = jnp.where(keep_mask(info, slots, rows), grad[...].astype(F32), 0.0).astype(BF)
    hidden = act.shape[1]
    grad_s[:, :hidden] = dense_tn(d_b, act[...])
    grad_s[:, hidden:] = dense_tn(normed[...], d_upper[...])
    split_rows(info, n_ctx, grad_s, give_ref, keep_ref)
    cols = down_own.shape[1]
    part_s[:, :cols] = dense(act[...], down_own[...])
    part_s[:, cols:] = dense(act[...], down_peer[...])
    part_give[...] = part_s[pl.ds((1 - info[ODD]) * rows, rows), :].astype(BF)
    part_keep[...] = part_s[pl.ds(info[ODD] * rows, rows), :]
    sums_ref[0:1, :] = jnp.sum(d_b.astype(F32), axis=0, keepdims=True)
    sums_ref[1:2, :] = jnp.sum(d_upper[...].astype(F32), axis=0, keepdims=True)


def student_in_kernel(
    heads, n_got, n_ctx, info, d_q, normed, d_a, att, own, peer, d_kv, *refs
):
    gots = refs[:n_got]
    give_ref, keep_ref, g_give, g_keep, bias_ref, part_s, grad_s = refs[n_got:]
    rows = give_ref.shape[0]
    pairs, single, unused = kv_tiles(heads)
    total = d_kv[...].astype(F32)
    for got in gots:
        total = total + got[...].astype(F32)
    total = total.astype(BF)
    d_k = [total[:, 2 * g * PAIR:(2 * g + 1) * PAIR] for g in range(pairs)]
    d_v = [total[:, (2 * g + 1) * PAIR:(2 * g + 2) * PAIR] for g in range(pairs)]
    if single:
        d_k.append(total[:, 2 * pairs * PAIR:2 * pairs * PAIR + HD])
        d_v.append(total[:, 2 * pairs * PAIR + HD:])
    d_k = jnp.concatenate(d_k, axis=1)
    d_v = jnp.concatenate(d_v, axis=1)
    half = own.shape[2]

    def back(w):
        return dense(d_q[...], w[0]) + dense(d_k, w[1]) + dense(d_v, w[2])

    part_s[:, :half] = back(own)
    part_s[:, half:] = back(peer)
    give_ref[...] = part_s[pl.ds((1 - info[ODD]) * rows, rows), :].astype(BF)
    keep_ref[...] = part_s[pl.ds(info[ODD] * rows, rows), :]
    cols = heads * HD
    n = normed[...]
    grad_s[:, :cols] = dense_tn(n, d_q[...])
    grad_s[:, cols:2 * cols] = dense_tn(n, d_k)
    grad_s[:, 2 * cols:3 * cols] = dense_tn(n, d_v)
    grad_s[:, 3 * cols:] = dense_tn(d_a[...], att[...])
    split_rows(info, n_ctx, grad_s, g_give, g_keep)
    bias_ref[0:1, :] = jnp.sum(d_q[...].astype(F32), axis=0, keepdims=True)
    bias_ref[1:2, :] = jnp.sum(d_v.astype(F32), axis=0, keepdims=True)


def student_last_kernel(
    info, x, gain, r_ref, other_ref, d_mid, sums_b, sums_f, sums_q, out_ref, sums_ref, d_s
):
    rows = r_ref.shape[0]
    d_s[pl.ds(info[ODD] * rows, rows), :] = ordered(info, r_ref[...]).astype(F32)
    d_s[pl.ds((1 - info[ODD]) * rows, rows), :] = ordered(info, other_ref[...]).astype(F32)
    xhat, factor = norm_parts(x[...].astype(F32))
    d_norm = d_s[...]
    out_ref[...] = d_mid[...] + norm_back(d_norm, xhat, factor, row(gain))
    sums_ref[0:1, :] = jnp.sum(d_norm * xhat, axis=0, keepdims=True)
    sums_ref[1:2, :] = jnp.sum(d_norm, axis=0, keepdims=True)
    sums_ref[2:5, :] = sums_b[...]
    sums_ref[5:7, :] = sums_f[...]
    rest = out_ref.shape[1] - 2 * sums_q.shape[1]
    sums_ref[7:8, :] = jnp.concatenate(
        [sums_q[0:1, :], sums_q[1:2, :], jnp.zeros((1, rest), F32)], axis=1
    )


def teacher_norm_kernel(info, x, gain, shift, mine_ref, theirs_ref):
    xhat, unused = norm_parts(x[...].astype(F32))
    normed = (xhat * row(gain) + row(shift)).astype(BF)
    mine, theirs = halves(info, normed)
    mine_ref[...] = mine
    theirs_ref[...] = theirs


def teacher_qkv_kernel(
    heads, cols, info, mine, other, w_hbm, wo, give_ref, own_ref, wo_ref, w, w_tail, sems
):
    pairs, unused, kv_width = kv_tiles(heads)
    col0 = pl.multiple_of(info[TP] * cols, cols)
    wide = w_hbm.shape[2]
    tail = w_tail.shape[2]
    copies = [
        pltpu.make_async_copy(w_hbm.at[:, :, pl.ds(col0, cols)], w, sems.at[0]),
        pltpu.make_async_copy(w_hbm.at[:, :, pl.ds(wide - tail, tail)], w_tail, sems.at[1]),
    ]
    for copy in copies:
        copy.start()
    wo_ref[:, :cols] = wo[:, pl.ds(col0, cols)]
    last = wo[:, wide - tail:]
    wo_ref[:, cols:] = jnp.concatenate([last, jnp.zeros_like(last)], axis=1)
    for copy in copies:
        copy.wait()
    for source, target in ((other, give_ref), (mine, own_ref)):
        x = source[...]
        k, v, q = (dense(x, w[i]) for i in (1, 2, 0))
        tk, tv, tq = (dense(x, w_tail[i]) for i in (1, 2, 0))
        kind = target.dtype
        for g in range(pairs):
            a = 2 * g * PAIR
            target[:, a:a + PAIR] = k[:, g * PAIR:(g + 1) * PAIR].astype(kind)
            target[:, a + PAIR:a + 2 * PAIR] = v[:, g * PAIR:(g + 1) * PAIR].astype(kind)
        target[:, 2 * pairs * PAIR:kv_width] = jnp.concatenate([tk, tv], axis=1).astype(kind)
        target[:, kv_width:kv_width + cols] = q.astype(kind)
        target[:, kv_width + cols:] = jnp.concatenate([tq, jnp.zeros_like(tq)], axis=1).astype(kind)


def teacher_join_kernel(heads, cols, info, own, got, bias, kv_ref, q_ref):
    pairs, unused, kv_width = kv_tiles(heads)
    whole = own[...] + got[...].astype(F32)
    b = bias[:, pl.ds(pl.multiple_of(info[TP] * cols, cols), cols)].astype(F32)
    t = bias[:, bias.shape[1] - HD:].astype(F32)
    zero = jnp.zeros_like(t[0:1])
    for g in range(pairs):
        a = 2 * g * PAIR
        kv_ref[:, a:a + PAIR] = whole[:, a:a + PAIR].astype(BF)
        kv_ref[:, a + PAIR:a + 2 * PAIR] = (
            whole[:, a + PAIR:a + 2 * PAIR] + b[1:2, g * PAIR:(g + 1) * PAIR]
        ).astype(BF)
    a = 2 * pairs * PAIR
    kv_ref[:, a:] = (whole[:, a:kv_width] + jnp.concatenate([zero, t[1:2]], axis=1)).astype(BF)
    q = (whole[:, kv_width:] + jnp.concatenate([b[0:1], t[0:1], zero], axis=1)).astype(BF)
    q_ref[...] = (q * (HD ** -0.5)).astype(BF)


def teacher_out_kernel(info, every, tail, w, peer, out_ref, out_tail_ref, w_s):
    half = w.shape[0]
    n, unused, cols = every.shape
    extra = tail.shape[1]
    own_at = pl.multiple_of(info[DP] * half, 16)
    peer_at = pl.multiple_of((1 - info[DP]) * half, 16)
    w_s[pl.ds(own_at, half), :cols] = w[:, pl.ds(pl.multiple_of(info[TP] * cols, cols), cols)]
    last = w[:, w.shape[1] - extra:]
    w_s[pl.ds(own_at, half), cols:] = jnp.concatenate([last, jnp.zeros_like(last)], axis=1)
    w_s[pl.ds(peer_at, half), :] = peer[...]
    total = dense(tail[...], w_s[n * cols:, :])
    for i in range(n):
        total = total + dense(every[i], w_s[i * cols:(i + 1) * cols, :])
    out_ref[...] = total[:, :cols].astype(BF)
    out_tail_ref[...] = total[:, cols:cols + extra].astype(BF)


def teacher_ffn_kernel(
    tile, slab, info, x, out_bias, gain, shift, up_bias, every, tail, p_give, p_keep,
    up_own, up_peer, down_own, down_peer,
    mid_ref, give_ref, keep_ref, up_s, down_s, act_s, normed_s, part_s, sems,
):
    half, hidden = up_own.shape
    own_at = pl.multiple_of(info[DP] * half, 16)
    peer_at = pl.multiple_of((1 - info[DP]) * half, 16)
    copies = [
        pltpu.make_async_copy(up_own, up_s.at[pl.ds(own_at, half)], sems.at[0]),
        pltpu.make_async_copy(up_peer, up_s.at[pl.ds(peer_at, half)], sems.at[1]),
        pltpu.make_async_copy(down_own, down_s.at[0], sems.at[2]),
        pltpu.make_async_copy(down_peer, down_s.at[1], sems.at[3]),
    ]
    for copy in copies:
        copy.start()
    n, unused, cols = every.shape
    bias = row(out_bias)
    for i in range(n):
        a = i * cols
        mid_ref[:, a:a + cols] = (
            x[:, a:a + cols].astype(F32) + every[i].astype(F32) + bias[:, a:a + cols]
        )
    a = n * cols
    mid_ref[:, a:] = x[:, a:].astype(F32) + tail[...].astype(F32) + bias[:, a:]
    xhat, unused = norm_parts(mid_ref[...])
    normed_s[...] = (xhat * row(gain) + row(shift)).astype(BF)
    rows = give_ref.shape[0]
    packed = give_ref.shape[1]
    give_ref[:, 2 * slab:] = p_give[...]
    keep_ref[:, 2 * slab:] = p_keep[...]
    for copy in copies[:2]:
        copy.wait()
    up_row = row(up_bias)
    at = 0
    while at < hidden:
        size = min(tile, hidden - at)
        v = dense(normed_s[...], up_s[:, at:at + size]) + up_row[:, at:at + size]
        act_s[:, at:at + size] = gelu_tanh(v).astype(BF)
        at += size
    for copy in copies[2:]:
        copy.wait()
    width = down_own.shape[0]
    for i in range(2):
        part_s[:, :width] = dense_nt(act_s[...], down_s[i])
        a = i * slab
        give_ref[:, a:a + width] = part_s[pl.ds((1 - info[ODD]) * rows, rows), :width].astype(BF)
        keep_ref[:, a:a + width] = part_s[pl.ds(info[ODD] * rows, rows), :width]
        give_ref[:, a + width:a + slab] = jnp.zeros((rows, slab - width), BF)
        keep_ref[:, a + width:a + slab] = jnp.zeros((rows, slab - width), F32)


def last_kernel(slab, info, t_mid, s_mid, t_bias, s_bias, r_ref, other_ref, t_out, s_out):
    rows = r_ref.shape[0]
    width = t_out.shape[1] // 2
    keep_at = pl.multiple_of(info[ODD] * rows, rows)
    give_at = pl.multiple_of((1 - info[ODD]) * rows, rows)
    first = info[DP] == 0
    for at, ref in ((keep_at, r_ref), (give_at, other_ref)):
        own, peer = ref[:, :width].astype(F32), ref[:, slab:slab + width].astype(F32)
        branch = jnp.concatenate(
            [jnp.where(first, own, peer), jnp.where(first, peer, own)], axis=1
        )
        t_out[pl.ds(at, rows), :] = (
            t_mid[pl.ds(at, rows), :] + branch + row(t_bias)
        ).astype(BF)
        s_out[pl.ds(at, rows), :] = (
            s_mid[pl.ds(at, rows), :]
            + ordered(info, ref[:, 2 * slab:].astype(F32))
            + row(s_bias)
        ).astype(BF)


def make_body(n_dp, n_ctx, n_tp):
    near = n_ctx <= 4

    def swap(x, axis, size, bit):
        return lax.ppermute(x, axis, [(i, i ^ bit) for i in range(size)])

    def tp_sum(give, keep):
        part = (keep + swap(give, "tp", n_tp, 1).astype(F32)).astype(BF)
        part = (part.astype(F32) + swap(part, "tp", n_tp, 2).astype(F32)).astype(BF)
        return part, swap(part, "tp", n_tp, 1)

    def gather_keys(kv):
        if not near:
            return [lax.all_gather(kv, "ctx", axis=1, tiled=True)]
        out = [kv]
        for k in range(1, n_ctx):
            out.append(lax.ppermute(kv, "ctx", [(i, i + k) for i in range(n_ctx - k)]))
        return out

    def small_sum(v):
        v = v + swap(v, "dp", n_dp, 1)
        bit = 1
        while bit < n_ctx:
            v = v + swap(v, "ctx", n_ctx, bit)
            bit *= 2
        return v

    def halving(give, keep, dp, ctx):
        keep = keep + swap(give, "ctx", n_ctx, 1).astype(F32)

        def split(x, index):
            half = x.shape[0] // 2
            return (
                lax.dynamic_slice_in_dim(x, (1 - index) * half, half).astype(BF),
                lax.dynamic_slice_in_dim(x, index * half, half),
            )

        give, keep = split(keep, dp)
        keep = keep + swap(give, "dp", n_dp, 1).astype(F32)
        if n_ctx == 4:
            give, keep = split(keep, ctx // 2)
            return keep + swap(give, "ctx", n_ctx, 2).astype(F32)
        groups = [[i for i in range(n_ctx) if i % 2 == b] for b in range(2)]
        return lax.psum_scatter(
            keep.astype(BF), "ctx", scatter_dimension=0, axis_index_groups=groups, tiled=True
        ).astype(F32)

    def body(
        teacher_in,
        teacher_gain_a,
        teacher_shift_a,
        teacher_attn_in,
        teacher_attn_bias,
        teacher_attn_out,
        teacher_out_bias,
        teacher_gain_b,
        teacher_shift_b,
        teacher_up,
        teacher_up_bias,
        teacher_down,
        teacher_down_bias,
        student_in,
        student_gain_a,
        student_shift_a,
        student_attn_in,
        student_attn_bias,
        student_attn_out,
        student_out_bias,
        student_gain_b,
        student_shift_b,
        student_up,
        student_up_bias,
        student_down,
        student_down_bias,
        out_grad,
        slot_lengths,
    ):
        slots, rows, wide = teacher_in.shape
        narrow = student_in.shape[2]
        total = slots * rows
        s_cols = student_attn_in.shape[2]
        s_heads = s_cols // HD
        hidden = student_up.shape[1]
        dp = lax.axis_index("dp")
        ctx = lax.axis_index("ctx")
        tp = lax.axis_index("tp")
        local_lengths = lax.dynamic_slice_in_dim(slot_lengths, dp * slots, slots)
        info = jnp.concatenate(
            [
                jnp.stack([ctx * rows, dp, tp % 2, tp, ctx]).astype(jnp.int32),
                local_lengths,
            ]
        )
        t_x = teacher_in.reshape(total, wide)
        s_x = student_in.reshape(total, narrow)
        grad = out_grad.reshape(total, narrow)

        s_in_t = jnp.swapaxes(student_attn_in, 1, 2)
        t_down_t = teacher_down.T
        peer_qkv = swap(s_in_t, "dp", n_dp, 1)
        t_half = wide // 2
        t_mine, t_theirs = run(
            teacher_norm_kernel,
            "teacher_norm",
            [((total, t_half), BF)] * 2,
            [info, t_x, teacher_gain_a, teacher_shift_a],
        )
        t_other = swap(t_theirs, "dp", n_dp, 1)
        s_x, t_theirs = lax.optimization_barrier((s_x, t_theirs))
        peer_out = swap(student_attn_out, "dp", n_dp, 1)
        peer_up = swap(student_up, "dp", n_dp, 1)
        peer_down = swap(student_down, "dp", n_dp, 1)

        unused_pairs, unused_single, s_kv_width = kv_tiles(s_heads)
        s_q_width = -(-s_cols // PAIR) * PAIR
        s_normed, s_q, s_kv = run(
            functools.partial(student_qkv_kernel, s_heads),
            "student_qkv",
            [((total, narrow), BF), ((total, s_q_width), BF), ((total, s_kv_width), BF)],
            [info, s_x, student_gain_a, student_shift_a, s_in_t, peer_qkv, student_attn_bias],
            flops=2 * total * narrow * 3 * s_cols,
        )
        s_q = s_q.reshape(slots, rows, s_q_width)
        s_kv_list = gather_keys(s_kv.reshape(slots, rows, s_kv_width))

        heads = wide // HD
        cols = heads // n_tp * HD
        tail = wide - n_tp * cols
        t_heads = (cols + tail) // HD
        unused_pairs, unused_single, t_kv_width = kv_tiles(t_heads)
        t_q_width = -(-(cols + tail) // PAIR) * PAIR
        packed = t_kv_width + t_q_width
        t_give, t_own, w_out_give = run(
            functools.partial(teacher_qkv_kernel, t_heads, cols),
            "teacher_qkv",
            [((total, packed), BF), ((total, packed), F32), ((t_half, t_q_width), BF)],
            [info, t_mine, t_other, teacher_attn_in, teacher_attn_out],
            specs=[SMEM, VMEM, VMEM, ANY, VMEM],
            scratch=[
                pltpu.VMEM((3, t_half, cols), BF),
                pltpu.VMEM((3, t_half, tail), BF),
                pltpu.SemaphoreType.DMA((2,)),
            ],
            flops=4 * total * wide * (cols + tail) * 3 // 2,
        )
        t_got = swap(t_give, "dp", n_dp, 1)
        t_kv, t_q = run(
            functools.partial(teacher_join_kernel, t_heads, cols),
            "teacher_join",
            [((total, t_kv_width), BF), ((total, t_q_width), BF)],
            [info, t_own, t_got, teacher_attn_bias],
        )
        t_kv_all = lax.all_gather(
            t_kv.reshape(slots, rows, t_kv_width), "ctx", axis=1, tiled=True
        )
        t_q = t_q.reshape(slots, rows, t_q_width)

        w_out_peer = swap(w_out_give, "dp", n_dp, 1)
        pairs_of_ctx = [[i, i + 1] for i in range(0, n_ctx, 2)]

        def fetch(w):
            quarter = w.shape[0] // 2
            part = lax.dynamic_slice_in_dim(w, (ctx % 2) * quarter, quarter)
            part = lax.all_gather(part, "dp", axis=0, tiled=True)
            part = lax.dynamic_slice_in_dim(part, (1 - dp) * quarter, quarter)
            return lax.all_gather(
                part, "ctx", axis=0, axis_index_groups=pairs_of_ctx, tiled=True
            )

        up_src, down_src, t_kv = lax.optimization_barrier((teacher_up, t_down_t, t_kv))
        up_peer = fetch(up_src)
        down_peer = fetch(down_src)

        blocks = len(s_kv_list)
        keys = blocks * s_kv_list[0].shape[1]
        block_scratch = [pltpu.VMEM((keys, s_kv_width), BF)] if blocks > 1 else []
        s_att, b_give, b_keep = run(
            functools.partial(student_attend_kernel, s_heads, blocks),
            "student_attend",
            [((slots, rows, s_cols), BF), ((rows, narrow), BF), ((rows, narrow), F32)],
            [info, s_q, student_attn_out, peer_out] + s_kv_list,
            scratch=block_scratch,
            flops=4 * total * s_cols * keys,
            extra=total * s_heads * keys,
        )
        r, other = tp_sum(b_give, b_keep)

        s_mid, b_normed, act, d_upper, give, keep = run(
            student_ffn_kernel,
            "student_ffn",
            [
                ((total, narrow), F32),
                ((total, narrow), BF),
                ((total, hidden), BF),
                ((total, hidden), BF),
                ((rows, narrow), BF),
                ((rows, narrow), F32),
            ],
            [
                info,
                s_x,
                student_out_bias,
                student_gain_b,
                student_shift_b,
                student_up_bias,
                r,
                other,
                student_up,
                peer_up,
                student_down,
                peer_down,
                grad,
            ],
            scratch=[pltpu.VMEM((total, narrow), F32)],
            flops=6 * total * narrow * hidden,
        )
        r2, other2 = tp_sum(give, keep)
        d_scratch = [
            pltpu.VMEM((total, s_q_width), BF),
            pltpu.VMEM((total, narrow), F32),
        ] + block_scratch
        d_outs = run(
            functools.partial(student_back_kernel, s_heads, blocks),
            "student_back",
            [
                ((total, narrow), F32),
                ((total, narrow), BF),
                ((slots, rows, s_cols), BF),
                ((3, narrow), F32),
            ]
            + [
                (item.shape, F32 if (blocks > 1 and i == 0) else BF)
                for i, item in enumerate(s_kv_list)
            ],
            [info, s_mid, student_gain_b, r2, other2, grad, student_attn_out, peer_out, s_q] + s_kv_list,
            scratch=d_scratch,
            flops=10 * total * s_cols * keys,
            extra=total * s_heads * keys,
        )
        d_mid, d_a, d_q, sums_b = d_outs[:4]
        d_parts = d_outs[4:]
        if near:
            d_own = d_parts[0]
            gots = [
                lax.ppermute(d_parts[k], "ctx", [(i + k, i) for i in range(n_ctx - k)])
                for k in range(1, n_ctx)
            ]
        else:
            d_own = lax.psum_scatter(d_parts[0], "ctx", scatter_dimension=1, tiled=True)
            gots = []
        b_normed, act, d_upper, d_q = lax.optimization_barrier((b_normed, act, d_upper, d_q))
        g_give, g_keep, p_give, p_keep, sums_f = run(
            functools.partial(student_ffn_grads_kernel, n_ctx),
            "student_ffn_grads",
            [
                ((narrow // 2, 2 * hidden), BF),
                ((narrow // 2, 2 * hidden), F32),
                ((rows, narrow), BF),
                ((rows, narrow), F32),
                ((2, narrow), F32),
            ],
            [info, b_normed, act, d_upper, grad, student_down, peer_down],
            scratch=[pltpu.VMEM((narrow, 2 * hidden), F32), pltpu.VMEM((total, narrow), F32)],
            flops=6 * total * narrow * hidden,
        )
        g_ffn = halving(g_give, g_keep, dp, ctx)
        d_own = d_own.reshape(total, s_kv_width)
        gots = [g.reshape(total, s_kv_width) for g in gots]
        a_give, a_keep, ga_give, ga_keep, sums_q = run(
            functools.partial(student_in_kernel, s_heads, len(gots), n_ctx),
            "student_in",
            [
                ((rows, narrow), BF),
                ((rows, narrow), F32),
                ((narrow // n_dp, 4 * s_cols), BF),
                ((narrow // n_dp, 4 * s_cols), F32),
                ((2, s_cols), F32),
            ],
            [
                info,
                d_q.reshape(total, s_cols),
                s_normed,
                d_a,
                s_att.reshape(total, s_cols),
                s_in_t,
                peer_qkv,
                d_own,
            ]
            + gots,
            scratch=[pltpu.VMEM((total, narrow), F32), pltpu.VMEM((narrow, 4 * s_cols), F32)],
            flops=2 * total * narrow * 7 * s_cols,
        )
        r3, other3 = tp_sum(a_give, a_keep)
        g_att = halving(ga_give, ga_keep, dp, ctx)
        in_grad, sums = run(
            student_last_kernel,
            "student_last",
            [((total, narrow), F32), ((8, narrow), F32)],
            [info, s_x, student_gain_a, r3, other3, d_mid, sums_b, sums_f, sums_q],
            scratch=[pltpu.VMEM((total, narrow), F32)],
        )

        t_att, t_att_tail = run(
            functools.partial(teacher_attend_kernel, t_heads, 1),
            "teacher_attend",
            [((slots, rows, cols), BF), ((slots, rows, tail), BF)],
            [info, t_q, t_kv_all],
            flops=4 * total * (cols + tail) * keys,
            extra=total * t_heads * keys,
        )
        every = lax.all_gather(t_att.reshape(total, cols), "tp", axis=0)
        o_cols, o_tail = run(
            teacher_out_kernel,
            "teacher_out",
            [((total, cols), BF), ((total, tail), BF)],
            [info, every, t_att_tail.reshape(total, tail), teacher_attn_out, w_out_peer],
            scratch=[pltpu.VMEM((wide, t_q_width), BF)],
            flops=2 * total * wide * (cols + tail),
        )
        o_every = lax.all_gather(o_cols, "tp", axis=0)
        t_hidden = teacher_up.shape[1]
        slab = -(-t_half // 128) * 128
        t_mid, f_give, f_keep = run(
            functools.partial(teacher_ffn_kernel, 256, slab),
            "teacher_ffn",
            [
                ((total, wide), F32),
                ((rows, 2 * slab + narrow), BF),
                ((rows, 2 * slab + narrow), F32),
            ],
            [
                info,
                t_x,
                teacher_out_bias,
                teacher_gain_b,
                teacher_shift_b,
                teacher_up_bias,
                o_every,
                o_tail,
                p_give,
                p_keep,
                teacher_up,
                up_peer,
                t_down_t,
                down_peer,
            ],
            specs=[SMEM] + [VMEM] * 9 + [ANY] * 4,
            scratch=[
                pltpu.VMEM((wide, t_hidden), BF),
                pltpu.VMEM((2, t_half, t_hidden), BF),
                pltpu.VMEM((total, t_hidden), BF),
                pltpu.VMEM((total, wide), BF),
                pltpu.VMEM((total, slab), F32),
                pltpu.SemaphoreType.DMA((4,)),
            ],
            flops=4 * total * wide * t_hidden,
        )
        r4, other4 = tp_sum(f_give, f_keep)
        t_result, s_result = run(
            functools.partial(last_kernel, slab),
            "last",
            [((total, wide), BF), ((total, narrow), BF)],
            [info, t_mid, s_mid, teacher_down_bias, student_down_bias, r4, other4],
        )

        small = small_sum(sums)
        piece = narrow // (n_dp * n_ctx)
        shards = lax.dynamic_slice_in_dim(small, (dp * n_ctx + ctx) * piece, piece, axis=1)

        grad_attn_in = jnp.stack([g_att[:, i * s_cols:(i + 1) * s_cols] for i in range(3)])
        return (
            t_result.reshape(slots, rows, wide),
            s_result.reshape(slots, rows, narrow),
            in_grad.reshape(slots, rows, narrow),
            shards[0],
            shards[1],
            grad_attn_in,
            small[7, :2 * s_cols].reshape(2, s_cols),
            g_att[:, 3 * s_cols:].T,
            shards[4],
            shards[2],
            shards[3],
            g_ffn[:, hidden:],
            small[6],
            g_ffn[:, :hidden].T,
            shards[5],
        )

    return body


def solution(mesh):
    sizes = mesh.shape
    return jax.shard_map(
        make_body(sizes["dp"], sizes["ctx"], sizes["tp"]),
        mesh=mesh,
        in_specs=(
            P("dp", "ctx", None),
            P(),
            P(),
            P(None, "dp", None),
            P(),
            P("dp", None),
            P(),
            P(),
            P(),
            P("dp", "tp"),
            P("tp"),
            P("tp", "dp"),
            P(),
            P("dp", "ctx", None),
            P(),
            P(),
            P(None, "dp", "tp"),
            P(None, "tp"),
            P("tp", "dp"),
            P(),
            P(),
            P(),
            P("dp", "tp"),
            P("tp"),
            P("tp", "dp"),
            P(),
            P("dp", "ctx", None),
            P(),
        ),
        out_specs=(
            P("dp", "ctx", None),
            P("dp", "ctx", None),
            P("dp", "ctx", None),
            P(("dp", "ctx")),
            P(("dp", "ctx")),
            P(None, ("dp", "ctx"), "tp"),
            P(None, "tp"),
            P("tp", ("dp", "ctx")),
            P(("dp", "ctx")),
            P(("dp", "ctx")),
            P(("dp", "ctx")),
            P(("dp", "ctx"), "tp"),
            P("tp"),
            P("tp", ("dp", "ctx")),
            P(("dp", "ctx")),
        ),
        check_vma=False,
    )
```

```python
import functools
import math

import jax
import jax.numpy as jnp
from jax import lax
from jax.experimental import pallas as pl
from jax.experimental.pallas import tpu as pltpu
from jax.sharding import PartitionSpec as P

HD = 64
PAIR = 2 * HD
EPS = 1e-05
MASKED = -1000000000.0
FAR = 1 << 30
BF = jnp.bfloat16
F32 = jnp.float32
GELU_C = math.sqrt(2.0 / math.pi)
SMEM = pl.BlockSpec(memory_space=pltpu.SMEM)
VMEM = pl.BlockSpec(memory_space=pltpu.VMEM)
ANY = pl.BlockSpec(memory_space=pl.ANY)
RING = 4
LIMIT = 60 * 1024 * 1024


def dense(left, right):
    return jnp.dot(left, right, preferred_element_type=F32)


def dense_tn(left, right):
    return lax.dot_general(left, right, (((0,), (0,)), ((), ())), preferred_element_type=F32)


def dense_nt(left, right):
    return lax.dot_general(left, right, (((1,), (1,)), ((), ())), preferred_element_type=F32)


def norm_parts(x):
    centered = x - jnp.mean(x, axis=-1, keepdims=True)
    spread = jnp.mean(centered * centered, axis=-1, keepdims=True)
    factor = lax.rsqrt(spread + EPS)
    return centered * factor, factor


def norm_back(d_out, xhat, factor, gain):
    e = d_out * gain
    return factor * (
        e - jnp.mean(e, axis=-1, keepdims=True) - xhat * jnp.mean(e * xhat, axis=-1, keepdims=True)
    )


def gelu_tanh(v):
    return 0.5 * v * (1.0 + jnp.tanh(GELU_C * (v + 0.044715 * v * v * v)))


def gelu_both(v):
    inner = jnp.tanh(GELU_C * (v + 0.044715 * v * v * v))
    slope = 0.5 * (1.0 + inner) + 0.5 * v * (1.0 - inner * inner) * GELU_C * (
        1.0 + 3.0 * 0.044715 * v * v
    )
    return 0.5 * v * (1.0 + inner), slope


BASE, DP, ODD, TP, CTX, LEN = 0, 1, 2, 3, 4, 5


def row(ref):
    return ref[...].astype(F32).reshape(1, -1)


def halves(info, x):
    mid = x.shape[-1] // 2
    first = info[DP] == 0
    left, right = x[:, :mid], x[:, mid:]
    return jnp.where(first, left, right), jnp.where(first, right, left)


def ordered(info, own_peer):
    mid = own_peer.shape[-1] // 2
    first = info[DP] == 0
    own, peer = own_peer[:, :mid], own_peer[:, mid:]
    return jnp.concatenate(
        [jnp.where(first, own, peer), jnp.where(first, peer, own)], axis=-1
    )


def run(kernel, name, outs, args, specs=None, scratch=(), flops=0, extra=0):
    out_shape = [jax.ShapeDtypeStruct(shape, kind) for shape, kind in outs]
    if specs is None:
        specs = [SMEM] + [VMEM] * (len(args) - 1)
    moved = sum(a.size * a.dtype.itemsize for a in args)
    moved += sum(math.prod(o.shape) * o.dtype.itemsize for o in out_shape)
    return pl.pallas_call(
        kernel,
        out_shape=out_shape,
        in_specs=specs,
        out_specs=[VMEM] * len(outs),
        scratch_shapes=list(scratch),
        compiler_params=pltpu.CompilerParams(vmem_limit_bytes=LIMIT),
        cost_estimate=pl.CostEstimate(
            flops=1, bytes_accessed=1, transcendentals=0
        ),
        name=name,
    )(*args)


def kv_tiles(heads):
    pairs = heads // 2
    return pairs, heads % 2, pairs * 2 * PAIR + (heads % 2) * PAIR


def put_kv(ref, k, v, heads):
    pairs, single, unused = kv_tiles(heads)
    for g in range(pairs):
        ref[:, 2 * g * PAIR:(2 * g + 1) * PAIR] = k[:, g * PAIR:(g + 1) * PAIR].astype(ref.dtype)
        ref[:, (2 * g + 1) * PAIR:(2 * g + 2) * PAIR] = v[:, g * PAIR:(g + 1) * PAIR].astype(
            ref.dtype
        )
    if single:
        tail = jnp.concatenate([k[:, pairs * PAIR:], v[:, pairs * PAIR:]], axis=1)
        ref[:, 2 * pairs * PAIR:] = tail.astype(ref.dtype)


def put_q(ref, q, heads):
    pairs, single, unused = kv_tiles(heads)
    q = q * (HD ** -0.5)
    ref[:, :pairs * PAIR] = q[:, :pairs * PAIR].astype(ref.dtype)
    if single:
        tail = q[:, pairs * PAIR:]
        ref[:, pairs * PAIR:] = jnp.concatenate([tail, jnp.zeros_like(tail)], axis=1).astype(
            ref.dtype
        )


def chunks_of(keys):
    width = math.gcd(keys, 512)
    return [(i * width, width) for i in range(keys // width)]


def key_rows(info, rows, blocks, chunks):
    out = []
    for start, width in chunks:
        place = start + lax.broadcasted_iota(jnp.int32, (1, width), 1)
        if blocks > 1:
            place = info[BASE] + place - 2 * rows * (place // rows)
            place = jnp.where(place < 0, FAR, place)
        out.append(place)
    return out


def soft(query, keys, places, bound):
    scores = [
        jnp.where(place <= bound, dense_nt(query, k), MASKED) for place, k in zip(places, keys)
    ]
    top = functools.reduce(jnp.maximum, [jnp.max(s, axis=-1, keepdims=True) for s in scores])
    raised = [jnp.exp(s - top) for s in scores]
    total = functools.reduce(jnp.add, [jnp.sum(r, axis=-1, keepdims=True) for r in raised])
    return raised, 1.0 / total


def add_all(items):
    return functools.reduce(jnp.add, items)


def query_bound(info, slot, rows):
    place = info[BASE] + lax.broadcasted_iota(jnp.int32, (rows, 1), 0)
    return jnp.minimum(place, info[LEN + slot] - 1)


def attend_slot(query_of, kv_of, heads, rows, places, bound):
    pairs, single, unused = kv_tiles(heads)
    lane = lax.broadcasted_iota(jnp.int32, (rows, PAIR), 1)
    low = lane < HD
    out = []
    for g in range(pairs):
        query = query_of(g)
        keys, values = kv_of(2 * g), kv_of(2 * g + 1)
        held = []
        for part in (low, jnp.logical_not(low)):
            one = jnp.where(part, query, jnp.zeros_like(query))
            raised, inverse = soft(one, keys, places, bound)
            held.append(add_all([dense(r.astype(BF), v) for r, v in zip(raised, values)]) * inverse)
        out.append(jnp.where(low, held[0], held[1]))
    if single:
        keys = kv_of(2 * pairs)
        raised, inverse = soft(query_of(pairs), keys, places, bound)
        held = add_all([dense(r.astype(BF), v) for r, v in zip(raised, keys)]) * inverse
        out.append(held[:, HD:])
    return out


def load_blocks(kv_s, kv_refs, slot, rows):
    if kv_s is not None:
        for i, ref in enumerate(kv_refs):
            kv_s[i * rows:(i + 1) * rows, :] = ref[slot]


def kv_reader(kv_s, kv_refs, slot, chunks):
    def kv_of(tile):
        if kv_s is not None:
            return [kv_s[a:a + w, tile * PAIR:(tile + 1) * PAIR] for a, w in chunks]
        return [kv_refs[0][slot, a:a + w, tile * PAIR:(tile + 1) * PAIR] for a, w in chunks]
    return kv_of


def student_attend_kernel(heads, blocks, info, q_ref, own_ref, peer_ref, *refs):
    kv_refs = refs[:blocks]
    att_ref, give_ref, keep_ref = refs[blocks:blocks + 3]
    kv_s = refs[blocks + 3] if blocks > 1 else None
    slots, rows, unused = q_ref.shape
    keys = blocks * kv_refs[0].shape[1]
    chunks = chunks_of(keys)
    half = own_ref.shape[1]

    def one_slot(i, carry):
        slot = jnp.where(i == 0, 1 - info[ODD], info[ODD])
        load_blocks(kv_s, kv_refs, slot, rows)
        out = attend_slot(
            lambda g: q_ref[slot, :, g * PAIR:(g + 1) * PAIR],
            kv_reader(kv_s, kv_refs, slot, chunks),
            heads,
            rows,
            key_rows(info, rows, blocks, chunks),
            query_bound(info, slot, rows),
        )
        att = jnp.concatenate(out, axis=1).astype(BF)
        att_ref[slot] = att
        part = jnp.concatenate([dense(att, own_ref[...]), dense(att, peer_ref[...])], axis=1)

        @pl.when(i == 0)
        def _():
            give_ref[...] = part.astype(BF)

        @pl.when(i == 1)
        def _():
            keep_ref[...] = part

        return carry

    lax.fori_loop(0, slots, one_slot, 0)


def teacher_attend_kernel(heads, blocks, info, q_ref, *refs):
    kv_refs = refs[:blocks]
    att_ref, tail_ref = refs[blocks:blocks + 2]
    kv_s = refs[blocks + 2] if blocks > 1 else None
    slots, rows, unused = q_ref.shape
    chunks = chunks_of(blocks * kv_refs[0].shape[1])
    pairs = heads // 2

    def one_slot(slot, carry):
        load_blocks(kv_s, kv_refs, slot, rows)
        out = attend_slot(
            lambda g: q_ref[slot, :, g * PAIR:(g + 1) * PAIR],
            kv_reader(kv_s, kv_refs, slot, chunks),
            heads,
            rows,
            key_rows(info, rows, blocks, chunks),
            query_bound(info, slot, rows),
        )
        for g in range(pairs):
            att_ref[slot, :, g * PAIR:(g + 1) * PAIR] = out[g].astype(BF)
        tail_ref[slot] = out[pairs].astype(BF)
        return carry

    lax.fori_loop(0, slots, one_slot, 0)


def keep_mask(info, slots, rows):
    row = lax.broadcasted_iota(jnp.int32, (rows, 1), 0) + info[BASE]
    return jnp.concatenate([row < info[LEN + s] for s in range(slots)], axis=0)


def student_back_kernel(
    heads, blocks, info, mid_ref, gain, r_ref, other_ref, grad_ref, own_ref, peer_ref, q_ref, *refs
):
    kv_refs = refs[:blocks]
    d_mid_ref, d_a_ref, d_q_ref, sums_ref = refs[blocks:blocks + 4]
    d_refs = refs[blocks + 4:2 * blocks + 4]
    d_att_s = refs[2 * blocks + 4]
    d_s = refs[2 * blocks + 5]
    kv_s = refs[2 * blocks + 6] if blocks > 1 else None
    slots, rows, unused = q_ref.shape
    chunks = chunks_of(blocks * kv_refs[0].shape[1])
    pairs, single, unused = kv_tiles(heads)
    scale = HD ** -0.5

    d_s[pl.ds(info[ODD] * rows, rows), :] = ordered(info, r_ref[...]).astype(F32)
    d_s[pl.ds((1 - info[ODD]) * rows, rows), :] = ordered(info, other_ref[...]).astype(F32)
    xhat, factor = norm_parts(mid_ref[...])
    d_norm = d_s[...]
    cot = jnp.where(keep_mask(info, slots, rows), grad_ref[...].astype(F32), 0.0)
    d_mid = cot + norm_back(d_norm, xhat, factor, row(gain))
    d_a = d_mid.astype(BF)
    d_mid_ref[...] = d_mid
    d_a_ref[...] = d_a
    sums_ref[0:1, :] = jnp.sum(d_norm * xhat, axis=0, keepdims=True)
    sums_ref[1:2, :] = jnp.sum(d_norm, axis=0, keepdims=True)
    sums_ref[2:3, :] = jnp.sum(d_a.astype(F32), axis=0, keepdims=True)
    mine, theirs = halves(info, d_a)
    d_att = dense_nt(mine, own_ref[...]) + dense_nt(theirs, peer_ref[...])
    width = heads * HD
    d_att_s[:, :pairs * PAIR] = d_att[:, :pairs * PAIR].astype(BF)
    if single:
        tail = d_att[:, pairs * PAIR:width]
        d_att_s[:, pairs * PAIR:] = jnp.concatenate([jnp.zeros_like(tail), tail], axis=1).astype(BF)

    def put(slot, tile, i, value):
        start, size = chunks[i]
        if blocks == 1:
            d_refs[0][slot, start:start + size, tile * PAIR:(tile + 1) * PAIR] = value.astype(
                d_refs[0].dtype
            )
        else:
            for b in range(blocks):
                d_refs[b][slot, :, tile * PAIR:(tile + 1) * PAIR] = value[
                    b * rows:(b + 1) * rows
                ].astype(d_refs[b].dtype)

    def one_slot(slot, carry):
        load_blocks(kv_s, kv_refs, slot, rows)
        kv_of = kv_reader(kv_s, kv_refs, slot, chunks)
        places = key_rows(info, rows, blocks, chunks)
        bound = query_bound(info, slot, rows)
        low = lax.broadcasted_iota(jnp.int32, (rows, PAIR), 1) < HD
        row0 = pl.multiple_of(slot * rows, rows)

        def head(query, d_out, keys, values):
            raised, inverse = soft(query, keys, places, bound)
            probs = [r * inverse for r in raised]
            d_probs = [dense_nt(d_out, v) for v in values]
            delta = add_all(
                [jnp.sum(p * d, axis=-1, keepdims=True) for p, d in zip(probs, d_probs)]
            )
            d_scores = [(p * (d - delta)).astype(BF) for p, d in zip(probs, d_probs)]
            d_query = add_all([dense(s, k) for s, k in zip(d_scores, keys)]) * scale
            d_keys = [dense_tn(s, query) for s in d_scores]
            d_values = [dense_tn(p.astype(BF), d_out) for p in probs]
            return d_query, d_keys, d_values

        for g in range(pairs):
            query = q_ref[slot, :, g * PAIR:(g + 1) * PAIR]
            d_out = d_att_s[pl.ds(row0, rows), g * PAIR:(g + 1) * PAIR]
            keys, values = kv_of(2 * g), kv_of(2 * g + 1)
            zero = jnp.zeros_like(query)
            a = head(jnp.where(low, query, zero), jnp.where(low, d_out, zero), keys, values)
            b = head(jnp.where(low, zero, query), jnp.where(low, zero, d_out), keys, values)
            d_q_ref[slot, :, g * PAIR:(g + 1) * PAIR] = jnp.where(low, a[0], b[0]).astype(BF)
            for i in range(len(chunks)):
                put(slot, 2 * g, i, a[1][i] + b[1][i])
                put(slot, 2 * g + 1, i, a[2][i] + b[2][i])
        if single:
            query = q_ref[slot, :, pairs * PAIR:]
            d_out = d_att_s[pl.ds(row0, rows), pairs * PAIR:]
            keys = kv_of(2 * pairs)
            a = head(query, d_out, keys, keys)
            d_q_ref[slot, :, pairs * PAIR:] = a[0][:, :HD].astype(BF)
            for i in range(len(chunks)):
                put(slot, 2 * pairs, i, a[1][i] + a[2][i])
        return carry

    lax.fori_loop(0, slots, one_slot, 0)


def student_qkv_kernel(heads, info, x, gain, shift, own, peer, bias, normed_ref, q_ref, kv_ref):
    xhat, unused = norm_parts(x[...].astype(F32))
    normed = (xhat * row(gain) + row(shift)).astype(BF)
    normed_ref[...] = normed
    mine, theirs = halves(info, normed)

    def project(i):
        return dense_nt(mine, own[i]) + dense_nt(theirs, peer[i])

    put_kv(kv_ref, project(1), project(2) + bias[1:2, :].astype(F32), heads)
    put_q(q_ref, (project(0) + bias[0:1, :].astype(F32)).astype(BF), heads)


def student_ffn_kernel(
    info, x, out_bias, gain, shift, up_bias, r_ref, other_ref, up_own, up_peer, down_own,
    down_peer, grad, mid_ref, normed_ref, act_ref, d_upper_ref, give_ref, keep_ref, part_s,
):
    rows = r_ref.shape[0]
    slots = x.shape[0] // rows
    keep_at = pl.multiple_of(info[ODD] * rows, rows)
    give_at = pl.multiple_of((1 - info[ODD]) * rows, rows)
    for at, ref in ((keep_at, r_ref), (give_at, other_ref)):
        mid_ref[pl.ds(at, rows), :] = (
            x[pl.ds(at, rows), :].astype(F32) + ordered(info, ref[...]).astype(F32) + row(out_bias)
        )
    xhat, unused = norm_parts(mid_ref[...])
    normed = (xhat * row(gain) + row(shift)).astype(BF)
    normed_ref[...] = normed
    mine, theirs = halves(info, normed)
    upper = dense(mine, up_own[...]) + dense(theirs, up_peer[...]) + row(up_bias)
    act, slope = gelu_both(upper)
    act_ref[...] = act.astype(BF)
    d_b = jnp.where(keep_mask(info, slots, rows), grad[...].astype(F32), 0.0).astype(BF)
    d_mine, d_theirs = halves(info, d_b)
    d_act = (dense_nt(d_mine, down_own[...]) + dense_nt(d_theirs, down_peer[...])).astype(BF)
    d_upper = (d_act.astype(F32) * slope).astype(BF)
    d_upper_ref[...] = d_upper
    half = up_own.shape[0]
    part_s[:, :half] = dense_nt(d_upper, up_own[...])
    part_s[:, half:] = dense_nt(d_upper, up_peer[...])
    give_ref[...] = part_s[pl.ds(give_at, rows), :].astype(BF)
    keep_ref[...] = part_s[pl.ds(keep_at, rows), :]


def split_rows(info, n_ctx, grad_s, give_ref, keep_ref):
    full = grad_s.shape[0]
    piece = full // (2 * n_ctx)
    count = n_ctx // RING
    if piece % 8:
        for half, ref in ((info[DP], keep_ref), (1 - info[DP], give_ref)):
            start = pl.multiple_of(half * (full // 2), 16)
            ref[...] = grad_s[pl.ds(start, full // 2), :].astype(ref.dtype)
        return
    place = lax.rem(info[CTX], RING)
    for i, flip in enumerate((0, 3, 1, 2)):
        for q in range(count):
            to = (i * count + q) * piece
            at = (q * RING + (place ^ flip)) * piece
            for half, ref in ((info[DP], keep_ref), (1 - info[DP], give_ref)):
                start = pl.multiple_of(half * (full // 2) + at, math.gcd(piece, 16))
                ref[to:to + piece, :] = grad_s[pl.ds(start, piece), :].astype(ref.dtype)


def student_ffn_grads_kernel(
    n_ctx, info, normed, act, d_upper, grad, give_ref, keep_ref, sums_ref, grad_s
):
    slots = info.shape[0] - LEN
    rows = normed.shape[0] // slots
    d_b = jnp.where(keep_mask(info, slots, rows), grad[...].astype(F32), 0.0).astype(BF)
    hidden = act.shape[1]
    grad_s[:, :hidden] = dense_tn(d_b, act[...])
    grad_s[:, hidden:] = dense_tn(normed[...], d_upper[...])
    split_rows(info, n_ctx, grad_s, give_ref, keep_ref)
    sums_ref[0:1, :] = jnp.sum(d_b.astype(F32), axis=0, keepdims=True)
    sums_ref[1:2, :] = jnp.sum(d_upper[...].astype(F32), axis=0, keepdims=True)


def student_in_kernel(
    heads, n_got, n_ctx, info, d_q, normed, d_a, att, own, peer, act, down_own, down_peer, d_kv,
    *refs
):
    gots = refs[:n_got]
    give_ref, keep_ref, g_give, g_keep, bias_ref, part_s, grad_s = refs[n_got:]
    rows = give_ref.shape[0]
    pairs, single, unused = kv_tiles(heads)
    total = d_kv[...].astype(F32)
    for got in gots:
        total = total + got[...].astype(F32)
    total = total.astype(BF)
    d_k = [total[:, 2 * g * PAIR:(2 * g + 1) * PAIR] for g in range(pairs)]
    d_v = [total[:, (2 * g + 1) * PAIR:(2 * g + 2) * PAIR] for g in range(pairs)]
    if single:
        d_k.append(total[:, 2 * pairs * PAIR:2 * pairs * PAIR + HD])
        d_v.append(total[:, 2 * pairs * PAIR + HD:])
    d_k = jnp.concatenate(d_k, axis=1)
    d_v = jnp.concatenate(d_v, axis=1)
    half = own.shape[2]

    def back(w):
        return dense(d_q[...], w[0]) + dense(d_k, w[1]) + dense(d_v, w[2])

    part_s[:, :half] = back(own)
    part_s[:, half:2 * half] = back(peer)
    part_s[:, 2 * half:3 * half] = dense(act[...], down_own[...])
    part_s[:, 3 * half:] = dense(act[...], down_peer[...])
    give_ref[...] = part_s[pl.ds((1 - info[ODD]) * rows, rows), :].astype(BF)
    keep_ref[...] = part_s[pl.ds(info[ODD] * rows, rows), :]
    cols = heads * HD
    n = normed[...]
    grad_s[:, :cols] = dense_tn(n, d_q[...])
    grad_s[:, cols:2 * cols] = dense_tn(n, d_k)
    grad_s[:, 2 * cols:3 * cols] = dense_tn(n, d_v)
    grad_s[:, 3 * cols:] = dense_tn(d_a[...], att[...])
    split_rows(info, n_ctx, grad_s, g_give, g_keep)
    bias_ref[0:1, :] = jnp.sum(d_q[...].astype(F32), axis=0, keepdims=True)
    bias_ref[1:2, :] = jnp.sum(d_v.astype(F32), axis=0, keepdims=True)


def student_last_kernel(
    info, x, gain, s_mid, s_bias, r_ref, other_ref, d_mid, sums_b, sums_f, sums_q,
    out_ref, s_out, sums_ref, d_s,
):
    rows = r_ref.shape[0]
    width = x.shape[1]
    for at, ref in ((info[ODD] * rows, r_ref), ((1 - info[ODD]) * rows, other_ref)):
        at = pl.multiple_of(at, rows)
        d_s[pl.ds(at, rows), :] = ordered(info, ref[:, :width]).astype(F32)
        s_out[pl.ds(at, rows), :] = (
            s_mid[pl.ds(at, rows), :] + ordered(info, ref[:, width:]).astype(F32) + row(s_bias)
        ).astype(BF)
    xhat, factor = norm_parts(x[...].astype(F32))
    d_norm = d_s[...]
    out_ref[...] = d_mid[...] + norm_back(d_norm, xhat, factor, row(gain))
    sums_ref[0:1, :] = jnp.sum(d_norm * xhat, axis=0, keepdims=True)
    sums_ref[1:2, :] = jnp.sum(d_norm, axis=0, keepdims=True)
    sums_ref[2:5, :] = sums_b[...]
    sums_ref[5:7, :] = sums_f[...]
    rest = out_ref.shape[1] - 2 * sums_q.shape[1]
    sums_ref[7:8, :] = jnp.concatenate(
        [sums_q[0:1, :], sums_q[1:2, :], jnp.zeros((1, rest), F32)], axis=1
    )


def teacher_norm_kernel(info, x, gain, shift, mine_ref, theirs_ref):
    xhat, unused = norm_parts(x[...].astype(F32))
    normed = (xhat * row(gain) + row(shift)).astype(BF)
    mine, theirs = halves(info, normed)
    mine_ref[...] = mine
    theirs_ref[...] = theirs


def teacher_qkv_kernel(
    heads, cols, info, mine, other, w_hbm, wo, give_ref, own_ref, wo_ref, w, w_tail, sems
):
    pairs, unused, kv_width = kv_tiles(heads)
    col0 = pl.multiple_of(info[TP] * cols, cols)
    wide = w_hbm.shape[2]
    tail = w_tail.shape[2]
    copies = [
        pltpu.make_async_copy(w_hbm.at[:, :, pl.ds(col0, cols)], w, sems.at[0]),
        pltpu.make_async_copy(w_hbm.at[:, :, pl.ds(wide - tail, tail)], w_tail, sems.at[1]),
    ]
    for copy in copies:
        copy.start()
    wo_ref[:, :cols] = wo[:, pl.ds(col0, cols)]
    last = wo[:, wide - tail:]
    wo_ref[:, cols:] = jnp.concatenate([last, jnp.zeros_like(last)], axis=1)
    for copy in copies:
        copy.wait()
    for source, target in ((other, give_ref), (mine, own_ref)):
        x = source[...]
        k, v, q = (dense(x, w[i]) for i in (1, 2, 0))
        tk, tv, tq = (dense(x, w_tail[i]) for i in (1, 2, 0))
        kind = target.dtype
        for g in range(pairs):
            a = 2 * g * PAIR
            target[:, a:a + PAIR] = k[:, g * PAIR:(g + 1) * PAIR].astype(kind)
            target[:, a + PAIR:a + 2 * PAIR] = v[:, g * PAIR:(g + 1) * PAIR].astype(kind)
        target[:, 2 * pairs * PAIR:kv_width] = jnp.concatenate([tk, tv], axis=1).astype(kind)
        target[:, kv_width:kv_width + cols] = q.astype(kind)
        target[:, kv_width + cols:] = jnp.concatenate([tq, jnp.zeros_like(tq)], axis=1).astype(kind)


def teacher_join_kernel(heads, cols, info, own, got, bias, kv_ref, q_ref):
    pairs, unused, kv_width = kv_tiles(heads)
    whole = own[...] + got[...].astype(F32)
    b = bias[:, pl.ds(pl.multiple_of(info[TP] * cols, cols), cols)].astype(F32)
    t = bias[:, bias.shape[1] - HD:].astype(F32)
    zero = jnp.zeros_like(t[0:1])
    for g in range(pairs):
        a = 2 * g * PAIR
        kv_ref[:, a:a + PAIR] = whole[:, a:a + PAIR].astype(BF)
        kv_ref[:, a + PAIR:a + 2 * PAIR] = (
            whole[:, a + PAIR:a + 2 * PAIR] + b[1:2, g * PAIR:(g + 1) * PAIR]
        ).astype(BF)
    a = 2 * pairs * PAIR
    kv_ref[:, a:] = (whole[:, a:kv_width] + jnp.concatenate([zero, t[1:2]], axis=1)).astype(BF)
    q = (whole[:, kv_width:] + jnp.concatenate([b[0:1], t[0:1], zero], axis=1)).astype(BF)
    q_ref[...] = (q * (HD ** -0.5)).astype(BF)


def teacher_out_kernel(info, every, tail, w, peer, out_ref, out_tail_ref, w_s):
    half = w.shape[0]
    n, unused, cols = every.shape
    extra = tail.shape[1]
    own_at = pl.multiple_of(info[DP] * half, 16)
    peer_at = pl.multiple_of((1 - info[DP]) * half, 16)
    w_s[pl.ds(own_at, half), :cols] = w[:, pl.ds(pl.multiple_of(info[TP] * cols, cols), cols)]
    last = w[:, w.shape[1] - extra:]
    w_s[pl.ds(own_at, half), cols:] = jnp.concatenate([last, jnp.zeros_like(last)], axis=1)
    w_s[pl.ds(peer_at, half), :] = peer[...]
    total = dense(tail[...], w_s[n * cols:, :])
    for i in range(n):
        total = total + dense(every[i], w_s[i * cols:(i + 1) * cols, :])
    out_ref[...] = total[:, :cols].astype(BF)
    out_tail_ref[...] = total[:, cols:cols + extra].astype(BF)


def teacher_ffn_kernel(
    tile, info, x, out_bias, gain, shift, up_bias, every, tail, up_own, down_own,
    up_near, up_far, down_near, down_far, mid_ref, give_ref, keep_ref, w_s, act_s, normed_s, part_s, sems,
):
    half, hidden = up_own.shape
    wide = 2 * half
    own_at = pl.multiple_of(info[DP] * half, 16)
    peer_at = (1 - info[DP]) * half
    copies = [
        pltpu.make_async_copy(up_own, w_s.at[pl.ds(own_at, half)], sems.at[0]),
        pltpu.make_async_copy(
            down_own, w_s.at[pl.ds(pl.multiple_of(own_at + wide, 16), half)], sems.at[1]
        ),
    ]
    size = up_near.shape[0]
    bit = lax.rem(info[CTX], 2)
    for i, (part, base, place) in enumerate(
        ((up_near, 0, bit), (up_far, 0, 1 - bit), (down_near, wide, bit), (down_far, wide, 1 - bit))
    ):
        at = pl.multiple_of(peer_at + base + place * size, 16)
        copies.append(pltpu.make_async_copy(part, w_s.at[pl.ds(at, size)], sems.at[i + 2]))
    for copy in copies:
        copy.start()
    n, unused, cols = every.shape
    bias = row(out_bias)
    for i in range(n):
        a = i * cols
        mid_ref[:, a:a + cols] = (
            x[:, a:a + cols].astype(F32) + every[i].astype(F32) + bias[:, a:a + cols]
        )
    a = n * cols
    mid_ref[:, a:] = x[:, a:].astype(F32) + tail[...].astype(F32) + bias[:, a:]
    xhat, unused = norm_parts(mid_ref[...])
    normed_s[...] = (xhat * row(gain) + row(shift)).astype(BF)
    rows, packed = give_ref.shape
    for copy in copies:
        copy.wait()
    up_row = row(up_bias)
    at = 0
    while at < hidden:
        size = min(tile, hidden - at)
        v = dense(normed_s[...], w_s[:wide, at:at + size]) + up_row[:, at:at + size]
        act_s[:, at:at + size] = gelu_tanh(v).astype(BF)
        at += size
    part_s[...] = dense_nt(act_s[...], w_s[wide:, :])
    give_ref[:, :wide] = part_s[pl.ds((1 - info[ODD]) * rows, rows), :].astype(BF)
    keep_ref[:, :wide] = part_s[pl.ds(info[ODD] * rows, rows), :]
    give_ref[:, wide:] = jnp.zeros((rows, packed - wide), BF)
    keep_ref[:, wide:] = jnp.zeros((rows, packed - wide), F32)


def last_kernel(info, t_mid, t_bias, r_ref, other_ref, t_out):
    rows = r_ref.shape[0]
    wide = t_out.shape[1]
    keep_at = pl.multiple_of(info[ODD] * rows, rows)
    give_at = pl.multiple_of((1 - info[ODD]) * rows, rows)
    for at, ref in ((keep_at, r_ref), (give_at, other_ref)):
        t_out[pl.ds(at, rows), :] = (
            t_mid[pl.ds(at, rows), :] + ref[:, :wide].astype(F32) + row(t_bias)
        ).astype(BF)


def make_body(n_dp, n_ctx, n_tp):
    near = n_ctx <= 4

    def swap(x, axis, size, bit):
        return lax.ppermute(x, axis, [(i, i ^ bit) for i in range(size)])

    def tp_sum(give, keep):
        part = (keep + swap(give, "tp", n_tp, 1).astype(F32)).astype(BF)
        part = (part.astype(F32) + swap(part, "tp", n_tp, 2).astype(F32)).astype(BF)
        return part, swap(part, "tp", n_tp, 1)

    def gather_keys(kv):
        if not near:
            return [lax.all_gather(kv, "ctx", axis=1, tiled=True)]
        out = [kv]
        for k in range(1, n_ctx):
            if k == 2:
                step = [(i, i + 1) for i in range(1, n_ctx - 1)]
                out.append(lax.ppermute(out[1], "ctx", step))
            else:
                out.append(lax.ppermute(kv, "ctx", [(i, i + k) for i in range(n_ctx - k)]))
        return out

    def small_sum(v):
        v = v + swap(v, "dp", n_dp, 1)
        bit = 1
        while bit < n_ctx:
            v = v + swap(v, "ctx", n_ctx, 3 if bit == 2 else bit)
            bit *= 2
        return v

    def halve(keep, bit):
        half = keep.shape[0] // 2
        got = swap(keep[half:].astype(BF), "ctx", n_ctx, bit)
        return keep[:half] + got.astype(F32)

    def ring_order(x, ctx):
        piece = x.shape[0] // n_ctx
        if piece % 8 == 0:
            return x
        parts = x.reshape(n_ctx // RING, RING, piece, x.shape[1])
        order = jnp.bitwise_xor(ctx % RING, jnp.array([0, 3, 1, 2], jnp.int32))
        return jnp.swapaxes(jnp.take(parts, order, axis=1), 0, 1).reshape(x.shape)

    def over_rings(keep):
        if n_ctx == RING:
            return keep
        groups = [list(range(r, n_ctx, RING)) for r in range(RING)]
        return lax.psum_scatter(
            keep.astype(BF), "ctx", scatter_dimension=0, axis_index_groups=groups, tiled=True
        ).astype(F32)

    def after(x, *first):
        return lax.optimization_barrier((x,) + first)[0]

    def body(
        teacher_in,
        teacher_gain_a,
        teacher_shift_a,
        teacher_attn_in,
        teacher_attn_bias,
        teacher_attn_out,
        teacher_out_bias,
        teacher_gain_b,
        teacher_shift_b,
        teacher_up,
        teacher_up_bias,
        teacher_down,
        teacher_down_bias,
        student_in,
        student_gain_a,
        student_shift_a,
        student_attn_in,
        student_attn_bias,
        student_attn_out,
        student_out_bias,
        student_gain_b,
        student_shift_b,
        student_up,
        student_up_bias,
        student_down,
        student_down_bias,
        out_grad,
        slot_lengths,
    ):
        slots, rows, wide = teacher_in.shape
        narrow = student_in.shape[2]
        total = slots * rows
        s_cols = student_attn_in.shape[2]
        s_heads = s_cols // HD
        hidden = student_up.shape[1]
        dp = lax.axis_index("dp")
        ctx = lax.axis_index("ctx")
        tp = lax.axis_index("tp")
        local_lengths = lax.dynamic_slice_in_dim(slot_lengths, dp * slots, slots)
        info = jnp.concatenate(
            [
                jnp.stack([ctx * rows, dp, tp % 2, tp, ctx]).astype(jnp.int32),
                local_lengths,
            ]
        )
        t_x = teacher_in.reshape(total, wide)
        s_x = student_in.reshape(total, narrow)
        grad = out_grad.reshape(total, narrow)

        s_in_t = jnp.swapaxes(student_attn_in, 1, 2)
        t_down_t = teacher_down.T
        peer_qkv = swap(s_in_t, "dp", n_dp, 1)
        t_half = wide // 2
        t_mine, t_theirs = run(
            teacher_norm_kernel,
            "teacher_norm",
            [((total, t_half), BF)] * 2,
            [info, t_x, teacher_gain_a, teacher_shift_a],
        )
        t_other = swap(t_theirs, "dp", n_dp, 1)
        peer_out = swap(after(student_attn_out, t_theirs), "dp", n_dp, 1)
        s_x = after(s_x, t_theirs)

        unused_pairs, unused_single, s_kv_width = kv_tiles(s_heads)
        s_q_width = -(-s_cols // PAIR) * PAIR
        s_normed, s_q, s_kv = run(
            functools.partial(student_qkv_kernel, s_heads),
            "student_qkv",
            [((total, narrow), BF), ((total, s_q_width), BF), ((total, s_kv_width), BF)],
            [info, s_x, student_gain_a, student_shift_a, s_in_t, peer_qkv, student_attn_bias],
            flops=2 * total * narrow * 3 * s_cols,
        )
        s_q = s_q.reshape(slots, rows, s_q_width)
        s_kv_list = gather_keys(s_kv.reshape(slots, rows, s_kv_width))

        heads = wide // HD
        cols = heads // n_tp * HD
        tail = wide - n_tp * cols
        t_heads = (cols + tail) // HD
        unused_pairs, unused_single, t_kv_width = kv_tiles(t_heads)
        t_q_width = -(-(cols + tail) // PAIR) * PAIR
        packed = t_kv_width + t_q_width
        t_mine = after(t_mine, s_kv_list[min(1, len(s_kv_list) - 1)], peer_out)
        peer_up = swap(after(student_up, s_kv), "dp", n_dp, 1)
        t_give, t_own, w_out_give = run(
            functools.partial(teacher_qkv_kernel, t_heads, cols),
            "teacher_qkv",
            [((total, packed), BF), ((total, packed), F32), ((t_half, t_q_width), BF)],
            [info, t_mine, t_other, teacher_attn_in, teacher_attn_out],
            specs=[SMEM, VMEM, VMEM, ANY, VMEM],
            scratch=[
                pltpu.VMEM((3, t_half, cols), BF),
                pltpu.VMEM((3, t_half, tail), BF),
                pltpu.SemaphoreType.DMA((2,)),
            ],
            flops=4 * total * wide * (cols + tail) * 3 // 2,
        )
        t_got = swap(t_give, "dp", n_dp, 1)
        blocks = len(s_kv_list)
        keys = blocks * s_kv_list[0].shape[1]
        block_scratch = [pltpu.VMEM((keys, s_kv_width), BF)] if blocks > 1 else []
        s_q = after(s_q, t_give, peer_up)
        s_att, b_give, b_keep = run(
            functools.partial(student_attend_kernel, s_heads, blocks),
            "student_attend",
            [((slots, rows, s_cols), BF), ((rows, narrow), BF), ((rows, narrow), F32)],
            [info, s_q, student_attn_out, peer_out] + s_kv_list,
            scratch=block_scratch,
            flops=4 * total * s_cols * keys,
            extra=total * s_heads * keys,
        )
        peer_down = swap(after(student_down, b_keep), "dp", n_dp, 1)
        b_keep, t_got = lax.optimization_barrier((b_keep, t_got))
        r, other = tp_sum(b_give, b_keep)
        t_own = after(t_own, s_att)
        t_kv, t_q = run(
            functools.partial(teacher_join_kernel, t_heads, cols),
            "teacher_join",
            [((total, t_kv_width), BF), ((total, t_q_width), BF)],
            [info, t_own, t_got, teacher_attn_bias],
        )
        t_kv_list = gather_keys(t_kv.reshape(slots, rows, t_kv_width))
        t_q = t_q.reshape(slots, rows, t_q_width)

        quarter = t_half // 2

        def half_of(w, *first):
            part = lax.dynamic_slice_in_dim(w, (ctx % 2) * quarter, quarter)
            return swap(after(part, *first), "dp", n_dp, 1)

        up_near = half_of(teacher_up, peer_up, peer_down)

        s_x = after(s_x, t_kv_list[-1], t_kv_list[min(1, len(t_kv_list) - 1)])
        s_mid, b_normed, act, d_upper, give, keep = run(
            student_ffn_kernel,
            "student_ffn",
            [
                ((total, narrow), F32),
                ((total, narrow), BF),
                ((total, hidden), BF),
                ((total, hidden), BF),
                ((rows, narrow), BF),
                ((rows, narrow), F32),
            ],
            [
                info,
                s_x,
                student_out_bias,
                student_gain_b,
                student_shift_b,
                student_up_bias,
                r,
                other,
                student_up,
                peer_up,
                student_down,
                peer_down,
                grad,
            ],
            scratch=[pltpu.VMEM((total, narrow), F32)],
            flops=6 * total * narrow * hidden,
        )
        r2, other2 = tp_sum(give, keep)
        t_q = after(t_q, give)
        t_blocks = len(t_kv_list)
        t_scratch = [pltpu.VMEM((keys, t_kv_width), BF)] if t_blocks > 1 else []
        t_att, t_att_tail = run(
            functools.partial(teacher_attend_kernel, t_heads, t_blocks),
            "teacher_attend",
            [((slots, rows, cols), BF), ((slots, rows, tail), BF)],
            [info, t_q] + t_kv_list,
            scratch=t_scratch,
            flops=4 * total * (cols + tail) * keys,
            extra=total * t_heads * keys,
        )
        every = lax.all_gather(t_att.reshape(total, cols), "tp", axis=0)

        s_mid = after(s_mid, every)
        d_scratch = [
            pltpu.VMEM((total, s_q_width), BF),
            pltpu.VMEM((total, narrow), F32),
        ] + block_scratch
        d_outs = run(
            functools.partial(student_back_kernel, s_heads, blocks),
            "student_back",
            [
                ((total, narrow), F32),
                ((total, narrow), BF),
                ((slots, rows, s_cols), BF),
                ((3, narrow), F32),
            ]
            + [
                (item.shape, F32 if (blocks > 1 and i == 0) else BF)
                for i, item in enumerate(s_kv_list)
            ],
            [info, s_mid, student_gain_b, r2, other2, grad, student_attn_out, peer_out, s_q] + s_kv_list,
            scratch=d_scratch,
            flops=10 * total * s_cols * keys,
            extra=total * s_heads * keys,
        )
        d_mid, d_a, d_q, sums_b = d_outs[:4]
        d_parts = d_outs[4:]
        if near:
            d_own = d_parts[0]
            gots = [
                lax.ppermute(d_parts[k], "ctx", [(i + k, i) for i in range(n_ctx - k)])
                for k in range(1, n_ctx)
            ]
        else:
            d_own = lax.psum_scatter(d_parts[0], "ctx", scatter_dimension=1, tiled=True)
            gots = []
        up_near = after(up_near, d_q)
        up_far = swap(up_near, "ctx", n_ctx, 1)
        down_near = half_of(t_down_t, peer_up, peer_down)
        b_normed = after(b_normed, up_near, down_near, d_q)

        g_give, g_keep, sums_f = run(
            functools.partial(student_ffn_grads_kernel, n_ctx),
            "student_ffn_grads",
            [
                ((narrow // 2, 2 * hidden), BF),
                ((narrow // 2, 2 * hidden), F32),
                ((2, narrow), F32),
            ],
            [info, b_normed, act, d_upper, grad],
            scratch=[pltpu.VMEM((narrow, 2 * hidden), F32)],
            flops=4 * total * narrow * hidden,
        )
        down_far = swap(after(down_near, *gots), "ctx", n_ctx, 1)
        w_out_peer = swap(after(w_out_give, peer_up, peer_down), "dp", n_dp, 1)
        every = after(every, g_give, up_far, *gots)
        pieces = [up_near, up_far, down_near, down_far]
        o_cols, o_tail = run(
            teacher_out_kernel,
            "teacher_out",
            [((total, cols), BF), ((total, tail), BF)],
            [info, every, t_att_tail.reshape(total, tail), teacher_attn_out, w_out_peer],
            scratch=[pltpu.VMEM((wide, t_q_width), BF)],
            flops=2 * total * wide * (cols + tail),
        )
        o_every = lax.all_gather(o_cols, "tp", axis=0)
        d_own = d_own.reshape(total, s_kv_width)
        gots = [g.reshape(total, s_kv_width) for g in gots]
        a_give, a_keep, ga_give, ga_keep, sums_q = run(
            functools.partial(student_in_kernel, s_heads, len(gots), n_ctx),
            "student_in",
            [
                ((rows, 2 * narrow), BF),
                ((rows, 2 * narrow), F32),
                ((narrow // n_dp, 4 * s_cols), BF),
                ((narrow // n_dp, 4 * s_cols), F32),
                ((2, s_cols), F32),
            ],
            [
                info,
                d_q.reshape(total, s_cols),
                after(s_normed, o_every),
                d_a,
                s_att.reshape(total, s_cols),
                s_in_t,
                peer_qkv,
                act,
                student_down,
                peer_down,
                d_own,
            ]
            + gots,
            scratch=[pltpu.VMEM((total, 2 * narrow), F32), pltpu.VMEM((narrow, 4 * s_cols), F32)],
            flops=2 * total * narrow * 7 * s_cols,
        )
        r3, other3 = tp_sum(a_give, a_keep)
        g_give, g_keep = ring_order(g_give, ctx), ring_order(g_keep, ctx)
        ga_give, ga_keep = ring_order(ga_give, ctx), ring_order(ga_keep, ctx)
        g_got = swap(after(g_give, w_out_peer), "dp", n_dp, 1)
        ga_got = swap(after(ga_give, w_out_peer), "dp", n_dp, 1)
        g_near = halve(g_keep + after(g_got, down_far).astype(F32), 1)
        d_mid = after(d_mid, g_got, down_far)
        in_grad, s_result, sums = run(
            student_last_kernel,
            "student_last",
            [((total, narrow), F32), ((total, narrow), BF), ((8, narrow), F32)],
            [
                info,
                s_x,
                student_gain_a,
                s_mid,
                student_down_bias,
                r3,
                other3,
                d_mid,
                sums_b,
                sums_f,
                sums_q,
            ],
            scratch=[pltpu.VMEM((total, narrow), F32)],
        )

        t_hidden = teacher_up.shape[1]
        packed = -(-wide // 128) * 128
        t_mid, f_give, f_keep = run(
            functools.partial(teacher_ffn_kernel, 256),
            "teacher_ffn",
            [((total, wide), F32), ((rows, packed), BF), ((rows, packed), F32)],
            [
                info,
                after(t_x, g_got, ga_got, sums),
                teacher_out_bias,
                teacher_gain_b,
                teacher_shift_b,
                teacher_up_bias,
                o_every,
                o_tail,
                teacher_up,
                t_down_t,
            ]
            + pieces,
            specs=[SMEM] + [VMEM] * 7 + [ANY] * 6,
            scratch=[
                pltpu.VMEM((2 * wide, t_hidden), BF),
                pltpu.VMEM((total, t_hidden), BF),
                pltpu.VMEM((total, wide), BF),
                pltpu.VMEM((total, wide), F32),
                pltpu.SemaphoreType.DMA((6,)),
            ],
            flops=4 * total * wide * t_hidden,
        )
        r4, other4 = tp_sum(f_give, after(f_keep, g_near))
        g_ffn = over_rings(halve(g_near, 3))
        ga_got = after(ga_got, f_give)
        g_att = over_rings(halve(halve(ga_keep + ga_got.astype(F32), 1), 3))
        t_result = run(
            last_kernel,
            "last",
            [((total, wide), BF)],
            [info, t_mid, teacher_down_bias, r4, other4],
        )[0]

        small = small_sum(after(sums, f_give))
        piece = narrow // (n_dp * n_ctx)
        shards = lax.dynamic_slice_in_dim(small, (dp * n_ctx + ctx) * piece, piece, axis=1)

        grad_attn_in = jnp.stack([g_att[:, i * s_cols:(i + 1) * s_cols] for i in range(3)])
        return (
            t_result.reshape(slots, rows, wide),
            s_result.reshape(slots, rows, narrow),
            in_grad.reshape(slots, rows, narrow),
            shards[0],
            shards[1],
            grad_attn_in,
            small[7, :2 * s_cols].reshape(2, s_cols),
            g_att[:, 3 * s_cols:].T,
            shards[4],
            shards[2],
            shards[3],
            g_ffn[:, hidden:],
            small[6],
            g_ffn[:, :hidden].T,
            shards[5],
        )

    return body


def solution(mesh):
    sizes = mesh.shape
    return jax.shard_map(
        make_body(sizes["dp"], sizes["ctx"], sizes["tp"]),
        mesh=mesh,
        in_specs=(
            P("dp", "ctx", None),
            P(),
            P(),
            P(None, "dp", None),
            P(),
            P("dp", None),
            P(),
            P(),
            P(),
            P("dp", "tp"),
            P("tp"),
            P("tp", "dp"),
            P(),
            P("dp", "ctx", None),
            P(),
            P(),
            P(None, "dp", "tp"),
            P(None, "tp"),
            P("tp", "dp"),
            P(),
            P(),
            P(),
            P("dp", "tp"),
            P("tp"),
            P("tp", "dp"),
            P(),
            P("dp", "ctx", None),
            P(),
        ),
        out_specs=(
            P("dp", "ctx", None),
            P("dp", "ctx", None),
            P("dp", "ctx", None),
            P(("dp", "ctx")),
            P(("dp", "ctx")),
            P(None, ("dp", "ctx"), "tp"),
            P(None, "tp"),
            P("tp", ("dp", "ctx")),
            P(("dp", "ctx")),
            P(("dp", "ctx")),
            P(("dp", "ctx")),
            P(("dp", "ctx"), "tp"),
            P("tp"),
            P("tp", ("dp", "ctx")),
            P(("dp", "ctx")),
        ),
        check_vma=False,
    )
```

```python
import functools
import math

import jax
import jax.numpy as jnp
from jax import lax
from jax.experimental import pallas as pl
from jax.experimental.pallas import tpu as pltpu
from jax.sharding import PartitionSpec as P

HD = 64
PAIR = 2 * HD
EPS = 1e-05
MASKED = -1000000000.0
FAR = 1 << 30
BF = jnp.bfloat16
F32 = jnp.float32
GELU_C = math.sqrt(2.0 / math.pi)
SMEM = pl.BlockSpec(memory_space=pltpu.SMEM)
VMEM = pl.BlockSpec(memory_space=pltpu.VMEM)
ANY = pl.BlockSpec(memory_space=pl.ANY)
RING = 4
LIMIT = 60 * 1024 * 1024


def dense(left, right):
    return jnp.dot(left, right, preferred_element_type=F32)


def dense_tn(left, right):
    return lax.dot_general(left, right, (((0,), (0,)), ((), ())), preferred_element_type=F32)


def dense_nt(left, right):
    return lax.dot_general(left, right, (((1,), (1,)), ((), ())), preferred_element_type=F32)


def norm_parts(x):
    centered = x - jnp.mean(x, axis=-1, keepdims=True)
    spread = jnp.mean(centered * centered, axis=-1, keepdims=True)
    factor = lax.rsqrt(spread + EPS)
    return centered * factor, factor


def norm_back(d_out, xhat, factor, gain):
    e = d_out * gain
    return factor * (
        e - jnp.mean(e, axis=-1, keepdims=True) - xhat * jnp.mean(e * xhat, axis=-1, keepdims=True)
    )


def gelu_tanh(v):
    return 0.5 * v * (1.0 + jnp.tanh(GELU_C * (v + 0.044715 * v * v * v)))


def gelu_both(v):
    inner = jnp.tanh(GELU_C * (v + 0.044715 * v * v * v))
    slope = 0.5 * (1.0 + inner) + 0.5 * v * (1.0 - inner * inner) * GELU_C * (
        1.0 + 3.0 * 0.044715 * v * v
    )
    return 0.5 * v * (1.0 + inner), slope


BASE, DP, ODD, TP, CTX, LEN = 0, 1, 2, 3, 4, 5


def row(ref):
    return ref[...].astype(F32).reshape(1, -1)


def halves(info, x):
    mid = x.shape[-1] // 2
    first = info[DP] == 0
    left, right = x[:, :mid], x[:, mid:]
    return jnp.where(first, left, right), jnp.where(first, right, left)


def ordered(info, own_peer):
    mid = own_peer.shape[-1] // 2
    first = info[DP] == 0
    own, peer = own_peer[:, :mid], own_peer[:, mid:]
    return jnp.concatenate(
        [jnp.where(first, own, peer), jnp.where(first, peer, own)], axis=-1
    )


def run(kernel, name, outs, args, specs=None, scratch=(), flops=0, extra=0):
    out_shape = [jax.ShapeDtypeStruct(shape, kind) for shape, kind in outs]
    if specs is None:
        specs = [SMEM] + [VMEM] * (len(args) - 1)
    moved = sum(a.size * a.dtype.itemsize for a in args)
    moved += sum(math.prod(o.shape) * o.dtype.itemsize for o in out_shape)
    return pl.pallas_call(
        kernel,
        out_shape=out_shape,
        in_specs=specs,
        out_specs=[VMEM] * len(outs),
        scratch_shapes=list(scratch),
        compiler_params=pltpu.CompilerParams(vmem_limit_bytes=LIMIT),
        cost_estimate=pl.CostEstimate(
            flops=1, bytes_accessed=1, transcendentals=0
        ),
        name=name,
    )(*args)


def kv_tiles(heads):
    pairs = heads // 2
    return pairs, heads % 2, pairs * 2 * PAIR + (heads % 2) * PAIR


def put_kv(ref, k, v, heads):
    pairs, single, unused = kv_tiles(heads)
    for g in range(pairs):
        ref[:, 2 * g * PAIR:(2 * g + 1) * PAIR] = k[:, g * PAIR:(g + 1) * PAIR].astype(ref.dtype)
        ref[:, (2 * g + 1) * PAIR:(2 * g + 2) * PAIR] = v[:, g * PAIR:(g + 1) * PAIR].astype(
            ref.dtype
        )
    if single:
        tail = jnp.concatenate([k[:, pairs * PAIR:], v[:, pairs * PAIR:]], axis=1)
        ref[:, 2 * pairs * PAIR:] = tail.astype(ref.dtype)


def put_q(ref, q, heads):
    pairs, single, unused = kv_tiles(heads)
    q = q * (HD ** -0.5)
    ref[:, :pairs * PAIR] = q[:, :pairs * PAIR].astype(ref.dtype)
    if single:
        tail = q[:, pairs * PAIR:]
        ref[:, pairs * PAIR:] = jnp.concatenate([tail, jnp.zeros_like(tail)], axis=1).astype(
            ref.dtype
        )


def chunks_of(keys):
    width = math.gcd(keys, 512)
    return [(i * width, width) for i in range(keys // width)]


def key_rows(info, rows, blocks, chunks):
    out = []
    for start, width in chunks:
        place = start + lax.broadcasted_iota(jnp.int32, (1, width), 1)
        if blocks > 1:
            place = info[BASE] + place - 2 * rows * (place // rows)
            place = jnp.where(place < 0, FAR, place)
        out.append(place)
    return out


def soft(query, keys, places, bound):
    scores = [
        jnp.where(place <= bound, dense_nt(query, k), MASKED) for place, k in zip(places, keys)
    ]
    top = functools.reduce(jnp.maximum, [jnp.max(s, axis=-1, keepdims=True) for s in scores])
    raised = [jnp.exp(s - top) for s in scores]
    total = functools.reduce(jnp.add, [jnp.sum(r, axis=-1, keepdims=True) for r in raised])
    return raised, 1.0 / total


def add_all(items):
    return functools.reduce(jnp.add, items)


def query_bound(info, slot, rows):
    place = info[BASE] + lax.broadcasted_iota(jnp.int32, (rows, 1), 0)
    return jnp.minimum(place, info[LEN + slot] - 1)


def attend_slot(query_of, kv_of, heads, rows, places, bound):
    pairs, single, unused = kv_tiles(heads)
    lane = lax.broadcasted_iota(jnp.int32, (rows, PAIR), 1)
    low = lane < HD
    out = []
    for g in range(pairs):
        query = query_of(g)
        keys, values = kv_of(2 * g), kv_of(2 * g + 1)
        held = []
        for part in (low, jnp.logical_not(low)):
            one = jnp.where(part, query, jnp.zeros_like(query))
            raised, inverse = soft(one, keys, places, bound)
            held.append(add_all([dense(r.astype(BF), v) for r, v in zip(raised, values)]) * inverse)
        out.append(jnp.where(low, held[0], held[1]))
    if single:
        keys = kv_of(2 * pairs)
        raised, inverse = soft(query_of(pairs), keys, places, bound)
        held = add_all([dense(r.astype(BF), v) for r, v in zip(raised, keys)]) * inverse
        out.append(held[:, HD:])
    return out


def load_blocks(kv_s, kv_refs, slot, rows):
    if kv_s is not None:
        for i, ref in enumerate(kv_refs):
            kv_s[i * rows:(i + 1) * rows, :] = ref[slot]


def kv_reader(kv_s, kv_refs, slot, chunks):
    def kv_of(tile):
        if kv_s is not None:
            return [kv_s[a:a + w, tile * PAIR:(tile + 1) * PAIR] for a, w in chunks]
        return [kv_refs[0][slot, a:a + w, tile * PAIR:(tile + 1) * PAIR] for a, w in chunks]
    return kv_of


def student_attend_kernel(heads, blocks, info, q_ref, own_ref, peer_ref, *refs):
    kv_refs = refs[:blocks]
    att_ref, give_ref, keep_ref = refs[blocks:blocks + 3]
    kv_s = refs[blocks + 3] if blocks > 1 else None
    slots, rows, unused = q_ref.shape
    keys = blocks * kv_refs[0].shape[1]
    chunks = chunks_of(keys)
    half = own_ref.shape[1]

    def one_slot(i, carry):
        slot = jnp.where(i == 0, 1 - info[ODD], info[ODD])
        load_blocks(kv_s, kv_refs, slot, rows)
        out = attend_slot(
            lambda g: q_ref[slot, :, g * PAIR:(g + 1) * PAIR],
            kv_reader(kv_s, kv_refs, slot, chunks),
            heads,
            rows,
            key_rows(info, rows, blocks, chunks),
            query_bound(info, slot, rows),
        )
        att = jnp.concatenate(out, axis=1).astype(BF)
        att_ref[slot] = att
        part = jnp.concatenate([dense(att, own_ref[...]), dense(att, peer_ref[...])], axis=1)

        @pl.when(i == 0)
        def _():
            give_ref[...] = part.astype(BF)

        @pl.when(i == 1)
        def _():
            keep_ref[...] = part

        return carry

    lax.fori_loop(0, slots, one_slot, 0)


def teacher_attend_kernel(heads, blocks, info, q_ref, *refs):
    kv_refs = refs[:blocks]
    att_ref, tail_ref = refs[blocks:blocks + 2]
    kv_s = refs[blocks + 2] if blocks > 1 else None
    slots, rows, unused = q_ref.shape
    chunks = chunks_of(blocks * kv_refs[0].shape[1])
    pairs = heads // 2

    def one_slot(slot, carry):
        load_blocks(kv_s, kv_refs, slot, rows)
        out = attend_slot(
            lambda g: q_ref[slot, :, g * PAIR:(g + 1) * PAIR],
            kv_reader(kv_s, kv_refs, slot, chunks),
            heads,
            rows,
            key_rows(info, rows, blocks, chunks),
            query_bound(info, slot, rows),
        )
        for g in range(pairs):
            att_ref[slot, :, g * PAIR:(g + 1) * PAIR] = out[g].astype(BF)
        tail_ref[slot] = out[pairs].astype(BF)
        return carry

    lax.fori_loop(0, slots, one_slot, 0)


def keep_mask(info, slots, rows):
    row = lax.broadcasted_iota(jnp.int32, (rows, 1), 0) + info[BASE]
    return jnp.concatenate([row < info[LEN + s] for s in range(slots)], axis=0)


def student_back_kernel(
    heads, blocks, info, mid_ref, gain, r_ref, other_ref, grad_ref, own_ref, peer_ref, q_ref, *refs
):
    kv_refs = refs[:blocks]
    d_mid_ref, d_a_ref, d_q_ref, sums_ref = refs[blocks:blocks + 4]
    d_refs = refs[blocks + 4:2 * blocks + 4]
    d_att_s = refs[2 * blocks + 4]
    d_s = refs[2 * blocks + 5]
    kv_s = refs[2 * blocks + 6] if blocks > 1 else None
    slots, rows, unused = q_ref.shape
    chunks = chunks_of(blocks * kv_refs[0].shape[1])
    pairs, single, unused = kv_tiles(heads)
    scale = HD ** -0.5

    d_s[pl.ds(info[ODD] * rows, rows), :] = ordered(info, r_ref[...]).astype(F32)
    d_s[pl.ds((1 - info[ODD]) * rows, rows), :] = ordered(info, other_ref[...]).astype(F32)
    xhat, factor = norm_parts(mid_ref[...])
    d_norm = d_s[...]
    cot = jnp.where(keep_mask(info, slots, rows), grad_ref[...].astype(F32), 0.0)
    d_mid = cot + norm_back(d_norm, xhat, factor, row(gain))
    d_a = d_mid.astype(BF)
    d_mid_ref[...] = d_mid
    d_a_ref[...] = d_a
    sums_ref[0:1, :] = jnp.sum(d_norm * xhat, axis=0, keepdims=True)
    sums_ref[1:2, :] = jnp.sum(d_norm, axis=0, keepdims=True)
    sums_ref[2:3, :] = jnp.sum(d_a.astype(F32), axis=0, keepdims=True)
    mine, theirs = halves(info, d_a)
    d_att = dense_nt(mine, own_ref[...]) + dense_nt(theirs, peer_ref[...])
    width = heads * HD
    d_att_s[:, :pairs * PAIR] = d_att[:, :pairs * PAIR].astype(BF)
    if single:
        tail = d_att[:, pairs * PAIR:width]
        d_att_s[:, pairs * PAIR:] = jnp.concatenate([jnp.zeros_like(tail), tail], axis=1).astype(BF)

    def put(slot, tile, i, value):
        start, size = chunks[i]
        if blocks == 1:
            d_refs[0][slot, start:start + size, tile * PAIR:(tile + 1) * PAIR] = value.astype(
                d_refs[0].dtype
            )
        else:
            for b in range(blocks):
                d_refs[b][slot, :, tile * PAIR:(tile + 1) * PAIR] = value[
                    b * rows:(b + 1) * rows
                ].astype(d_refs[b].dtype)

    def one_slot(slot, carry):
        load_blocks(kv_s, kv_refs, slot, rows)
        kv_of = kv_reader(kv_s, kv_refs, slot, chunks)
        places = key_rows(info, rows, blocks, chunks)
        bound = query_bound(info, slot, rows)
        low = lax.broadcasted_iota(jnp.int32, (rows, PAIR), 1) < HD
        row0 = pl.multiple_of(slot * rows, rows)

        def head(query, d_out, keys, values):
            raised, inverse = soft(query, keys, places, bound)
            probs = [r * inverse for r in raised]
            d_probs = [dense_nt(d_out, v) for v in values]
            delta = add_all(
                [jnp.sum(p * d, axis=-1, keepdims=True) for p, d in zip(probs, d_probs)]
            )
            d_scores = [(p * (d - delta)).astype(BF) for p, d in zip(probs, d_probs)]
            d_query = add_all([dense(s, k) for s, k in zip(d_scores, keys)]) * scale
            d_keys = [dense_tn(s, query) for s in d_scores]
            d_values = [dense_tn(p.astype(BF), d_out) for p in probs]
            return d_query, d_keys, d_values

        for g in range(pairs):
            query = q_ref[slot, :, g * PAIR:(g + 1) * PAIR]
            d_out = d_att_s[pl.ds(row0, rows), g * PAIR:(g + 1) * PAIR]
            keys, values = kv_of(2 * g), kv_of(2 * g + 1)
            zero = jnp.zeros_like(query)
            a = head(jnp.where(low, query, zero), jnp.where(low, d_out, zero), keys, values)
            b = head(jnp.where(low, zero, query), jnp.where(low, zero, d_out), keys, values)
            d_q_ref[slot, :, g * PAIR:(g + 1) * PAIR] = jnp.where(low, a[0], b[0]).astype(BF)
            for i in range(len(chunks)):
                put(slot, 2 * g, i, a[1][i] + b[1][i])
                put(slot, 2 * g + 1, i, a[2][i] + b[2][i])
        if single:
            query = q_ref[slot, :, pairs * PAIR:]
            d_out = d_att_s[pl.ds(row0, rows), pairs * PAIR:]
            keys = kv_of(2 * pairs)
            a = head(query, d_out, keys, keys)
            d_q_ref[slot, :, pairs * PAIR:] = a[0][:, :HD].astype(BF)
            for i in range(len(chunks)):
                put(slot, 2 * pairs, i, a[1][i] + a[2][i])
        return carry

    lax.fori_loop(0, slots, one_slot, 0)


def student_qkv_kernel(heads, info, x, gain, shift, own, peer, bias, normed_ref, q_ref, kv_ref):
    xhat, unused = norm_parts(x[...].astype(F32))
    normed = (xhat * row(gain) + row(shift)).astype(BF)
    normed_ref[...] = normed
    mine, theirs = halves(info, normed)

    def project(i):
        return dense_nt(mine, own[i]) + dense_nt(theirs, peer[i])

    put_kv(kv_ref, project(1), project(2) + bias[1:2, :].astype(F32), heads)
    put_q(q_ref, (project(0) + bias[0:1, :].astype(F32)).astype(BF), heads)


def student_ffn_kernel(
    info, x, out_bias, gain, shift, up_bias, r_ref, other_ref, up_own, up_peer, down_own,
    down_peer, grad, mid_ref, normed_ref, act_ref, d_upper_ref, give_ref, keep_ref, part_s,
):
    rows = r_ref.shape[0]
    slots = x.shape[0] // rows
    keep_at = pl.multiple_of(info[ODD] * rows, rows)
    give_at = pl.multiple_of((1 - info[ODD]) * rows, rows)
    for at, ref in ((keep_at, r_ref), (give_at, other_ref)):
        mid_ref[pl.ds(at, rows), :] = (
            x[pl.ds(at, rows), :].astype(F32) + ordered(info, ref[...]).astype(F32) + row(out_bias)
        )
    xhat, unused = norm_parts(mid_ref[...])
    normed = (xhat * row(gain) + row(shift)).astype(BF)
    normed_ref[...] = normed
    mine, theirs = halves(info, normed)
    upper = dense(mine, up_own[...]) + dense(theirs, up_peer[...]) + row(up_bias)
    act, slope = gelu_both(upper)
    act_ref[...] = act.astype(BF)
    d_b = jnp.where(keep_mask(info, slots, rows), grad[...].astype(F32), 0.0).astype(BF)
    d_mine, d_theirs = halves(info, d_b)
    d_act = (dense_nt(d_mine, down_own[...]) + dense_nt(d_theirs, down_peer[...])).astype(BF)
    d_upper = (d_act.astype(F32) * slope).astype(BF)
    d_upper_ref[...] = d_upper
    half = up_own.shape[0]
    part_s[:, :half] = dense_nt(d_upper, up_own[...])
    part_s[:, half:] = dense_nt(d_upper, up_peer[...])
    give_ref[...] = part_s[pl.ds(give_at, rows), :].astype(BF)
    keep_ref[...] = part_s[pl.ds(keep_at, rows), :]


def split_rows(info, n_ctx, grad_s, give_ref, keep_ref):
    full = grad_s.shape[0]
    piece = full // (2 * n_ctx)
    count = n_ctx // RING
    if piece % 8:
        for half, ref in ((info[DP], keep_ref), (1 - info[DP], give_ref)):
            start = pl.multiple_of(half * (full // 2), 16)
            ref[...] = grad_s[pl.ds(start, full // 2), :].astype(ref.dtype)
        return
    place = lax.rem(info[CTX], RING)
    for i, flip in enumerate((0, 3, 1, 2)):
        for q in range(count):
            to = (i * count + q) * piece
            at = (q * RING + (place ^ flip)) * piece
            for half, ref in ((info[DP], keep_ref), (1 - info[DP], give_ref)):
                start = pl.multiple_of(half * (full // 2) + at, math.gcd(piece, 16))
                ref[to:to + piece, :] = grad_s[pl.ds(start, piece), :].astype(ref.dtype)


def student_ffn_grads_kernel(
    n_ctx, info, normed, act, d_upper, grad, give_ref, keep_ref, sums_ref, grad_s
):
    slots = info.shape[0] - LEN
    rows = normed.shape[0] // slots
    d_b = jnp.where(keep_mask(info, slots, rows), grad[...].astype(F32), 0.0).astype(BF)
    hidden = act.shape[1]
    grad_s[:, :hidden] = dense_tn(d_b, act[...])
    grad_s[:, hidden:] = dense_tn(normed[...], d_upper[...])
    split_rows(info, n_ctx, grad_s, give_ref, keep_ref)
    sums_ref[0:1, :] = jnp.sum(d_b.astype(F32), axis=0, keepdims=True)
    sums_ref[1:2, :] = jnp.sum(d_upper[...].astype(F32), axis=0, keepdims=True)


def student_in_kernel(
    heads, n_got, n_ctx, info, d_q, normed, d_a, att, own, peer, act, down_own, down_peer, d_kv,
    *refs
):
    gots = refs[:n_got]
    give_ref, keep_ref, g_give, g_keep, bias_ref, part_s, grad_s = refs[n_got:]
    rows = give_ref.shape[0]
    pairs, single, unused = kv_tiles(heads)
    total = d_kv[...].astype(F32)
    for got in gots:
        total = total + got[...].astype(F32)
    total = total.astype(BF)
    d_k = [total[:, 2 * g * PAIR:(2 * g + 1) * PAIR] for g in range(pairs)]
    d_v = [total[:, (2 * g + 1) * PAIR:(2 * g + 2) * PAIR] for g in range(pairs)]
    if single:
        d_k.append(total[:, 2 * pairs * PAIR:2 * pairs * PAIR + HD])
        d_v.append(total[:, 2 * pairs * PAIR + HD:])
    d_k = jnp.concatenate(d_k, axis=1)
    d_v = jnp.concatenate(d_v, axis=1)
    half = own.shape[2]

    def back(w):
        return dense(d_q[...], w[0]) + dense(d_k, w[1]) + dense(d_v, w[2])

    part_s[:, :half] = back(own)
    part_s[:, half:2 * half] = back(peer)
    part_s[:, 2 * half:3 * half] = dense(act[...], down_own[...])
    part_s[:, 3 * half:] = dense(act[...], down_peer[...])
    give_ref[...] = part_s[pl.ds((1 - info[ODD]) * rows, rows), :].astype(BF)
    keep_ref[...] = part_s[pl.ds(info[ODD] * rows, rows), :]
    cols = heads * HD
    n = normed[...]
    grad_s[:, :cols] = dense_tn(n, d_q[...])
    grad_s[:, cols:2 * cols] = dense_tn(n, d_k)
    grad_s[:, 2 * cols:3 * cols] = dense_tn(n, d_v)
    grad_s[:, 3 * cols:] = dense_tn(d_a[...], att[...])
    split_rows(info, n_ctx, grad_s, g_give, g_keep)
    bias_ref[0:1, :] = jnp.sum(d_q[...].astype(F32), axis=0, keepdims=True)
    bias_ref[1:2, :] = jnp.sum(d_v.astype(F32), axis=0, keepdims=True)


def student_last_kernel(
    info, x, gain, s_mid, s_bias, r_ref, other_ref, d_mid, sums_b, sums_f, sums_q,
    out_ref, s_out, sums_ref, d_s,
):
    rows = r_ref.shape[0]
    width = x.shape[1]
    for at, ref in ((info[ODD] * rows, r_ref), ((1 - info[ODD]) * rows, other_ref)):
        at = pl.multiple_of(at, rows)
        d_s[pl.ds(at, rows), :] = ordered(info, ref[:, :width]).astype(F32)
        s_out[pl.ds(at, rows), :] = (
            s_mid[pl.ds(at, rows), :] + ordered(info, ref[:, width:]).astype(F32) + row(s_bias)
        ).astype(BF)
    xhat, factor = norm_parts(x[...].astype(F32))
    d_norm = d_s[...]
    out_ref[...] = d_mid[...] + norm_back(d_norm, xhat, factor, row(gain))
    sums_ref[0:1, :] = jnp.sum(d_norm * xhat, axis=0, keepdims=True)
    sums_ref[1:2, :] = jnp.sum(d_norm, axis=0, keepdims=True)
    sums_ref[2:5, :] = sums_b[...]
    sums_ref[5:7, :] = sums_f[...]
    rest = out_ref.shape[1] - 2 * sums_q.shape[1]
    sums_ref[7:8, :] = jnp.concatenate(
        [sums_q[0:1, :], sums_q[1:2, :], jnp.zeros((1, rest), F32)], axis=1
    )


def teacher_norm_kernel(info, x, gain, shift, mine_ref, theirs_ref):
    xhat, unused = norm_parts(x[...].astype(F32))
    normed = (xhat * row(gain) + row(shift)).astype(BF)
    mine, theirs = halves(info, normed)
    mine_ref[...] = mine
    theirs_ref[...] = theirs


def teacher_qkv_kernel(
    heads, cols, info, mine, other, w_hbm, wo, give_ref, own_ref, wo_ref, w, w_tail, sems
):
    pairs, unused, kv_width = kv_tiles(heads)
    col0 = pl.multiple_of(info[TP] * cols, cols)
    wide = w_hbm.shape[2]
    tail = w_tail.shape[2]
    copies = [
        pltpu.make_async_copy(w_hbm.at[:, :, pl.ds(col0, cols)], w, sems.at[0]),
        pltpu.make_async_copy(w_hbm.at[:, :, pl.ds(wide - tail, tail)], w_tail, sems.at[1]),
    ]
    for copy in copies:
        copy.start()
    wo_ref[:, :cols] = wo[:, pl.ds(col0, cols)]
    last = wo[:, wide - tail:]
    wo_ref[:, cols:] = jnp.concatenate([last, jnp.zeros_like(last)], axis=1)
    for copy in copies:
        copy.wait()
    for source, target in ((other, give_ref), (mine, own_ref)):
        x = source[...]
        k, v, q = (dense(x, w[i]) for i in (1, 2, 0))
        tk, tv, tq = (dense(x, w_tail[i]) for i in (1, 2, 0))
        kind = target.dtype
        for g in range(pairs):
            a = 2 * g * PAIR
            target[:, a:a + PAIR] = k[:, g * PAIR:(g + 1) * PAIR].astype(kind)
            target[:, a + PAIR:a + 2 * PAIR] = v[:, g * PAIR:(g + 1) * PAIR].astype(kind)
        target[:, 2 * pairs * PAIR:kv_width] = jnp.concatenate([tk, tv], axis=1).astype(kind)
        target[:, kv_width:kv_width + cols] = q.astype(kind)
        target[:, kv_width + cols:] = jnp.concatenate([tq, jnp.zeros_like(tq)], axis=1).astype(kind)


def teacher_join_kernel(heads, cols, info, own, got, bias, kv_ref, q_ref):
    pairs, unused, kv_width = kv_tiles(heads)
    whole = own[...] + got[...].astype(F32)
    b = bias[:, pl.ds(pl.multiple_of(info[TP] * cols, cols), cols)].astype(F32)
    t = bias[:, bias.shape[1] - HD:].astype(F32)
    zero = jnp.zeros_like(t[0:1])
    for g in range(pairs):
        a = 2 * g * PAIR
        kv_ref[:, a:a + PAIR] = whole[:, a:a + PAIR].astype(BF)
        kv_ref[:, a + PAIR:a + 2 * PAIR] = (
            whole[:, a + PAIR:a + 2 * PAIR] + b[1:2, g * PAIR:(g + 1) * PAIR]
        ).astype(BF)
    a = 2 * pairs * PAIR
    kv_ref[:, a:] = (whole[:, a:kv_width] + jnp.concatenate([zero, t[1:2]], axis=1)).astype(BF)
    q = (whole[:, kv_width:] + jnp.concatenate([b[0:1], t[0:1], zero], axis=1)).astype(BF)
    q_ref[...] = (q * (HD ** -0.5)).astype(BF)


def teacher_out_kernel(info, every, tail, w, peer, out_ref, out_tail_ref, w_s):
    half = w.shape[0]
    n, unused, cols = every.shape
    extra = tail.shape[1]
    own_at = pl.multiple_of(info[DP] * half, 16)
    peer_at = pl.multiple_of((1 - info[DP]) * half, 16)
    w_s[pl.ds(own_at, half), :cols] = w[:, pl.ds(pl.multiple_of(info[TP] * cols, cols), cols)]
    last = w[:, w.shape[1] - extra:]
    w_s[pl.ds(own_at, half), cols:] = jnp.concatenate([last, jnp.zeros_like(last)], axis=1)
    w_s[pl.ds(peer_at, half), :] = peer[...]
    total = dense(tail[...], w_s[n * cols:, :])
    for i in range(n):
        total = total + dense(every[i], w_s[i * cols:(i + 1) * cols, :])
    out_ref[...] = total[:, :cols].astype(BF)
    out_tail_ref[...] = total[:, cols:cols + extra].astype(BF)


def teacher_ffn_kernel(
    tile, info, x, out_bias, gain, shift, up_bias, every, tail, up_own, down_own,
    up_near, up_far, down_near, down_far, mid_ref, give_ref, keep_ref, w_s, act_s, normed_s, part_s, sems,
):
    half, hidden = up_own.shape
    wide = 2 * half
    own_at = pl.multiple_of(info[DP] * half, 16)
    peer_at = (1 - info[DP]) * half
    copies = [
        pltpu.make_async_copy(up_own, w_s.at[pl.ds(own_at, half)], sems.at[0]),
        pltpu.make_async_copy(
            down_own, w_s.at[pl.ds(pl.multiple_of(own_at + wide, 16), half)], sems.at[1]
        ),
    ]
    size = up_near.shape[0]
    bit = lax.rem(info[CTX], 2)
    for i, (part, base, place) in enumerate(
        ((up_near, 0, bit), (up_far, 0, 1 - bit), (down_near, wide, bit), (down_far, wide, 1 - bit))
    ):
        at = pl.multiple_of(peer_at + base + place * size, 16)
        copies.append(pltpu.make_async_copy(part, w_s.at[pl.ds(at, size)], sems.at[i + 2]))
    for copy in copies:
        copy.start()
    n, unused, cols = every.shape
    bias = row(out_bias)
    for i in range(n):
        a = i * cols
        mid_ref[:, a:a + cols] = (
            x[:, a:a + cols].astype(F32) + every[i].astype(F32) + bias[:, a:a + cols]
        )
    a = n * cols
    mid_ref[:, a:] = x[:, a:].astype(F32) + tail[...].astype(F32) + bias[:, a:]
    xhat, unused = norm_parts(mid_ref[...])
    normed_s[...] = (xhat * row(gain) + row(shift)).astype(BF)
    rows, packed = give_ref.shape
    for copy in copies:
        copy.wait()
    up_row = row(up_bias)
    at = 0
    while at < hidden:
        size = min(tile, hidden - at)
        v = dense(normed_s[...], w_s[:wide, at:at + size]) + up_row[:, at:at + size]
        act_s[:, at:at + size] = gelu_tanh(v).astype(BF)
        at += size
    part_s[...] = dense_nt(act_s[...], w_s[wide:, :])
    give_ref[:, :wide] = part_s[pl.ds((1 - info[ODD]) * rows, rows), :].astype(BF)
    keep_ref[:, :wide] = part_s[pl.ds(info[ODD] * rows, rows), :]
    give_ref[:, wide:] = jnp.zeros((rows, packed - wide), BF)
    keep_ref[:, wide:] = jnp.zeros((rows, packed - wide), F32)


def last_kernel(info, t_mid, t_bias, r_ref, other_ref, t_out):
    rows = r_ref.shape[0]
    wide = t_out.shape[1]
    keep_at = pl.multiple_of(info[ODD] * rows, rows)
    give_at = pl.multiple_of((1 - info[ODD]) * rows, rows)
    for at, ref in ((keep_at, r_ref), (give_at, other_ref)):
        t_out[pl.ds(at, rows), :] = (
            t_mid[pl.ds(at, rows), :] + ref[:, :wide].astype(F32) + row(t_bias)
        ).astype(BF)


def make_body(n_dp, n_ctx, n_tp):
    near = n_ctx <= 4

    def swap(x, axis, size, bit):
        return lax.ppermute(x, axis, [(i, i ^ bit) for i in range(size)])

    def tp_sum(give, keep):
        part = (keep + swap(give, "tp", n_tp, 1).astype(F32)).astype(BF)
        part = (part.astype(F32) + swap(part, "tp", n_tp, 2).astype(F32)).astype(BF)
        return part, swap(part, "tp", n_tp, 1)

    def gather_keys(kv):
        if not near:
            return [lax.all_gather(kv, "ctx", axis=1, tiled=True)]
        out = [kv]
        for k in range(1, n_ctx):
            if k == 2:
                step = [(i, i + 1) for i in range(1, n_ctx - 1)]
                out.append(lax.ppermute(out[1], "ctx", step))
            else:
                out.append(lax.ppermute(kv, "ctx", [(i, i + k) for i in range(n_ctx - k)]))
        return out

    def small_sum(v):
        v = v + swap(v, "dp", n_dp, 1)
        bit = 1
        while bit < n_ctx:
            v = v + swap(v, "ctx", n_ctx, 3 if bit == 2 else bit)
            bit *= 2
        return v

    def halve(keep, bit):
        half = keep.shape[0] // 2
        got = swap(keep[half:].astype(BF), "ctx", n_ctx, bit)
        return keep[:half] + got.astype(F32)

    def ring_order(x, ctx):
        piece = x.shape[0] // n_ctx
        if piece % 8 == 0:
            return x
        parts = x.reshape(n_ctx // RING, RING, piece, x.shape[1])
        order = jnp.bitwise_xor(ctx % RING, jnp.array([0, 3, 1, 2], jnp.int32))
        return jnp.swapaxes(jnp.take(parts, order, axis=1), 0, 1).reshape(x.shape)

    def over_rings(keep):
        if n_ctx == RING:
            return keep
        groups = [list(range(r, n_ctx, RING)) for r in range(RING)]
        return lax.psum_scatter(
            keep.astype(BF), "ctx", scatter_dimension=0, axis_index_groups=groups, tiled=True
        ).astype(F32)

    def after(x, *first):
        return lax.optimization_barrier((x,) + first)[0]

    def body(
        teacher_in,
        teacher_gain_a,
        teacher_shift_a,
        teacher_attn_in,
        teacher_attn_bias,
        teacher_attn_out,
        teacher_out_bias,
        teacher_gain_b,
        teacher_shift_b,
        teacher_up,
        teacher_up_bias,
        teacher_down,
        teacher_down_bias,
        student_in,
        student_gain_a,
        student_shift_a,
        student_attn_in,
        student_attn_bias,
        student_attn_out,
        student_out_bias,
        student_gain_b,
        student_shift_b,
        student_up,
        student_up_bias,
        student_down,
        student_down_bias,
        out_grad,
        slot_lengths,
    ):
        slots, rows, wide = teacher_in.shape
        narrow = student_in.shape[2]
        total = slots * rows
        s_cols = student_attn_in.shape[2]
        s_heads = s_cols // HD
        hidden = student_up.shape[1]
        dp = lax.axis_index("dp")
        ctx = lax.axis_index("ctx")
        tp = lax.axis_index("tp")
        local_lengths = lax.dynamic_slice_in_dim(slot_lengths, dp * slots, slots)
        info = jnp.concatenate(
            [
                jnp.stack([ctx * rows, dp, tp % 2, tp, ctx]).astype(jnp.int32),
                local_lengths,
            ]
        )
        t_x = teacher_in.reshape(total, wide)
        s_x = student_in.reshape(total, narrow)
        grad = out_grad.reshape(total, narrow)

        s_in_t = jnp.swapaxes(student_attn_in, 1, 2)
        t_down_t = teacher_down.T
        peer_qkv = swap(s_in_t, "dp", n_dp, 1)
        t_half = wide // 2
        t_mine, t_theirs = run(
            teacher_norm_kernel,
            "teacher_norm",
            [((total, t_half), BF)] * 2,
            [info, t_x, teacher_gain_a, teacher_shift_a],
        )
        t_other = swap(t_theirs, "dp", n_dp, 1)
        peer_out = swap(after(student_attn_out, t_theirs), "dp", n_dp, 1)
        s_x = after(s_x, t_theirs)

        unused_pairs, unused_single, s_kv_width = kv_tiles(s_heads)
        s_q_width = -(-s_cols // PAIR) * PAIR
        s_normed, s_q, s_kv = run(
            functools.partial(student_qkv_kernel, s_heads),
            "student_qkv",
            [((total, narrow), BF), ((total, s_q_width), BF), ((total, s_kv_width), BF)],
            [info, s_x, student_gain_a, student_shift_a, s_in_t, peer_qkv, student_attn_bias],
            flops=2 * total * narrow * 3 * s_cols,
        )
        s_q = s_q.reshape(slots, rows, s_q_width)
        s_kv_list = gather_keys(s_kv.reshape(slots, rows, s_kv_width))

        heads = wide // HD
        cols = heads // n_tp * HD
        tail = wide - n_tp * cols
        t_heads = (cols + tail) // HD
        unused_pairs, unused_single, t_kv_width = kv_tiles(t_heads)
        t_q_width = -(-(cols + tail) // PAIR) * PAIR
        packed = t_kv_width + t_q_width
        t_mine = after(t_mine, s_kv_list[min(1, len(s_kv_list) - 1)], peer_out)
        peer_up = swap(after(student_up, s_kv), "dp", n_dp, 1)
        t_give, t_own, w_out_give = run(
            functools.partial(teacher_qkv_kernel, t_heads, cols),
            "teacher_qkv",
            [((total, packed), BF), ((total, packed), F32), ((t_half, t_q_width), BF)],
            [info, t_mine, t_other, teacher_attn_in, teacher_attn_out],
            specs=[SMEM, VMEM, VMEM, ANY, VMEM],
            scratch=[
                pltpu.VMEM((3, t_half, cols), BF),
                pltpu.VMEM((3, t_half, tail), BF),
                pltpu.SemaphoreType.DMA((2,)),
            ],
            flops=4 * total * wide * (cols + tail) * 3 // 2,
        )
        t_got = swap(t_give, "dp", n_dp, 1)
        blocks = len(s_kv_list)
        keys = blocks * s_kv_list[0].shape[1]
        block_scratch = [pltpu.VMEM((keys, s_kv_width), BF)] if blocks > 1 else []
        s_q = after(s_q, t_give, peer_up)
        s_att, b_give, b_keep = run(
            functools.partial(student_attend_kernel, s_heads, blocks),
            "student_attend",
            [((slots, rows, s_cols), BF), ((rows, narrow), BF), ((rows, narrow), F32)],
            [info, s_q, student_attn_out, peer_out] + s_kv_list,
            scratch=block_scratch,
            flops=4 * total * s_cols * keys,
            extra=total * s_heads * keys,
        )
        peer_down = swap(after(student_down, b_keep), "dp", n_dp, 1)
        b_keep, t_got = lax.optimization_barrier((b_keep, t_got))
        r, other = tp_sum(b_give, b_keep)
        t_own = after(t_own, s_att)
        t_kv, t_q = run(
            functools.partial(teacher_join_kernel, t_heads, cols),
            "teacher_join",
            [((total, t_kv_width), BF), ((total, t_q_width), BF)],
            [info, t_own, t_got, teacher_attn_bias],
        )
        t_kv_list = gather_keys(t_kv.reshape(slots, rows, t_kv_width))
        t_q = t_q.reshape(slots, rows, t_q_width)

        quarter = t_half // 2

        def half_of(w, *first):
            part = lax.dynamic_slice_in_dim(w, (ctx % 2) * quarter, quarter)
            return swap(after(part, *first), "dp", n_dp, 1)

        up_near = half_of(teacher_up, peer_up, peer_down)

        s_x = after(s_x, t_kv_list[-1], t_kv_list[min(1, len(t_kv_list) - 1)])
        s_mid, b_normed, act, d_upper, give, keep = run(
            student_ffn_kernel,
            "student_ffn",
            [
                ((total, narrow), F32),
                ((total, narrow), BF),
                ((total, hidden), BF),
                ((total, hidden), BF),
                ((rows, narrow), BF),
                ((rows, narrow), F32),
            ],
            [
                info,
                s_x,
                student_out_bias,
                student_gain_b,
                student_shift_b,
                student_up_bias,
                r,
                other,
                student_up,
                peer_up,
                student_down,
                peer_down,
                grad,
            ],
            scratch=[pltpu.VMEM((total, narrow), F32)],
            flops=6 * total * narrow * hidden,
        )
        r2, other2 = tp_sum(give, keep)
        t_q = after(t_q, give)
        t_blocks = len(t_kv_list)
        t_scratch = [pltpu.VMEM((keys, t_kv_width), BF)] if t_blocks > 1 else []
        t_att, t_att_tail = run(
            functools.partial(teacher_attend_kernel, t_heads, t_blocks),
            "teacher_attend",
            [((slots, rows, cols), BF), ((slots, rows, tail), BF)],
            [info, t_q] + t_kv_list,
            scratch=t_scratch,
            flops=4 * total * (cols + tail) * keys,
            extra=total * t_heads * keys,
        )
        every = lax.all_gather(t_att.reshape(total, cols), "tp", axis=0)

        s_mid = after(s_mid, every)
        d_scratch = [
            pltpu.VMEM((total, s_q_width), BF),
            pltpu.VMEM((total, narrow), F32),
        ] + block_scratch
        d_outs = run(
            functools.partial(student_back_kernel, s_heads, blocks),
            "student_back",
            [
                ((total, narrow), F32),
                ((total, narrow), BF),
                ((slots, rows, s_cols), BF),
                ((3, narrow), F32),
            ]
            + [
                (item.shape, F32 if (blocks > 1 and i == 0) else BF)
                for i, item in enumerate(s_kv_list)
            ],
            [info, s_mid, student_gain_b, r2, other2, grad, student_attn_out, peer_out, s_q] + s_kv_list,
            scratch=d_scratch,
            flops=10 * total * s_cols * keys,
            extra=total * s_heads * keys,
        )
        d_mid, d_a, d_q, sums_b = d_outs[:4]
        d_parts = d_outs[4:]
        if near:
            d_own = d_parts[0]
            gots = [
                lax.ppermute(d_parts[k], "ctx", [(i + k, i) for i in range(n_ctx - k)])
                for k in range(1, n_ctx)
            ]
        else:
            d_own = lax.psum_scatter(d_parts[0], "ctx", scatter_dimension=1, tiled=True)
            gots = []
        up_near = after(up_near, d_q)
        up_far = swap(up_near, "ctx", n_ctx, 1)
        down_near = half_of(t_down_t, peer_up, peer_down)
        b_normed = after(b_normed, up_near, d_q)

        g_give, g_keep, sums_f = run(
            functools.partial(student_ffn_grads_kernel, n_ctx),
            "student_ffn_grads",
            [
                ((narrow // 2, 2 * hidden), BF),
                ((narrow // 2, 2 * hidden), F32),
                ((2, narrow), F32),
            ],
            [info, b_normed, act, d_upper, grad],
            scratch=[pltpu.VMEM((narrow, 2 * hidden), F32)],
            flops=4 * total * narrow * hidden,
        )
        down_far = swap(down_near, "ctx", n_ctx, 1)
        w_out_peer = swap(after(w_out_give, peer_up, peer_down), "dp", n_dp, 1)
        every = after(every, g_give, down_near)
        pieces = [up_near, up_far, down_near, down_far]
        o_cols, o_tail = run(
            teacher_out_kernel,
            "teacher_out",
            [((total, cols), BF), ((total, tail), BF)],
            [info, every, t_att_tail.reshape(total, tail), teacher_attn_out, w_out_peer],
            scratch=[pltpu.VMEM((wide, t_q_width), BF)],
            flops=2 * total * wide * (cols + tail),
        )
        o_every = lax.all_gather(o_cols, "tp", axis=0)
        d_own = d_own.reshape(total, s_kv_width)
        gots = [g.reshape(total, s_kv_width) for g in gots]
        a_give, a_keep, ga_give, ga_keep, sums_q = run(
            functools.partial(student_in_kernel, s_heads, len(gots), n_ctx),
            "student_in",
            [
                ((rows, 2 * narrow), BF),
                ((rows, 2 * narrow), F32),
                ((narrow // n_dp, 4 * s_cols), BF),
                ((narrow // n_dp, 4 * s_cols), F32),
                ((2, s_cols), F32),
            ],
            [
                info,
                d_q.reshape(total, s_cols),
                after(s_normed, o_every),
                d_a,
                s_att.reshape(total, s_cols),
                s_in_t,
                peer_qkv,
                act,
                student_down,
                peer_down,
                d_own,
            ]
            + gots,
            scratch=[pltpu.VMEM((total, 2 * narrow), F32), pltpu.VMEM((narrow, 4 * s_cols), F32)],
            flops=2 * total * narrow * 7 * s_cols,
        )
        r3, other3 = tp_sum(a_give, a_keep)
        g_give, g_keep = ring_order(g_give, ctx), ring_order(g_keep, ctx)
        ga_give, ga_keep = ring_order(ga_give, ctx), ring_order(ga_keep, ctx)
        g_got = swap(after(g_give, w_out_peer), "dp", n_dp, 1)
        ga_got = swap(after(ga_give, w_out_peer), "dp", n_dp, 1)
        g_near = halve(g_keep + after(g_got, down_far).astype(F32), 1)
        t_hidden = teacher_up.shape[1]
        packed = -(-wide // 128) * 128
        t_mid, f_give, f_keep = run(
            functools.partial(teacher_ffn_kernel, 256),
            "teacher_ffn",
            [((total, wide), F32), ((rows, packed), BF), ((rows, packed), F32)],
            [
                info,
                after(t_x, g_got),
                teacher_out_bias,
                teacher_gain_b,
                teacher_shift_b,
                teacher_up_bias,
                o_every,
                o_tail,
                teacher_up,
                t_down_t,
            ]
            + pieces,
            specs=[SMEM] + [VMEM] * 7 + [ANY] * 6,
            scratch=[
                pltpu.VMEM((2 * wide, t_hidden), BF),
                pltpu.VMEM((total, t_hidden), BF),
                pltpu.VMEM((total, wide), BF),
                pltpu.VMEM((total, wide), F32),
                pltpu.SemaphoreType.DMA((6,)),
            ],
            flops=4 * total * wide * t_hidden,
        )
        part = (after(f_keep, g_near) + swap(f_give, "tp", n_tp, 1).astype(F32)).astype(BF)
        r4 = (part.astype(F32) + swap(part, "tp", n_tp, 2).astype(F32)).astype(BF)
        other4 = swap(r4, "tp", n_tp, 1)
        g_ffn = over_rings(halve(after(g_near, part), 3))
        ga_got = after(ga_got, part)
        g_att = over_rings(halve(halve(ga_keep + ga_got.astype(F32), 1), 3))
        d_mid = after(d_mid, part)
        in_grad, s_result, sums = run(
            student_last_kernel,
            "student_last",
            [((total, narrow), F32), ((total, narrow), BF), ((8, narrow), F32)],
            [
                info,
                s_x,
                student_gain_a,
                s_mid,
                student_down_bias,
                r3,
                other3,
                d_mid,
                sums_b,
                sums_f,
                sums_q,
            ],
            scratch=[pltpu.VMEM((total, narrow), F32)],
        )

        t_result = run(
            last_kernel,
            "last",
            [((total, wide), BF)],
            [info, t_mid, teacher_down_bias, r4, other4],
        )[0]

        small = small_sum(after(sums, r4))
        piece = narrow // (n_dp * n_ctx)
        shards = lax.dynamic_slice_in_dim(small, (dp * n_ctx + ctx) * piece, piece, axis=1)

        grad_attn_in = jnp.stack([g_att[:, i * s_cols:(i + 1) * s_cols] for i in range(3)])
        return (
            t_result.reshape(slots, rows, wide),
            s_result.reshape(slots, rows, narrow),
            in_grad.reshape(slots, rows, narrow),
            shards[0],
            shards[1],
            grad_attn_in,
            small[7, :2 * s_cols].reshape(2, s_cols),
            g_att[:, 3 * s_cols:].T,
            shards[4],
            shards[2],
            shards[3],
            g_ffn[:, hidden:],
            small[6],
            g_ffn[:, :hidden].T,
            shards[5],
        )

    return body


def solution(mesh):
    sizes = mesh.shape
    return jax.shard_map(
        make_body(sizes["dp"], sizes["ctx"], sizes["tp"]),
        mesh=mesh,
        in_specs=(
            P("dp", "ctx", None),
            P(),
            P(),
            P(None, "dp", None),
            P(),
            P("dp", None),
            P(),
            P(),
            P(),
            P("dp", "tp"),
            P("tp"),
            P("tp", "dp"),
            P(),
            P("dp", "ctx", None),
            P(),
            P(),
            P(None, "dp", "tp"),
            P(None, "tp"),
            P("tp", "dp"),
            P(),
            P(),
            P(),
            P("dp", "tp"),
            P("tp"),
            P("tp", "dp"),
            P(),
            P("dp", "ctx", None),
            P(),
        ),
        out_specs=(
            P("dp", "ctx", None),
            P("dp", "ctx", None),
            P("dp", "ctx", None),
            P(("dp", "ctx")),
            P(("dp", "ctx")),
            P(None, ("dp", "ctx"), "tp"),
            P(None, "tp"),
            P("tp", ("dp", "ctx")),
            P(("dp", "ctx")),
            P(("dp", "ctx")),
            P(("dp", "ctx")),
            P(("dp", "ctx"), "tp"),
            P("tp"),
            P("tp", ("dp", "ctx")),
            P(("dp", "ctx")),
        ),
        check_vma=False,
    )
```

```python
import functools
import math

import jax
import jax.numpy as jnp
from jax import lax
from jax.experimental import pallas as pl
from jax.experimental.pallas import tpu as pltpu
from jax.sharding import PartitionSpec as P

HD = 64
PAIR = 2 * HD
EPS = 1e-05
MASKED = -1000000000.0
FAR = 1 << 30
BF = jnp.bfloat16
F32 = jnp.float32
GELU_C = math.sqrt(2.0 / math.pi)
SMEM = pl.BlockSpec(memory_space=pltpu.SMEM)
VMEM = pl.BlockSpec(memory_space=pltpu.VMEM)
ANY = pl.BlockSpec(memory_space=pl.ANY)
RING = 4
LIMIT = 60 * 1024 * 1024


def dense(left, right):
    return jnp.dot(left, right, preferred_element_type=F32)


def dense_tn(left, right):
    return lax.dot_general(left, right, (((0,), (0,)), ((), ())), preferred_element_type=F32)


def dense_nt(left, right):
    return lax.dot_general(left, right, (((1,), (1,)), ((), ())), preferred_element_type=F32)


def norm_parts(x):
    centered = x - jnp.mean(x, axis=-1, keepdims=True)
    spread = jnp.mean(centered * centered, axis=-1, keepdims=True)
    factor = lax.rsqrt(spread + EPS)
    return centered * factor, factor


def norm_back(d_out, xhat, factor, gain):
    e = d_out * gain
    return factor * (
        e - jnp.mean(e, axis=-1, keepdims=True) - xhat * jnp.mean(e * xhat, axis=-1, keepdims=True)
    )


def gelu_tanh(v):
    return 0.5 * v * (1.0 + jnp.tanh(GELU_C * (v + 0.044715 * v * v * v)))


def gelu_both(v):
    inner = jnp.tanh(GELU_C * (v + 0.044715 * v * v * v))
    slope = 0.5 * (1.0 + inner) + 0.5 * v * (1.0 - inner * inner) * GELU_C * (
        1.0 + 3.0 * 0.044715 * v * v
    )
    return 0.5 * v * (1.0 + inner), slope


BASE, DP, ODD, TP, CTX, LEN = 0, 1, 2, 3, 4, 5


def row(ref):
    return ref[...].astype(F32).reshape(1, -1)


def halves(info, x):
    mid = x.shape[-1] // 2
    first = info[DP] == 0
    left, right = x[:, :mid], x[:, mid:]
    return jnp.where(first, left, right), jnp.where(first, right, left)


def ordered(info, own_peer):
    mid = own_peer.shape[-1] // 2
    first = info[DP] == 0
    own, peer = own_peer[:, :mid], own_peer[:, mid:]
    return jnp.concatenate(
        [jnp.where(first, own, peer), jnp.where(first, peer, own)], axis=-1
    )


def run(kernel, name, outs, args, specs=None, scratch=(), flops=0, extra=0):
    out_shape = [jax.ShapeDtypeStruct(shape, kind) for shape, kind in outs]
    if specs is None:
        specs = [SMEM] + [VMEM] * (len(args) - 1)
    moved = sum(a.size * a.dtype.itemsize for a in args)
    moved += sum(math.prod(o.shape) * o.dtype.itemsize for o in out_shape)
    return pl.pallas_call(
        kernel,
        out_shape=out_shape,
        in_specs=specs,
        out_specs=[VMEM] * len(outs),
        scratch_shapes=list(scratch),
        compiler_params=pltpu.CompilerParams(vmem_limit_bytes=LIMIT),
        cost_estimate=pl.CostEstimate(
            flops=1, bytes_accessed=1, transcendentals=0
        ),
        name=name,
    )(*args)


def kv_tiles(heads):
    pairs = heads // 2
    return pairs, heads % 2, pairs * 2 * PAIR + (heads % 2) * PAIR


def put_kv(ref, k, v, heads):
    pairs, single, unused = kv_tiles(heads)
    for g in range(pairs):
        ref[:, 2 * g * PAIR:(2 * g + 1) * PAIR] = k[:, g * PAIR:(g + 1) * PAIR].astype(ref.dtype)
        ref[:, (2 * g + 1) * PAIR:(2 * g + 2) * PAIR] = v[:, g * PAIR:(g + 1) * PAIR].astype(
            ref.dtype
        )
    if single:
        tail = jnp.concatenate([k[:, pairs * PAIR:], v[:, pairs * PAIR:]], axis=1)
        ref[:, 2 * pairs * PAIR:] = tail.astype(ref.dtype)


def put_q(ref, q, heads):
    pairs, single, unused = kv_tiles(heads)
    q = q * (HD ** -0.5)
    ref[:, :pairs * PAIR] = q[:, :pairs * PAIR].astype(ref.dtype)
    if single:
        tail = q[:, pairs * PAIR:]
        ref[:, pairs * PAIR:] = jnp.concatenate([tail, jnp.zeros_like(tail)], axis=1).astype(
            ref.dtype
        )


def chunks_of(keys):
    width = math.gcd(keys, 512)
    return [(i * width, width) for i in range(keys // width)]


def key_rows(info, rows, blocks, chunks):
    out = []
    for start, width in chunks:
        place = start + lax.broadcasted_iota(jnp.int32, (1, width), 1)
        if blocks > 1:
            place = info[BASE] + place - 2 * rows * (place // rows)
            place = jnp.where(place < 0, FAR, place)
        out.append(place)
    return out


def soft(query, keys, places, bound):
    scores = [
        jnp.where(place <= bound, dense_nt(query, k), MASKED) for place, k in zip(places, keys)
    ]
    top = functools.reduce(jnp.maximum, [jnp.max(s, axis=-1, keepdims=True) for s in scores])
    raised = [jnp.exp(s - top) for s in scores]
    total = functools.reduce(jnp.add, [jnp.sum(r, axis=-1, keepdims=True) for r in raised])
    return raised, 1.0 / total


def add_all(items):
    return functools.reduce(jnp.add, items)


def query_bound(info, slot, rows):
    place = info[BASE] + lax.broadcasted_iota(jnp.int32, (rows, 1), 0)
    return jnp.minimum(place, info[LEN + slot] - 1)


def attend_slot(query_of, kv_of, heads, rows, places, bound):
    pairs, single, unused = kv_tiles(heads)
    lane = lax.broadcasted_iota(jnp.int32, (rows, PAIR), 1)
    low = lane < HD
    out = []
    for g in range(pairs):
        query = query_of(g)
        keys, values = kv_of(2 * g), kv_of(2 * g + 1)
        held = []
        for part in (low, jnp.logical_not(low)):
            one = jnp.where(part, query, jnp.zeros_like(query))
            raised, inverse = soft(one, keys, places, bound)
            held.append(add_all([dense(r.astype(BF), v) for r, v in zip(raised, values)]) * inverse)
        out.append(jnp.where(low, held[0], held[1]))
    if single:
        keys = kv_of(2 * pairs)
        raised, inverse = soft(query_of(pairs), keys, places, bound)
        held = add_all([dense(r.astype(BF), v) for r, v in zip(raised, keys)]) * inverse
        out.append(held[:, HD:])
    return out


def load_blocks(kv_s, kv_refs, slot, rows):
    if kv_s is not None:
        for i, ref in enumerate(kv_refs):
            kv_s[i * rows:(i + 1) * rows, :] = ref[slot]


def kv_reader(kv_s, kv_refs, slot, chunks):
    def kv_of(tile):
        if kv_s is not None:
            return [kv_s[a:a + w, tile * PAIR:(tile + 1) * PAIR] for a, w in chunks]
        return [kv_refs[0][slot, a:a + w, tile * PAIR:(tile + 1) * PAIR] for a, w in chunks]
    return kv_of


def student_attend_kernel(heads, blocks, info, q_ref, own_ref, peer_ref, *refs):
    kv_refs = refs[:blocks]
    att_ref, give_ref, keep_ref = refs[blocks:blocks + 3]
    kv_s = refs[blocks + 3] if blocks > 1 else None
    slots, rows, unused = q_ref.shape
    keys = blocks * kv_refs[0].shape[1]
    chunks = chunks_of(keys)
    half = own_ref.shape[1]

    def one_slot(i, carry):
        slot = jnp.where(i == 0, 1 - info[ODD], info[ODD])
        load_blocks(kv_s, kv_refs, slot, rows)
        out = attend_slot(
            lambda g: q_ref[slot, :, g * PAIR:(g + 1) * PAIR],
            kv_reader(kv_s, kv_refs, slot, chunks),
            heads,
            rows,
            key_rows(info, rows, blocks, chunks),
            query_bound(info, slot, rows),
        )
        att = jnp.concatenate(out, axis=1).astype(BF)
        att_ref[slot] = att
        part = jnp.concatenate([dense(att, own_ref[...]), dense(att, peer_ref[...])], axis=1)

        @pl.when(i == 0)
        def _():
            give_ref[...] = part.astype(BF)

        @pl.when(i == 1)
        def _():
            keep_ref[...] = part

        return carry

    lax.fori_loop(0, slots, one_slot, 0)


def teacher_attend_kernel(heads, blocks, info, q_ref, *refs):
    kv_refs = refs[:blocks]
    att_ref, tail_ref = refs[blocks:blocks + 2]
    kv_s = refs[blocks + 2] if blocks > 1 else None
    slots, rows, unused = q_ref.shape
    chunks = chunks_of(blocks * kv_refs[0].shape[1])
    pairs = heads // 2

    def one_slot(slot, carry):
        load_blocks(kv_s, kv_refs, slot, rows)
        out = attend_slot(
            lambda g: q_ref[slot, :, g * PAIR:(g + 1) * PAIR],
            kv_reader(kv_s, kv_refs, slot, chunks),
            heads,
            rows,
            key_rows(info, rows, blocks, chunks),
            query_bound(info, slot, rows),
        )
        for g in range(pairs):
            att_ref[slot, :, g * PAIR:(g + 1) * PAIR] = out[g].astype(BF)
        tail_ref[slot] = out[pairs].astype(BF)
        return carry

    lax.fori_loop(0, slots, one_slot, 0)


def keep_mask(info, slots, rows):
    row = lax.broadcasted_iota(jnp.int32, (rows, 1), 0) + info[BASE]
    return jnp.concatenate([row < info[LEN + s] for s in range(slots)], axis=0)


def student_back_kernel(
    heads, blocks, info, mid_ref, gain, r_ref, other_ref, grad_ref, own_ref, peer_ref, q_ref, *refs
):
    kv_refs = refs[:blocks]
    d_mid_ref, d_a_ref, d_q_ref, sums_ref = refs[blocks:blocks + 4]
    d_refs = refs[blocks + 4:2 * blocks + 4]
    d_att_s = refs[2 * blocks + 4]
    d_s = refs[2 * blocks + 5]
    kv_s = refs[2 * blocks + 6] if blocks > 1 else None
    slots, rows, unused = q_ref.shape
    chunks = chunks_of(blocks * kv_refs[0].shape[1])
    pairs, single, unused = kv_tiles(heads)
    scale = HD ** -0.5

    d_s[pl.ds(info[ODD] * rows, rows), :] = ordered(info, r_ref[...]).astype(F32)
    d_s[pl.ds((1 - info[ODD]) * rows, rows), :] = ordered(info, other_ref[...]).astype(F32)
    xhat, factor = norm_parts(mid_ref[...])
    d_norm = d_s[...]
    cot = jnp.where(keep_mask(info, slots, rows), grad_ref[...].astype(F32), 0.0)
    d_mid = cot + norm_back(d_norm, xhat, factor, row(gain))
    d_a = d_mid.astype(BF)
    d_mid_ref[...] = d_mid
    d_a_ref[...] = d_a
    sums_ref[0:1, :] = jnp.sum(d_norm * xhat, axis=0, keepdims=True)
    sums_ref[1:2, :] = jnp.sum(d_norm, axis=0, keepdims=True)
    sums_ref[2:3, :] = jnp.sum(d_a.astype(F32), axis=0, keepdims=True)
    mine, theirs = halves(info, d_a)
    d_att = dense_nt(mine, own_ref[...]) + dense_nt(theirs, peer_ref[...])
    width = heads * HD
    d_att_s[:, :pairs * PAIR] = d_att[:, :pairs * PAIR].astype(BF)
    if single:
        tail = d_att[:, pairs * PAIR:width]
        d_att_s[:, pairs * PAIR:] = jnp.concatenate([jnp.zeros_like(tail), tail], axis=1).astype(BF)

    def put(slot, tile, i, value):
        start, size = chunks[i]
        if blocks == 1:
            d_refs[0][slot, start:start + size, tile * PAIR:(tile + 1) * PAIR] = value.astype(
                d_refs[0].dtype
            )
        else:
            for b in range(blocks):
                d_refs[b][slot, :, tile * PAIR:(tile + 1) * PAIR] = value[
                    b * rows:(b + 1) * rows
                ].astype(d_refs[b].dtype)

    def one_slot(slot, carry):
        load_blocks(kv_s, kv_refs, slot, rows)
        kv_of = kv_reader(kv_s, kv_refs, slot, chunks)
        places = key_rows(info, rows, blocks, chunks)
        bound = query_bound(info, slot, rows)
        low = lax.broadcasted_iota(jnp.int32, (rows, PAIR), 1) < HD
        row0 = pl.multiple_of(slot * rows, rows)

        def head(query, d_out, keys, values):
            raised, inverse = soft(query, keys, places, bound)
            probs = [r * inverse for r in raised]
            d_probs = [dense_nt(d_out, v) for v in values]
            delta = add_all(
                [jnp.sum(p * d, axis=-1, keepdims=True) for p, d in zip(probs, d_probs)]
            )
            d_scores = [(p * (d - delta)).astype(BF) for p, d in zip(probs, d_probs)]
            d_query = add_all([dense(s, k) for s, k in zip(d_scores, keys)]) * scale
            d_keys = [dense_tn(s, query) for s in d_scores]
            d_values = [dense_tn(p.astype(BF), d_out) for p in probs]
            return d_query, d_keys, d_values

        for g in range(pairs):
            query = q_ref[slot, :, g * PAIR:(g + 1) * PAIR]
            d_out = d_att_s[pl.ds(row0, rows), g * PAIR:(g + 1) * PAIR]
            keys, values = kv_of(2 * g), kv_of(2 * g + 1)
            zero = jnp.zeros_like(query)
            a = head(jnp.where(low, query, zero), jnp.where(low, d_out, zero), keys, values)
            b = head(jnp.where(low, zero, query), jnp.where(low, zero, d_out), keys, values)
            d_q_ref[slot, :, g * PAIR:(g + 1) * PAIR] = jnp.where(low, a[0], b[0]).astype(BF)
            for i in range(len(chunks)):
                put(slot, 2 * g, i, a[1][i] + b[1][i])
                put(slot, 2 * g + 1, i, a[2][i] + b[2][i])
        if single:
            query = q_ref[slot, :, pairs * PAIR:]
            d_out = d_att_s[pl.ds(row0, rows), pairs * PAIR:]
            keys = kv_of(2 * pairs)
            a = head(query, d_out, keys, keys)
            d_q_ref[slot, :, pairs * PAIR:] = a[0][:, :HD].astype(BF)
            for i in range(len(chunks)):
                put(slot, 2 * pairs, i, a[1][i] + a[2][i])
        return carry

    lax.fori_loop(0, slots, one_slot, 0)


def student_qkv_kernel(heads, info, x, gain, shift, own, peer, bias, normed_ref, q_ref, kv_ref):
    xhat, unused = norm_parts(x[...].astype(F32))
    normed = (xhat * row(gain) + row(shift)).astype(BF)
    normed_ref[...] = normed
    mine, theirs = halves(info, normed)

    def project(i):
        return dense_nt(mine, own[i]) + dense_nt(theirs, peer[i])

    put_kv(kv_ref, project(1), project(2) + bias[1:2, :].astype(F32), heads)
    put_q(q_ref, (project(0) + bias[0:1, :].astype(F32)).astype(BF), heads)


def student_ffn_kernel(
    info, x, out_bias, gain, shift, up_bias, r_ref, other_ref, up_own, up_peer, down_own,
    down_peer, grad, mid_ref, normed_ref, act_ref, d_upper_ref, give_ref, keep_ref, part_s,
):
    rows = r_ref.shape[0]
    slots = x.shape[0] // rows
    keep_at = pl.multiple_of(info[ODD] * rows, rows)
    give_at = pl.multiple_of((1 - info[ODD]) * rows, rows)
    for at, ref in ((keep_at, r_ref), (give_at, other_ref)):
        mid_ref[pl.ds(at, rows), :] = (
            x[pl.ds(at, rows), :].astype(F32) + ordered(info, ref[...]).astype(F32) + row(out_bias)
        )
    xhat, unused = norm_parts(mid_ref[...])
    normed = (xhat * row(gain) + row(shift)).astype(BF)
    normed_ref[...] = normed
    mine, theirs = halves(info, normed)
    upper = dense(mine, up_own[...]) + dense(theirs, up_peer[...]) + row(up_bias)
    act, slope = gelu_both(upper)
    act_ref[...] = act.astype(BF)
    d_b = jnp.where(keep_mask(info, slots, rows), grad[...].astype(F32), 0.0).astype(BF)
    d_mine, d_theirs = halves(info, d_b)
    d_act = (dense_nt(d_mine, down_own[...]) + dense_nt(d_theirs, down_peer[...])).astype(BF)
    d_upper = (d_act.astype(F32) * slope).astype(BF)
    d_upper_ref[...] = d_upper
    half = up_own.shape[0]
    part_s[:, :half] = dense_nt(d_upper, up_own[...])
    part_s[:, half:] = dense_nt(d_upper, up_peer[...])
    give_ref[...] = part_s[pl.ds(give_at, rows), :].astype(BF)
    keep_ref[...] = part_s[pl.ds(keep_at, rows), :]


def split_rows(info, n_ctx, grad_s, give_ref, keep_ref):
    full = grad_s.shape[0]
    piece = full // (2 * n_ctx)
    count = n_ctx // RING
    if piece % 8:
        for half, ref in ((info[DP], keep_ref), (1 - info[DP], give_ref)):
            start = pl.multiple_of(half * (full // 2), 16)
            ref[...] = grad_s[pl.ds(start, full // 2), :].astype(ref.dtype)
        return
    place = lax.rem(info[CTX], RING)
    for i, flip in enumerate((0, 3, 1, 2)):
        for q in range(count):
            to = (i * count + q) * piece
            at = (q * RING + (place ^ flip)) * piece
            for half, ref in ((info[DP], keep_ref), (1 - info[DP], give_ref)):
                start = pl.multiple_of(half * (full // 2) + at, math.gcd(piece, 16))
                ref[to:to + piece, :] = grad_s[pl.ds(start, piece), :].astype(ref.dtype)


def student_ffn_grads_kernel(
    n_ctx, info, normed, act, d_upper, grad, give_ref, keep_ref, sums_ref, grad_s
):
    slots = info.shape[0] - LEN
    rows = normed.shape[0] // slots
    d_b = jnp.where(keep_mask(info, slots, rows), grad[...].astype(F32), 0.0).astype(BF)
    hidden = act.shape[1]
    grad_s[:, :hidden] = dense_tn(d_b, act[...])
    grad_s[:, hidden:] = dense_tn(normed[...], d_upper[...])
    split_rows(info, n_ctx, grad_s, give_ref, keep_ref)
    sums_ref[0:1, :] = jnp.sum(d_b.astype(F32), axis=0, keepdims=True)
    sums_ref[1:2, :] = jnp.sum(d_upper[...].astype(F32), axis=0, keepdims=True)


def student_in_kernel(
    heads, n_got, n_ctx, info, d_q, normed, d_a, att, own, peer, act, down_own, down_peer, d_kv,
    *refs
):
    gots = refs[:n_got]
    give_ref, keep_ref, g_give, g_keep, bias_ref, part_s, grad_s = refs[n_got:]
    rows = give_ref.shape[0]
    pairs, single, unused = kv_tiles(heads)
    total = d_kv[...].astype(F32)
    for got in gots:
        total = total + got[...].astype(F32)
    total = total.astype(BF)
    d_k = [total[:, 2 * g * PAIR:(2 * g + 1) * PAIR] for g in range(pairs)]
    d_v = [total[:, (2 * g + 1) * PAIR:(2 * g + 2) * PAIR] for g in range(pairs)]
    if single:
        d_k.append(total[:, 2 * pairs * PAIR:2 * pairs * PAIR + HD])
        d_v.append(total[:, 2 * pairs * PAIR + HD:])
    d_k = jnp.concatenate(d_k, axis=1)
    d_v = jnp.concatenate(d_v, axis=1)
    half = own.shape[2]

    def back(w):
        return dense(d_q[...], w[0]) + dense(d_k, w[1]) + dense(d_v, w[2])

    part_s[:, :half] = back(own)
    part_s[:, half:2 * half] = back(peer)
    part_s[:, 2 * half:3 * half] = dense(act[...], down_own[...])
    part_s[:, 3 * half:] = dense(act[...], down_peer[...])
    give_ref[...] = part_s[pl.ds((1 - info[ODD]) * rows, rows), :].astype(BF)
    keep_ref[...] = part_s[pl.ds(info[ODD] * rows, rows), :]
    cols = heads * HD
    n = normed[...]
    grad_s[:, :cols] = dense_tn(n, d_q[...])
    grad_s[:, cols:2 * cols] = dense_tn(n, d_k)
    grad_s[:, 2 * cols:3 * cols] = dense_tn(n, d_v)
    grad_s[:, 3 * cols:] = dense_tn(d_a[...], att[...])
    split_rows(info, n_ctx, grad_s, g_give, g_keep)
    bias_ref[0:1, :] = jnp.sum(d_q[...].astype(F32), axis=0, keepdims=True)
    bias_ref[1:2, :] = jnp.sum(d_v.astype(F32), axis=0, keepdims=True)


def student_last_kernel(
    info, x, gain, s_mid, s_bias, r_ref, other_ref, d_mid, sums_b, sums_f, sums_q,
    out_ref, s_out, sums_ref, d_s,
):
    rows = r_ref.shape[0]
    width = x.shape[1]
    for at, ref in ((info[ODD] * rows, r_ref), ((1 - info[ODD]) * rows, other_ref)):
        at = pl.multiple_of(at, rows)
        d_s[pl.ds(at, rows), :] = ordered(info, ref[:, :width]).astype(F32)
        s_out[pl.ds(at, rows), :] = (
            s_mid[pl.ds(at, rows), :] + ordered(info, ref[:, width:]).astype(F32) + row(s_bias)
        ).astype(BF)
    xhat, factor = norm_parts(x[...].astype(F32))
    d_norm = d_s[...]
    out_ref[...] = d_mid[...] + norm_back(d_norm, xhat, factor, row(gain))
    sums_ref[0:1, :] = jnp.sum(d_norm * xhat, axis=0, keepdims=True)
    sums_ref[1:2, :] = jnp.sum(d_norm, axis=0, keepdims=True)
    sums_ref[2:5, :] = sums_b[...]
    sums_ref[5:7, :] = sums_f[...]
    rest = out_ref.shape[1] - 2 * sums_q.shape[1]
    sums_ref[7:8, :] = jnp.concatenate(
        [sums_q[0:1, :], sums_q[1:2, :], jnp.zeros((1, rest), F32)], axis=1
    )


def teacher_norm_kernel(info, x, gain, shift, mine_ref, theirs_ref):
    xhat, unused = norm_parts(x[...].astype(F32))
    normed = (xhat * row(gain) + row(shift)).astype(BF)
    mine, theirs = halves(info, normed)
    mine_ref[...] = mine
    theirs_ref[...] = theirs


def teacher_qkv_kernel(
    heads, cols, info, mine, other, w_hbm, wo, give_ref, own_ref, wo_ref, w, w_tail, sems
):
    pairs, unused, kv_width = kv_tiles(heads)
    col0 = pl.multiple_of(info[TP] * cols, cols)
    wide = w_hbm.shape[2]
    tail = w_tail.shape[2]
    copies = [
        pltpu.make_async_copy(w_hbm.at[:, :, pl.ds(col0, cols)], w, sems.at[0]),
        pltpu.make_async_copy(w_hbm.at[:, :, pl.ds(wide - tail, tail)], w_tail, sems.at[1]),
    ]
    for copy in copies:
        copy.start()
    wo_ref[:, :cols] = wo[:, pl.ds(col0, cols)]
    last = wo[:, wide - tail:]
    wo_ref[:, cols:] = jnp.concatenate([last, jnp.zeros_like(last)], axis=1)
    for copy in copies:
        copy.wait()
    for source, target in ((other, give_ref), (mine, own_ref)):
        x = source[...]
        k, v, q = (dense(x, w[i]) for i in (1, 2, 0))
        tk, tv, tq = (dense(x, w_tail[i]) for i in (1, 2, 0))
        kind = target.dtype
        for g in range(pairs):
            a = 2 * g * PAIR
            target[:, a:a + PAIR] = k[:, g * PAIR:(g + 1) * PAIR].astype(kind)
            target[:, a + PAIR:a + 2 * PAIR] = v[:, g * PAIR:(g + 1) * PAIR].astype(kind)
        target[:, 2 * pairs * PAIR:kv_width] = jnp.concatenate([tk, tv], axis=1).astype(kind)
        target[:, kv_width:kv_width + cols] = q.astype(kind)
        target[:, kv_width + cols:] = jnp.concatenate([tq, jnp.zeros_like(tq)], axis=1).astype(kind)


def teacher_join_kernel(heads, cols, info, own, got, bias, kv_ref, q_ref):
    pairs, unused, kv_width = kv_tiles(heads)
    whole = own[...] + got[...].astype(F32)
    b = bias[:, pl.ds(pl.multiple_of(info[TP] * cols, cols), cols)].astype(F32)
    t = bias[:, bias.shape[1] - HD:].astype(F32)
    zero = jnp.zeros_like(t[0:1])
    for g in range(pairs):
        a = 2 * g * PAIR
        kv_ref[:, a:a + PAIR] = whole[:, a:a + PAIR].astype(BF)
        kv_ref[:, a + PAIR:a + 2 * PAIR] = (
            whole[:, a + PAIR:a + 2 * PAIR] + b[1:2, g * PAIR:(g + 1) * PAIR]
        ).astype(BF)
    a = 2 * pairs * PAIR
    kv_ref[:, a:] = (whole[:, a:kv_width] + jnp.concatenate([zero, t[1:2]], axis=1)).astype(BF)
    q = (whole[:, kv_width:] + jnp.concatenate([b[0:1], t[0:1], zero], axis=1)).astype(BF)
    q_ref[...] = (q * (HD ** -0.5)).astype(BF)


def teacher_out_kernel(info, every, tail, w, peer, out_ref, out_tail_ref, w_s):
    half = w.shape[0]
    n, unused, cols = every.shape
    extra = tail.shape[1]
    own_at = pl.multiple_of(info[DP] * half, 16)
    peer_at = pl.multiple_of((1 - info[DP]) * half, 16)
    w_s[pl.ds(own_at, half), :cols] = w[:, pl.ds(pl.multiple_of(info[TP] * cols, cols), cols)]
    last = w[:, w.shape[1] - extra:]
    w_s[pl.ds(own_at, half), cols:] = jnp.concatenate([last, jnp.zeros_like(last)], axis=1)
    w_s[pl.ds(peer_at, half), :] = peer[...]
    total = dense(tail[...], w_s[n * cols:, :])
    for i in range(n):
        total = total + dense(every[i], w_s[i * cols:(i + 1) * cols, :])
    out_ref[...] = total[:, :cols].astype(BF)
    out_tail_ref[...] = total[:, cols:cols + extra].astype(BF)


def teacher_ffn_kernel(
    tile, info, x, out_bias, gain, shift, up_bias, every, tail, up_own, down_own,
    up_near, up_far, down_near, down_far, mid_ref, give_ref, keep_ref, w_s, act_s, normed_s, part_s, sems,
):
    half, hidden = up_own.shape
    wide = 2 * half
    own_at = pl.multiple_of(info[DP] * half, 16)
    peer_at = (1 - info[DP]) * half
    copies = [
        pltpu.make_async_copy(up_own, w_s.at[pl.ds(own_at, half)], sems.at[0]),
        pltpu.make_async_copy(
            down_own, w_s.at[pl.ds(pl.multiple_of(own_at + wide, 16), half)], sems.at[1]
        ),
    ]
    size = up_near.shape[0]
    bit = lax.rem(info[CTX], 2)
    for i, (part, base, place) in enumerate(
        ((up_near, 0, bit), (up_far, 0, 1 - bit), (down_near, wide, bit), (down_far, wide, 1 - bit))
    ):
        at = pl.multiple_of(peer_at + base + place * size, 16)
        copies.append(pltpu.make_async_copy(part, w_s.at[pl.ds(at, size)], sems.at[i + 2]))
    for copy in copies:
        copy.start()
    n, unused, cols = every.shape
    bias = row(out_bias)
    for i in range(n):
        a = i * cols
        mid_ref[:, a:a + cols] = (
            x[:, a:a + cols].astype(F32) + every[i].astype(F32) + bias[:, a:a + cols]
        )
    a = n * cols
    mid_ref[:, a:] = x[:, a:].astype(F32) + tail[...].astype(F32) + bias[:, a:]
    xhat, unused = norm_parts(mid_ref[...])
    normed_s[...] = (xhat * row(gain) + row(shift)).astype(BF)
    rows, packed = give_ref.shape
    for copy in copies:
        copy.wait()
    up_row = row(up_bias)
    at = 0
    while at < hidden:
        size = min(tile, hidden - at)
        v = dense(normed_s[...], w_s[:wide, at:at + size]) + up_row[:, at:at + size]
        act_s[:, at:at + size] = gelu_tanh(v).astype(BF)
        at += size
    part_s[...] = dense_nt(act_s[...], w_s[wide:, :])
    give_ref[:, :wide] = part_s[pl.ds((1 - info[ODD]) * rows, rows), :].astype(BF)
    keep_ref[:, :wide] = part_s[pl.ds(info[ODD] * rows, rows), :]
    give_ref[:, wide:] = jnp.zeros((rows, packed - wide), BF)
    keep_ref[:, wide:] = jnp.zeros((rows, packed - wide), F32)


def last_kernel(info, t_mid, t_bias, r_ref, other_ref, t_out):
    rows = r_ref.shape[0]
    wide = t_out.shape[1]
    keep_at = pl.multiple_of(info[ODD] * rows, rows)
    give_at = pl.multiple_of((1 - info[ODD]) * rows, rows)
    for at, ref in ((keep_at, r_ref), (give_at, other_ref)):
        t_out[pl.ds(at, rows), :] = (
            t_mid[pl.ds(at, rows), :] + ref[:, :wide].astype(F32) + row(t_bias)
        ).astype(BF)


def make_body(n_dp, n_ctx, n_tp):
    near = n_ctx <= 4

    def swap(x, axis, size, bit):
        return lax.ppermute(x, axis, [(i, i ^ bit) for i in range(size)])

    def tp_sum(give, keep):
        part = (keep + swap(give, "tp", n_tp, 1).astype(F32)).astype(BF)
        part = (part.astype(F32) + swap(part, "tp", n_tp, 2).astype(F32)).astype(BF)
        return part, swap(part, "tp", n_tp, 1)

    def gather_keys(kv):
        if not near:
            return [lax.all_gather(kv, "ctx", axis=1, tiled=True)]
        out = [kv]
        for k in range(1, n_ctx):
            if k == 2:
                step = [(i, i + 1) for i in range(1, n_ctx - 1)]
                out.append(lax.ppermute(out[1], "ctx", step))
            else:
                out.append(lax.ppermute(kv, "ctx", [(i, i + k) for i in range(n_ctx - k)]))
        return out

    def small_sum(v):
        v = v + swap(v, "dp", n_dp, 1)
        bit = 1
        while bit < n_ctx:
            v = v + swap(v, "ctx", n_ctx, 3 if bit == 2 else bit)
            bit *= 2
        return v

    def halve(keep, bit):
        half = keep.shape[0] // 2
        got = swap(keep[half:].astype(BF), "ctx", n_ctx, bit)
        return keep[:half] + got.astype(F32)

    def ring_order(x, ctx):
        piece = x.shape[0] // n_ctx
        if piece % 8 == 0:
            return x
        parts = x.reshape(n_ctx // RING, RING, piece, x.shape[1])
        order = jnp.bitwise_xor(ctx % RING, jnp.array([0, 3, 1, 2], jnp.int32))
        return jnp.swapaxes(jnp.take(parts, order, axis=1), 0, 1).reshape(x.shape)

    def over_rings(keep):
        if n_ctx == RING:
            return keep
        groups = [list(range(r, n_ctx, RING)) for r in range(RING)]
        return lax.psum_scatter(
            keep.astype(BF), "ctx", scatter_dimension=0, axis_index_groups=groups, tiled=True
        ).astype(F32)

    def after(x, *first):
        return lax.optimization_barrier((x,) + first)[0]

    def body(
        teacher_in,
        teacher_gain_a,
        teacher_shift_a,
        teacher_attn_in,
        teacher_attn_bias,
        teacher_attn_out,
        teacher_out_bias,
        teacher_gain_b,
        teacher_shift_b,
        teacher_up,
        teacher_up_bias,
        teacher_down,
        teacher_down_bias,
        student_in,
        student_gain_a,
        student_shift_a,
        student_attn_in,
        student_attn_bias,
        student_attn_out,
        student_out_bias,
        student_gain_b,
        student_shift_b,
        student_up,
        student_up_bias,
        student_down,
        student_down_bias,
        out_grad,
        slot_lengths,
    ):
        slots, rows, wide = teacher_in.shape
        narrow = student_in.shape[2]
        total = slots * rows
        s_cols = student_attn_in.shape[2]
        s_heads = s_cols // HD
        hidden = student_up.shape[1]
        dp = lax.axis_index("dp")
        ctx = lax.axis_index("ctx")
        tp = lax.axis_index("tp")
        local_lengths = lax.dynamic_slice_in_dim(slot_lengths, dp * slots, slots)
        info = jnp.concatenate(
            [
                jnp.stack([ctx * rows, dp, tp % 2, tp, ctx]).astype(jnp.int32),
                local_lengths,
            ]
        )
        t_x = teacher_in.reshape(total, wide)
        s_x = student_in.reshape(total, narrow)
        grad = out_grad.reshape(total, narrow)

        s_in_t = jnp.swapaxes(student_attn_in, 1, 2)
        t_down_t = teacher_down.T
        peer_qkv = swap(s_in_t, "dp", n_dp, 1)
        t_half = wide // 2
        t_mine, t_theirs = run(
            teacher_norm_kernel,
            "teacher_norm",
            [((total, t_half), BF)] * 2,
            [info, t_x, teacher_gain_a, teacher_shift_a],
        )
        t_other = swap(t_theirs, "dp", n_dp, 1)
        peer_out = swap(after(student_attn_out, t_theirs), "dp", n_dp, 1)
        s_x = after(s_x, t_theirs)

        unused_pairs, unused_single, s_kv_width = kv_tiles(s_heads)
        s_q_width = -(-s_cols // PAIR) * PAIR
        s_normed, s_q, s_kv = run(
            functools.partial(student_qkv_kernel, s_heads),
            "student_qkv",
            [((total, narrow), BF), ((total, s_q_width), BF), ((total, s_kv_width), BF)],
            [info, s_x, student_gain_a, student_shift_a, s_in_t, peer_qkv, student_attn_bias],
            flops=2 * total * narrow * 3 * s_cols,
        )
        s_q = s_q.reshape(slots, rows, s_q_width)
        s_kv_list = gather_keys(s_kv.reshape(slots, rows, s_kv_width))

        heads = wide // HD
        cols = heads // n_tp * HD
        tail = wide - n_tp * cols
        t_heads = (cols + tail) // HD
        unused_pairs, unused_single, t_kv_width = kv_tiles(t_heads)
        t_q_width = -(-(cols + tail) // PAIR) * PAIR
        packed = t_kv_width + t_q_width
        t_mine = after(t_mine, s_kv_list[min(1, len(s_kv_list) - 1)], peer_out)
        peer_up = swap(after(student_up, s_kv), "dp", n_dp, 1)
        t_give, t_own, w_out_give = run(
            functools.partial(teacher_qkv_kernel, t_heads, cols),
            "teacher_qkv",
            [((total, packed), BF), ((total, packed), F32), ((t_half, t_q_width), BF)],
            [info, t_mine, t_other, teacher_attn_in, teacher_attn_out],
            specs=[SMEM, VMEM, VMEM, ANY, VMEM],
            scratch=[
                pltpu.VMEM((3, t_half, cols), BF),
                pltpu.VMEM((3, t_half, tail), BF),
                pltpu.SemaphoreType.DMA((2,)),
            ],
            flops=4 * total * wide * (cols + tail) * 3 // 2,
        )
        t_got = swap(t_give, "dp", n_dp, 1)
        blocks = len(s_kv_list)
        keys = blocks * s_kv_list[0].shape[1]
        block_scratch = [pltpu.VMEM((keys, s_kv_width), BF)] if blocks > 1 else []
        s_q = after(s_q, t_give, peer_up)
        s_att, b_give, b_keep = run(
            functools.partial(student_attend_kernel, s_heads, blocks),
            "student_attend",
            [((slots, rows, s_cols), BF), ((rows, narrow), BF), ((rows, narrow), F32)],
            [info, s_q, student_attn_out, peer_out] + s_kv_list,
            scratch=block_scratch,
            flops=4 * total * s_cols * keys,
            extra=total * s_heads * keys,
        )
        peer_down = swap(after(student_down, b_keep), "dp", n_dp, 1)
        b_keep, t_got = lax.optimization_barrier((b_keep, t_got))
        r, other = tp_sum(b_give, b_keep)
        t_own = after(t_own, s_att)
        t_kv, t_q = run(
            functools.partial(teacher_join_kernel, t_heads, cols),
            "teacher_join",
            [((total, t_kv_width), BF), ((total, t_q_width), BF)],
            [info, t_own, t_got, teacher_attn_bias],
        )
        t_kv_list = gather_keys(t_kv.reshape(slots, rows, t_kv_width))
        t_q = t_q.reshape(slots, rows, t_q_width)

        quarter = t_half // 2

        def half_of(w, *first):
            part = lax.dynamic_slice_in_dim(w, (ctx % 2) * quarter, quarter)
            return swap(after(part, *first), "dp", n_dp, 1)

        up_near = half_of(teacher_up, peer_up, peer_down)

        s_x = after(s_x, t_kv_list[-1], t_kv_list[min(1, len(t_kv_list) - 1)])
        s_mid, b_normed, act, d_upper, give, keep = run(
            student_ffn_kernel,
            "student_ffn",
            [
                ((total, narrow), F32),
                ((total, narrow), BF),
                ((total, hidden), BF),
                ((total, hidden), BF),
                ((rows, narrow), BF),
                ((rows, narrow), F32),
            ],
            [
                info,
                s_x,
                student_out_bias,
                student_gain_b,
                student_shift_b,
                student_up_bias,
                r,
                other,
                student_up,
                peer_up,
                student_down,
                peer_down,
                grad,
            ],
            scratch=[pltpu.VMEM((total, narrow), F32)],
            flops=6 * total * narrow * hidden,
        )
        r2, other2 = tp_sum(give, keep)
        t_q = after(t_q, give)
        t_blocks = len(t_kv_list)
        t_scratch = [pltpu.VMEM((keys, t_kv_width), BF)] if t_blocks > 1 else []
        t_att, t_att_tail = run(
            functools.partial(teacher_attend_kernel, t_heads, t_blocks),
            "teacher_attend",
            [((slots, rows, cols), BF), ((slots, rows, tail), BF)],
            [info, t_q] + t_kv_list,
            scratch=t_scratch,
            flops=4 * total * (cols + tail) * keys,
            extra=total * t_heads * keys,
        )
        every = lax.all_gather(t_att.reshape(total, cols), "tp", axis=0)

        s_mid = after(s_mid, every)
        d_scratch = [
            pltpu.VMEM((total, s_q_width), BF),
            pltpu.VMEM((total, narrow), F32),
        ] + block_scratch
        d_outs = run(
            functools.partial(student_back_kernel, s_heads, blocks),
            "student_back",
            [
                ((total, narrow), F32),
                ((total, narrow), BF),
                ((slots, rows, s_cols), BF),
                ((3, narrow), F32),
            ]
            + [
                (item.shape, F32 if (blocks > 1 and i == 0) else BF)
                for i, item in enumerate(s_kv_list)
            ],
            [info, s_mid, student_gain_b, r2, other2, grad, student_attn_out, peer_out, s_q] + s_kv_list,
            scratch=d_scratch,
            flops=10 * total * s_cols * keys,
            extra=total * s_heads * keys,
        )
        d_mid, d_a, d_q, sums_b = d_outs[:4]
        d_parts = d_outs[4:]
        if near:
            d_own = d_parts[0]
            gots = [
                lax.ppermute(d_parts[k], "ctx", [(i + k, i) for i in range(n_ctx - k)])
                for k in range(1, n_ctx)
            ]
        else:
            d_own = lax.psum_scatter(d_parts[0], "ctx", scatter_dimension=1, tiled=True)
            gots = []
        up_near = after(up_near, d_q)
        up_far = swap(up_near, "ctx", n_ctx, 1)
        down_near = half_of(t_down_t, peer_up, peer_down)
        b_normed = after(b_normed, up_near, d_q)

        g_give, g_keep, sums_f = run(
            functools.partial(student_ffn_grads_kernel, n_ctx),
            "student_ffn_grads",
            [
                ((narrow // 2, 2 * hidden), BF),
                ((narrow // 2, 2 * hidden), F32),
                ((2, narrow), F32),
            ],
            [info, b_normed, act, d_upper, grad],
            scratch=[pltpu.VMEM((narrow, 2 * hidden), F32)],
            flops=4 * total * narrow * hidden,
        )
        down_far = swap(down_near, "ctx", n_ctx, 1)
        w_out_peer = swap(after(w_out_give, peer_up, peer_down), "dp", n_dp, 1)
        every = after(every, g_give, down_near)
        pieces = [up_near, up_far, down_near, down_far]
        o_cols, o_tail = run(
            teacher_out_kernel,
            "teacher_out",
            [((total, cols), BF), ((total, tail), BF)],
            [info, every, t_att_tail.reshape(total, tail), teacher_attn_out, w_out_peer],
            scratch=[pltpu.VMEM((wide, t_q_width), BF)],
            flops=2 * total * wide * (cols + tail),
        )
        o_every = lax.all_gather(o_cols, "tp", axis=0)
        d_own = d_own.reshape(total, s_kv_width)
        gots = [g.reshape(total, s_kv_width) for g in gots]
        a_give, a_keep, ga_give, ga_keep, sums_q = run(
            functools.partial(student_in_kernel, s_heads, len(gots), n_ctx),
            "student_in",
            [
                ((rows, 2 * narrow), BF),
                ((rows, 2 * narrow), F32),
                ((narrow // n_dp, 4 * s_cols), BF),
                ((narrow // n_dp, 4 * s_cols), F32),
                ((2, s_cols), F32),
            ],
            [
                info,
                d_q.reshape(total, s_cols),
                after(s_normed, o_every),
                d_a,
                s_att.reshape(total, s_cols),
                s_in_t,
                peer_qkv,
                act,
                student_down,
                peer_down,
                d_own,
            ]
            + gots,
            scratch=[pltpu.VMEM((total, 2 * narrow), F32), pltpu.VMEM((narrow, 4 * s_cols), F32)],
            flops=2 * total * narrow * 7 * s_cols,
        )
        r3, other3 = tp_sum(a_give, a_keep)
        g_give, g_keep = ring_order(g_give, ctx), ring_order(g_keep, ctx)
        ga_give, ga_keep = ring_order(ga_give, ctx), ring_order(ga_keep, ctx)
        g_got = swap(after(g_give, w_out_peer), "dp", n_dp, 1)
        ga_got = swap(after(ga_give, w_out_peer), "dp", n_dp, 1)
        g_near = halve(g_keep + after(g_got, down_far).astype(F32), 1)
        d_mid = after(d_mid, g_got)
        in_grad, s_result, sums = run(
            student_last_kernel,
            "student_last",
            [((total, narrow), F32), ((total, narrow), BF), ((8, narrow), F32)],
            [
                info,
                s_x,
                student_gain_a,
                s_mid,
                student_down_bias,
                r3,
                other3,
                d_mid,
                sums_b,
                sums_f,
                sums_q,
            ],
            scratch=[pltpu.VMEM((total, narrow), F32)],
        )

        t_hidden = teacher_up.shape[1]
        packed = -(-wide // 128) * 128
        t_mid, f_give, f_keep = run(
            functools.partial(teacher_ffn_kernel, 256),
            "teacher_ffn",
            [((total, wide), F32), ((rows, packed), BF), ((rows, packed), F32)],
            [
                info,
                after(t_x, g_got, in_grad),
                teacher_out_bias,
                teacher_gain_b,
                teacher_shift_b,
                teacher_up_bias,
                o_every,
                o_tail,
                teacher_up,
                t_down_t,
            ]
            + pieces,
            specs=[SMEM] + [VMEM] * 7 + [ANY] * 6,
            scratch=[
                pltpu.VMEM((2 * wide, t_hidden), BF),
                pltpu.VMEM((total, t_hidden), BF),
                pltpu.VMEM((total, wide), BF),
                pltpu.VMEM((total, wide), F32),
                pltpu.SemaphoreType.DMA((6,)),
            ],
            flops=4 * total * wide * t_hidden,
        )
        part = (after(f_keep, g_near) + swap(f_give, "tp", n_tp, 1).astype(F32)).astype(BF)
        r4 = (part.astype(F32) + swap(part, "tp", n_tp, 2).astype(F32)).astype(BF)
        other4 = swap(r4, "tp", n_tp, 1)
        g_ffn = over_rings(halve(after(g_near, part), 3))
        ga_got = after(ga_got, part)
        ga_near = halve(ga_keep + ga_got.astype(F32), 1)
        g_att = over_rings(halve(after(ga_near, r4), 3))
        t_result = run(
            last_kernel,
            "last",
            [((total, wide), BF)],
            [info, t_mid, teacher_down_bias, r4, other4],
        )[0]

        small = small_sum(after(sums, other4))
        piece = narrow // (n_dp * n_ctx)
        shards = lax.dynamic_slice_in_dim(small, (dp * n_ctx + ctx) * piece, piece, axis=1)

        grad_attn_in = jnp.stack([g_att[:, i * s_cols:(i + 1) * s_cols] for i in range(3)])
        return (
            t_result.reshape(slots, rows, wide),
            s_result.reshape(slots, rows, narrow),
            in_grad.reshape(slots, rows, narrow),
            shards[0],
            shards[1],
            grad_attn_in,
            small[7, :2 * s_cols].reshape(2, s_cols),
            g_att[:, 3 * s_cols:].T,
            shards[4],
            shards[2],
            shards[3],
            g_ffn[:, hidden:],
            small[6],
            g_ffn[:, :hidden].T,
            shards[5],
        )

    return body


def solution(mesh):
    sizes = mesh.shape
    return jax.shard_map(
        make_body(sizes["dp"], sizes["ctx"], sizes["tp"]),
        mesh=mesh,
        in_specs=(
            P("dp", "ctx", None),
            P(),
            P(),
            P(None, "dp", None),
            P(),
            P("dp", None),
            P(),
            P(),
            P(),
            P("dp", "tp"),
            P("tp"),
            P("tp", "dp"),
            P(),
            P("dp", "ctx", None),
            P(),
            P(),
            P(None, "dp", "tp"),
            P(None, "tp"),
            P("tp", "dp"),
            P(),
            P(),
            P(),
            P("dp", "tp"),
            P("tp"),
            P("tp", "dp"),
            P(),
            P("dp", "ctx", None),
            P(),
        ),
        out_specs=(
            P("dp", "ctx", None),
            P("dp", "ctx", None),
            P("dp", "ctx", None),
            P(("dp", "ctx")),
            P(("dp", "ctx")),
            P(None, ("dp", "ctx"), "tp"),
            P(None, "tp"),
            P("tp", ("dp", "ctx")),
            P(("dp", "ctx")),
            P(("dp", "ctx")),
            P(("dp", "ctx")),
            P(("dp", "ctx"), "tp"),
            P("tp"),
            P("tp", ("dp", "ctx")),
            P(("dp", "ctx")),
        ),
        check_vma=False,
    )
```
